32 devices in a mesh: box: 8 (over z, x), angle: 4 (over y, core).
Axes of the slice: x: 2, y: 2, z: 4, core: 2. Of those that a mesh axis runs over, the one named last changes fastest.
Arguments:
- top_patterns: bfloat16 [16, 2, 256, 512], P('box', None, 'angle'), may hold values from -6 to 6
- theta_upper: bfloat16 [128, 256], replicated, may hold values from -0.375 to 0.375
- phi_upper: bfloat16 [256, 512], replicated, may hold values from -0.25 to 0.25
- angles_upper: float32 [8, 128, 256], P(None, 'angle'), may hold values from -3.140625 to 3.140625
- table_upper: bfloat16 [316, 2, 128, 256], P(None, None, 'angle'), may hold values from -0.59765625 to 0.59765625
- outgoing_upper: bfloat16 [128, 2, 128, 256], P('box', None, 'angle'), may hold values from -6 to 6
- list_upper: int32 [128, 16], P('box'), may hold values from 0 to 127, as said below
- offset_upper: int32 [128, 16], P('box'), may hold values from 0 to 315
- theta_lower: bfloat16 [64, 128], replicated, may hold values from -0.5 to 0.5
- phi_lower: bfloat16 [128, 256], replicated, may hold values from -0.375 to 0.375
- angles_lower: float32 [8, 64, 128], P(None, 'angle'), may hold values from -3.140625 to 3.140625
- table_lower: bfloat16 [316, 2, 64, 128], P(None, None, 'angle'), may hold values from -0.59765625 to 0.59765625
- outgoing_lower: bfloat16 [1024, 2, 64, 128], P('box', None, 'angle'), may hold values from -6 to 6
- list_lower: int32 [1024, 16], P('box'), may hold values from 0 to 1023, as said below
- offset_lower: int32 [1024, 16], P('box'), may hold values from 0 to 315
- switch_theta: bfloat16 [64, 64], replicated, may hold values from -0.75 to 0.75
- switch_phi: bfloat16 [2, 128, 128], replicated, may hold values from -0.5 to 0.5
Outputs:
- coefficients: float32 [1024, 2, 8192], P(('box', 'angle'))
The draws below stay inside these ranges and needn't reach their ends.
Inputs may be any that keep to these rules, and one draw needn't show every extreme that they name: `list_upper`: Upper-level boxes form blocks of 16 consecutive ids, block k being ids k * 16 to (k + 1) * 16 - 1. Every entry of box g lies in g's own block or in the block whose number is g's block number XOR 4; entry 0 is the box at g's position within that other block. `list_lower`: Lower-level boxes form blocks of 128 consecutive ids. Every entry of box h lies in h's own block or in the block whose number is h's block number XOR 1; entry 0 is the box at h's position within that other block.
All inputs are finite; a program needn't handle non-finite values.
Results may differ from the reference program's by a relative error of at most 0.0039.
Values may be sent and summed in bfloat16 or wider, within the bound.
No kernel may reach another device: no remote copies, remote signals or barrier semaphores. Data moves between devices by JAX's collectives and lax.ppermute only.
A program may use at most 128 MiB of HBM per device.

```python
import jax
import jax.numpy as jnp
from jax import lax

NT0 = 256
NP0 = 512
NT1 = 128
NP1 = 256
NT2 = 64
NP2 = 128
NCT = 64
NCP = 128
NOFF = 316
NL = 16
B0 = 16
B1D = 16
B1 = 128
B2D = 128
B2 = 1024
FAR = 4


def sibling_lists(key, box_count, block_size, partner_step):
    box_ids = jnp.arange(box_count, dtype=jnp.int32)
    home_block = box_ids // block_size
    far_block = jnp.bitwise_xor(home_block, partner_step)
    drawn_pick = jax.random.randint(key, (box_count, NL), 0, 2 * block_size, dtype=jnp.int32)
    position = drawn_pick % block_size
    entries = jnp.where(drawn_pick < block_size, home_block[:, None] * block_size + position, far_block[:, None] * block_size + position)
    mirrored = far_block * block_size + box_ids % block_size
    return entries.at[:, 0].set(mirrored)


def draw_list_upper(key, part):
    return sibling_lists(jax.random.fold_in(key, 11), B1, B1D, FAR)


def draw_list_lower(key, part):
    return sibling_lists(jax.random.fold_in(key, 12), B2, B2D, 1)


def with_ends(drawn, rng, least, largest):
    longest = drawn.shape.index(max(drawn.shape))
    spots = []
    for shift in (0, 1):
        where = [jax.random.randint(jax.random.fold_in(rng, axis), (), 0, length) for axis, length in enumerate(drawn.shape)]
        where[longest] = (where[longest] + shift) % drawn.shape[longest]
        spots.append(tuple(where))
    return drawn.at[spots[0]].set(least).at[spots[1]].set(largest)


def shard_levels(key, shape, pieces, smallest, high):
    gain = 1.0
    for dim, parts in pieces:
        heights = jax.random.uniform(jax.random.fold_in(jax.random.fold_in(key, 6), dim), (parts,), jnp.float32, smallest / len(pieces), high / len(pieces))
        gain = gain * jnp.repeat(jnp.exp(heights), shape[dim] // parts).reshape((-1,) + (1,) * (len(shape) - 1 - dim))
    return gain


def scatter_about(stream_key, extent, spread, most, cuts=(), kind=jnp.bfloat16):
    drawn = spread * jax.random.normal(stream_key, extent, jnp.float32)
    if cuts:
        drawn = drawn * shard_levels(stream_key, extent, cuts, -0.22, 0.18)
    return jnp.clip(drawn, -most, most).astype(kind)


def setup_inputs(seed: int = 0) -> dict:
    streams_of = jax.random.split(jax.random.key(seed), 18)
    top_patterns = scatter_about(streams_of[0], (B0, 2, NT0, NP0), 1.0, 6.0, ((0, 8), (2, 4)))
    theta_upper = scatter_about(streams_of[1], (NT1, NT0), NT0 ** -0.5, 0.375)
    phi_upper = scatter_about(streams_of[2], (NP1, NP0), NP0 ** -0.5, 0.25)
    angles_upper = jnp.clip(jax.random.uniform(streams_of[3], (8, NT1, NP1), jnp.float32, -3.140625, 3.140625), -3.140625, 3.140625)
    table_upper = scatter_about(streams_of[4], (NOFF, 2, NT1, NP1), 0.1, 0.59765625, ((2, 4),))
    outgoing_upper = scatter_about(streams_of[5], (B1, 2, NT1, NP1), 1.0, 6.0, ((0, 8), (2, 4)))
    list_upper = draw_list_upper(jax.random.fold_in(streams_of[17], 71), 0)
    offset_upper = with_ends(jax.random.randint(streams_of[7], (B1, NL), 0, NOFF), jax.random.fold_in(streams_of[7], 1), 0, NOFF - 1).astype(jnp.int32)
    theta_lower = scatter_about(streams_of[8], (NT2, NT1), NT1 ** -0.5, 0.5)
    phi_lower = scatter_about(streams_of[9], (NP2, NP1), NP1 ** -0.5, 0.375)
    angles_lower = jnp.clip(jax.random.uniform(streams_of[10], (8, NT2, NP2), jnp.float32, -3.140625, 3.140625), -3.140625, 3.140625)
    table_lower = scatter_about(streams_of[11], (NOFF, 2, NT2, NP2), 0.1, 0.59765625, ((2, 4),))
    outgoing_lower = scatter_about(streams_of[12], (B2, 2, NT2, NP2), 1.0, 6.0, ((0, 8), (2, 4)))
    list_lower = draw_list_lower(jax.random.fold_in(streams_of[17], 71), 0)
    offset_lower = with_ends(jax.random.randint(streams_of[14], (B2, NL), 0, NOFF), jax.random.fold_in(streams_of[14], 1), 0, NOFF - 1).astype(jnp.int32)
    switch_theta = scatter_about(streams_of[15], (NCT, NT2), NT2 ** -0.5, 0.75)
    switch_phi = scatter_about(streams_of[16], (2, NCP, NP2), NP2 ** -0.5, 0.5)
    return dict(top_patterns=top_patterns, theta_upper=theta_upper, phi_upper=phi_upper, angles_upper=angles_upper, table_upper=table_upper, outgoing_upper=outgoing_upper, list_upper=list_upper, offset_upper=offset_upper, theta_lower=theta_lower, phi_lower=phi_lower, angles_lower=angles_lower, table_lower=table_lower, outgoing_lower=outgoing_lower, list_lower=list_lower, offset_lower=offset_lower, switch_theta=switch_theta, switch_phi=switch_phi)


def anterpolate(patterns, theta_map, phi_map):
    values = patterns.astype(jnp.float32)
    theta_pass = jnp.einsum("ut,bctp->bcup", theta_map.astype(jnp.float32), values, precision=lax.Precision.HIGHEST)
    return jnp.einsum("bcup,qp->bcuq", theta_pass, phi_map.astype(jnp.float32), precision=lax.Precision.HIGHEST)


def shift_children(coarse, angles):
    cosines = jnp.cos(angles)[None]
    sine_part = jnp.sin(angles)[None]
    real_part = coarse[:, 0][:, None] * cosines - coarse[:, 1][:, None] * sine_part
    imag_part = coarse[:, 0][:, None] * sine_part + coarse[:, 1][:, None] * cosines
    stacked = jnp.stack([real_part, imag_part], axis=2)
    return stacked.reshape((stacked.shape[0] * stacked.shape[1],) + stacked.shape[2:])


def translate(outgoing, table_rows, entry_lists, offsets):
    def one_box(entry_pair):
        source = jnp.take(outgoing, entry_pair[0], axis=0).astype(jnp.float32)
        factor = jnp.take(table_rows, entry_pair[1], axis=0).astype(jnp.float32)
        real_sum = jnp.sum(factor[:, 0] * source[:, 0] - factor[:, 1] * source[:, 1], axis=0)
        imag_sum = jnp.sum(factor[:, 0] * source[:, 1] + factor[:, 1] * source[:, 0], axis=0)
        return jnp.stack([real_sum, imag_sum])
    return lax.map(one_box, (entry_lists, offsets))


def reference(top_patterns, theta_upper, phi_upper, angles_upper, table_upper, outgoing_upper, list_upper, offset_upper, theta_lower, phi_lower, angles_lower, table_lower, outgoing_lower, list_lower, offset_lower, switch_theta, switch_phi):
    coarse = anterpolate(top_patterns, theta_upper, phi_upper)
    incoming_upper = (shift_children(coarse, angles_upper) + translate(outgoing_upper, table_upper, list_upper, offset_upper)).astype(jnp.bfloat16)
    coarse = anterpolate(incoming_upper, theta_lower, phi_lower)
    incoming_lower = (shift_children(coarse, angles_lower) + translate(outgoing_lower, table_lower, list_lower, offset_lower)).astype(jnp.bfloat16)
    theta_pass = jnp.einsum("ut,bctp->bcup", switch_theta.astype(jnp.float32), incoming_lower.astype(jnp.float32), precision=lax.Precision.HIGHEST)
    phi_real = switch_phi[0].astype(jnp.float32)
    phi_imag = switch_phi[1].astype(jnp.float32)
    coeff_real = jnp.einsum("bup,vp->buv", theta_pass[:, 0], phi_real, precision=lax.Precision.HIGHEST) - jnp.einsum("bup,vp->buv", theta_pass[:, 1], phi_imag, precision=lax.Precision.HIGHEST)
    coeff_imag = jnp.einsum("bup,vp->buv", theta_pass[:, 0], phi_imag, precision=lax.Precision.HIGHEST) + jnp.einsum("bup,vp->buv", theta_pass[:, 1], phi_real, precision=lax.Precision.HIGHEST)
    stacked = jnp.stack([coeff_real, coeff_imag], axis=1)
    return stacked.reshape(stacked.shape[0], 2, stacked.shape[2] * stacked.shape[3])
```

```python
import functools

import jax
import jax.numpy as jnp
from jax import lax
from jax.experimental import pallas as pl
from jax.experimental.pallas import tpu as pltpu
from jax.sharding import PartitionSpec as P

F32, BF16 = jnp.float32, jnp.bfloat16
VM = pl.BlockSpec(memory_space=pltpu.VMEM)
SM = pl.BlockSpec(memory_space=pltpu.SMEM)
SHIFT = 9
NT = (((1,), (1,)), ((), ()))


def swap(value, axis, mask):
    pairs = [(source, source ^ mask) for source in range(lax.axis_size(axis))]
    return lax.ppermute(value, axis, pairs)


def kernel_call(body, outs, scalars, arrays, name, scratch=(), vmem=16 << 20, flops=0):
    moved = sum(a.size * a.dtype.itemsize for a in arrays)
    return pl.pallas_call(
        body,
        out_shape=outs,
        in_specs=[SM] * len(scalars) + [VM] * len(arrays),
        out_specs=[VM] * len(outs),
        scratch_shapes=list(scratch),
        compiler_params=pltpu.CompilerParams(vmem_limit_bytes=vmem),
        cost_estimate=pl.CostEstimate(flops=flops, bytes_accessed=moved, transcendentals=0),
        name=name,
    )(*scalars, *arrays)


def split_dot(left, value, dims):
    high = value.astype(BF16)
    low = (value - high.astype(F32)).astype(BF16)
    return lax.dot_general(left, high, dims, preferred_element_type=F32) + lax.dot_general(
        left, low, dims, preferred_element_type=F32
    )


def widen_body(table, source, table_out, source_out):
    count = source.shape[0]
    table_out[...] = table[...].astype(F32)
    source_out[0:count] = source[...].astype(F32)
    source_out[count] = jnp.zeros(source.shape[1:], F32)


def box_sum(box, entries, code, table, source):
    rows = table.shape[1] // 2
    real = imag = None
    for entry in range(entries):
        word = code[box * entries + entry]
        factor = table[word & ((1 << SHIFT) - 1)]
        value = source[word >> SHIFT]
        fr, fi, sr, si = factor[:rows], factor[rows:], value[:rows], value[rows:]
        re, im = fr * sr - fi * si, fr * si + fi * sr
        real = re if real is None else real + re
        imag = im if imag is None else imag + im
    return real, imag


def sums_body(groups, per, entries, me, *refs):
    codes = max(which for _, which in groups) + 1
    code_refs, (table, source), outs = refs[:codes], refs[codes : codes + 2], refs[codes + 2 :]
    rows = table.shape[1] // 2
    for (masks, which), out in zip(groups, outs, strict=True):
        for place, mask in enumerate(masks):
            first = jnp.bitwise_xor(me[0], mask) * per

            def one(i, carry, first=first, place=place, which=which, out=out):
                real, imag = box_sum(first + i, entries, code_refs[which], table, source)
                out[place * per + i, 0:rows] = real.astype(out.dtype)
                out[place * per + i, rows:] = imag.astype(out.dtype)
                return carry

            lax.fori_loop(0, per, one, 0, unroll=2)


def early_body(peers, rows, me, top, theta, phi, angles, *refs):
    outs, (padded, summed) = refs[:peers], refs[peers:]
    held = top.shape[0] // 4
    narrowed = lax.dot_general(top[...], phi[...], NT, preferred_element_type=F32)
    padded[...] = jnp.zeros(padded.shape, F32)
    for k in range(4):
        padded[k, me[0]] = narrowed[k * held : (k + 1) * held]
    for k in range(4):
        full = padded[k].reshape(peers * held, narrowed.shape[1])
        part = split_dot(theta[...], full, (((1,), (0,)), ((), ())))
        summed[k] = part.reshape(peers, rows, narrowed.shape[1])
    low = angles.shape[1]
    half = angles.shape[0] // 2
    for mask, out in enumerate(outs):
        for k in range(4):
            out[k * rows : (k + 1) * rows] = summed[k, jnp.bitwise_xor(me[0], mask)]
        for c in range(half):
            start = 4 * rows + c * low
            out[start : start + low, 0:128] = angles[c]
            out[start : start + low, 128:256] = angles[half + c]


def shift_body(peers, rows, low, me, angles, *refs):
    parts, (shifted, trig) = refs[:peers], refs[peers:]
    children = angles.shape[0]
    half = children // 2
    for c in range(children):
        cosine, sine = jnp.cos(angles[c]), jnp.sin(angles[c])
        for b in range(2):
            re = parts[0][2 * b * rows : (2 * b + 1) * rows]
            im = parts[0][(2 * b + 1) * rows : (2 * b + 2) * rows]
            for part in parts[1:]:
                re = re + part[2 * b * rows : (2 * b + 1) * rows]
                im = im + part[(2 * b + 1) * rows : (2 * b + 2) * rows]
            shifted[b * children + c, 0] = re * cosine - im * sine
            shifted[b * children + c, 1] = re * sine + im * cosine
    for mask, part in enumerate(parts):
        for c in range(half):
            start = 4 * rows + c * low
            for side in range(2):
                angle = part[start : start + low, side * 128 : side * 128 + 128]
                place = jnp.bitwise_xor(me[0], mask)
                trig[0, side * half + c, place] = jnp.cos(angle)
                trig[1, side * half + c, place] = jnp.sin(angle)


def upper_body(peers, entries, me, code, own, far, table, shifted, phi, *refs):
    outs, (pool, whole) = refs[:peers], refs[peers:]
    boxes, _, rows, _ = own.shape
    pool[0:boxes] = own[...].astype(F32)
    pool[boxes:] = far[...].astype(F32)
    step = min(16, rows)
    per = boxes // peers

    def one(box, carry):
        for r in range(0, rows, step):
            span = slice(r, r + step)
            real, imag = shifted[box, 0, span], shifted[box, 1, span]
            for entry in range(entries):
                word = code[box * entries + entry]
                offset, place = word & ((1 << SHIFT) - 1), word >> SHIFT
                fr, fi = table[offset, 0, span].astype(F32), table[offset, 1, span].astype(F32)
                sr, si = pool[place, 0, span], pool[place, 1, span]
                real = real + (fr * sr - fi * si)
                imag = imag + (fr * si + fi * sr)
            whole[box, 0, span] = real
            whole[box, 1, span] = imag
        return carry

    lax.fori_loop(0, boxes, one, 0)
    for mask in range(peers):
        first = jnp.bitwise_xor(me[0], mask) * per
        for i in range(per):
            for c in range(2):
                incoming = whole[first + i, c].astype(BF16)
                narrow = lax.dot_general(incoming, phi[...], NT, preferred_element_type=F32)
                outs[mask][i, c * rows : (c + 1) * rows] = narrow.astype(BF16)


def final_body(peers, me, *refs):
    ups, lows = refs[:peers], refs[peers : 2 * peers]
    trig, theta, mix, expand, out, rows_up, rows_low, pattern = refs[2 * peers :]
    children, rows = trig.shape[1], trig.shape[2]
    high_rows, low_rows = rows_up.shape[2], rows_low.shape[3]
    for mask in range(peers):
        place = jnp.bitwise_xor(me[0], mask)
        for c in range(2):
            rows_up[c, place] = ups[mask][0, c * high_rows : (c + 1) * high_rows].astype(F32)
            for k in range(children):
                piece = lows[mask][k, c * low_rows : (c + 1) * low_rows]
                rows_low[k, c, place] = piece.astype(F32)
    coarse = []
    for c in range(2):
        full = rows_up[c].reshape(peers * high_rows, 128).astype(BF16)
        coarse.append(jnp.dot(theta[...], full, preferred_element_type=F32))
    for k in range(children):
        cosine, sine = trig[0, k], trig[1, k]
        real = coarse[0] * cosine - coarse[1] * sine + rows_low[k, 0].reshape(rows, 128)
        imag = coarse[0] * sine + coarse[1] * cosine + rows_low[k, 1].reshape(rows, 128)
        pattern[k * rows : (k + 1) * rows, 0:128] = real.astype(BF16)
        pattern[k * rows : (k + 1) * rows, 128:256] = imag.astype(BF16)
    for k in range(0, children, 2):
        block = pattern[k * rows : (k + 2) * rows]
        turned = lax.dot_general(block, mix[...], NT, preferred_element_type=F32)
        one, two = turned[:rows], turned[rows:]
        stacked = jnp.concatenate(
            [
                jnp.concatenate([one[:, :128], two[:, :128]], axis=1),
                jnp.concatenate([one[:, 128:], two[:, 128:]], axis=1),
            ],
            axis=0,
        )
        result = split_dot(expand[...], stacked, (((1,), (0,)), ((), ())))
        size = expand.shape[0]
        out[k * size : (k + 1) * size] = result[:, :128]
        out[(k + 1) * size : (k + 2) * size] = result[:, 128:]


def struct(shape, dtype):
    return jax.ShapeDtypeStruct(shape, dtype)


def per_device(
    top_patterns,
    theta_upper,
    phi_upper,
    angles_upper,
    table_upper,
    outgoing_upper,
    list_upper,
    offset_upper,
    theta_lower,
    phi_lower,
    angles_lower,
    table_lower,
    outgoing_lower,
    list_lower,
    offset_lower,
    switch_theta,
    switch_phi,
):
    peers = lax.axis_size("angle")
    home = lax.axis_index("box")
    me = lax.axis_index("angle").astype(jnp.int32).reshape(1)
    far_mask = lax.axis_size("box") // 2
    boxes, _, low, lanes = outgoing_lower.shape
    per = boxes // peers
    entries = list_lower.shape[1]
    upper_boxes, _, rows, wide = outgoing_upper.shape
    upper_per = upper_boxes // peers

    other = list_lower // boxes != home
    spot = list_lower % boxes
    ask_code = ((jnp.where(other, spot, boxes) << SHIFT) + offset_lower).reshape(-1)
    own_code = ((jnp.where(other, boxes, spot) << SHIFT) + offset_lower).reshape(-1)
    far_code = swap(ask_code, "box", 1)
    far_upper = swap(outgoing_upper, "box", far_mask)
    upper_spot = list_upper % upper_boxes + jnp.where(list_upper // upper_boxes != home, upper_boxes, 0)
    upper_code = ((upper_spot << SHIFT) + offset_upper).reshape(-1)

    children = angles_lower.shape[0]
    part_rows = 4 * rows + children * low // 2
    held = top_patterns.shape[2]
    parts = kernel_call(
        functools.partial(early_body, peers, rows),
        [struct((part_rows, wide), F32)] * peers,
        [me],
        [top_patterns.reshape(4 * held, -1), theta_upper, phi_upper, angles_lower],
        "early",
        scratch=[pltpu.VMEM((4, peers, held, wide), F32), pltpu.VMEM((4, peers, rows, wide), F32)],
        flops=4 * held * wide * 512 * 2,
    )
    parts = [swap(part, "angle", mask) if mask else part for mask, part in enumerate(parts)]
    shifted, trig = kernel_call(
        functools.partial(shift_body, peers, rows, low),
        [
            struct((upper_boxes, 2, rows, wide), F32),
            struct((2, children, peers, low, lanes), F32),
        ],
        [me],
        [angles_upper, *parts],
        "shift",
    )
    trig = trig.reshape(2, children, peers * low, lanes)

    table, source = kernel_call(
        widen_body,
        [
            struct((table_lower.shape[0], 2 * low, lanes), F32),
            struct((boxes + 1, 2 * low, lanes), F32),
        ],
        [],
        [table_lower.reshape(-1, 2 * low, lanes), outgoing_lower.reshape(-1, 2 * low, lanes)],
        "widen",
    )
    outer, inner = list(range(peers - 1, peers // 2 - 1, -1)), list(range(peers // 2 - 1, -1, -1))
    first = kernel_call(
        functools.partial(sums_body, [((mask,), 0) for mask in outer], per, entries),
        [struct((per, 2 * low, lanes), BF16)] * len(outer),
        [me, far_code],
        [table, source],
        "sums_first",
    )
    rest = kernel_call(
        functools.partial(
            sums_body,
            [(tuple(inner), 0)] + [((mask,), 1) for mask in outer + inner],
            per,
            entries,
        ),
        [struct((len(inner) * per, 2 * low, lanes), BF16)]
        + [struct((per, 2 * low, lanes), F32)] * peers,
        [me, far_code, own_code],
        [table, source],
        "sums_rest",
    )
    own = dict(zip(outer + inner, rest[1:], strict=True))
    got = {mask: swap(value, "box", 1) for mask, value in zip(outer, first, strict=True)}
    last = swap(rest[0], "box", 1)
    for place, mask in enumerate(inner):
        got[mask] = last[place * per : (place + 1) * per]
    lows = []
    for mask in outer + inner:
        total = (own[mask] + got[mask].astype(F32)).astype(BF16)
        lows.append((mask, swap(total, "angle", mask) if mask else total))
    lows = [value for _, value in sorted(lows, key=lambda item: item[0])]

    ups = kernel_call(
        functools.partial(upper_body, peers, entries),
        [struct((upper_per, 2 * rows, lanes), BF16)] * peers,
        [me, upper_code],
        [outgoing_upper, far_upper, table_upper, shifted, phi_lower],
        "upper",
        scratch=[
            pltpu.VMEM((2 * upper_boxes, 2, rows, wide), F32),
            pltpu.VMEM((upper_boxes, 2, rows, wide), F32),
        ],
    )
    ups = [swap(value, "angle", mask) if mask else value for mask, value in enumerate(ups)]

    orders, angles = switch_theta.shape
    pair = jnp.eye(2, dtype=BF16)
    expand = (switch_theta[:, None, None, :] * pair[None, :, :, None]).reshape(2 * orders, 2 * angles)
    mix = jnp.concatenate(
        [
            jnp.concatenate([switch_phi[0], -switch_phi[1]], axis=1),
            jnp.concatenate([switch_phi[1], switch_phi[0]], axis=1),
        ],
        axis=0,
    )
    azimuths = switch_phi.shape[1]
    whole = lambda shape: pl.BlockSpec(shape, lambda b: (0,) * len(shape))
    out = pl.pallas_call(
        functools.partial(final_body, peers),
        out_shape=struct((per * 2 * orders, azimuths), F32),
        grid=(upper_per,),
        in_specs=[SM]
        + [pl.BlockSpec((1, 2 * rows, lanes), lambda b: (b, 0, 0))] * peers
        + [pl.BlockSpec((children, 2 * low, lanes), lambda b: (b, 0, 0))] * peers
        + [whole(trig.shape), whole(theta_lower.shape), whole(mix.shape), whole(expand.shape)],
        out_specs=pl.BlockSpec((children * 2 * orders, azimuths), lambda b: (b, 0)),
        scratch_shapes=[
            pltpu.VMEM((2, peers, rows, lanes), F32),
            pltpu.VMEM((children, 2, peers, low, lanes), F32),
            pltpu.VMEM((children * peers * low, 2 * lanes), BF16),
        ],
        compiler_params=pltpu.CompilerParams(vmem_limit_bytes=16 << 20),
        name="expand",
    )(me, *ups, *lows, trig, theta_lower, mix, expand)
    out = out.reshape(per, orders, 2, azimuths)
    return jnp.transpose(out, (0, 2, 1, 3)).reshape(per, 2, orders * azimuths)


def solution(mesh):
    return jax.shard_map(
        per_device,
        mesh=mesh,
        in_specs=(
            P("box", None, "angle", None),
            P(),
            P(),
            P(None, "angle", None),
            P(None, None, "angle", None),
            P("box", None, "angle", None),
            P("box", None),
            P("box", None),
            P(),
            P(),
            P(None, "angle", None),
            P(None, None, "angle", None),
            P("box", None, "angle", None),
            P("box", None),
            P("box", None),
            P(),
            P(),
        ),
        out_specs=P(("box", "angle"), None, None),
        check_vma=False,
    )
```

```python
import functools

import jax
import jax.numpy as jnp
from jax import lax
from jax.experimental import pallas as pl
from jax.experimental.pallas import tpu as pltpu
from jax.sharding import PartitionSpec as P

F32, BF16 = jnp.float32, jnp.bfloat16
VM = pl.BlockSpec(memory_space=pltpu.VMEM)
SM = pl.BlockSpec(memory_space=pltpu.SMEM)
HB = pl.BlockSpec(memory_space=pltpu.HBM)
SHIFT = 9
NT = (((1,), (1,)), ((), ()))


def swap(value, axis, mask):
    pairs = [(source, source ^ mask) for source in range(lax.axis_size(axis))]
    return lax.ppermute(value, axis, pairs)


def after(value, *others):
    return lax.optimization_barrier((value, *others))[0]


def kernel_call(body, outs, scalars, arrays, name, scratch=(), held=0, vmem=6 << 20):
    near = len(arrays) - held
    return pl.pallas_call(
        body,
        out_shape=outs,
        in_specs=[SM] * len(scalars) + [VM] * near + [HB] * held,
        out_specs=[VM] * len(outs),
        scratch_shapes=list(scratch),
        compiler_params=pltpu.CompilerParams(vmem_limit_bytes=vmem),
        cost_estimate=pl.CostEstimate(flops=4000000000, bytes_accessed=1, transcendentals=0),
        name=name,
    )(*scalars, *arrays)


def fetch(pairs, sems):
    copies = [pltpu.make_async_copy(a, b, sems.at[k]) for k, (a, b) in enumerate(pairs)]
    for copy in copies:
        copy.start()
    return copies


def split_dot(left, value, dims):
    high = value.astype(BF16)
    low = (value - high.astype(F32)).astype(BF16)
    return lax.dot_general(left, high, dims, preferred_element_type=F32) + lax.dot_general(
        left, low, dims, preferred_element_type=F32
    )


def widen_body(table, source, table_out, source_out, table_in, source_in, sems):
    count, total = source.shape[0], table.shape[0]
    half = total // 2
    copies = fetch(
        [
            (source, source_in),
            (table.at[0:half], table_in.at[0:half]),
            (table.at[half:], table_in.at[half:]),
        ],
        sems,
    )
    copies[0].wait()
    source_out[0:count] = source_in[...].astype(F32)
    source_out[count] = jnp.zeros(source.shape[1:], F32)
    copies[1].wait()
    table_out[0:half] = table_in[0:half].astype(F32)
    copies[2].wait()
    table_out[half:] = table_in[half:].astype(F32)


def box_sum(box, entries, code, table, source):
    rows = table.shape[1] // 2
    real = imag = None
    for entry in range(entries):
        word = code[entry, box]
        factor = table[word & ((1 << SHIFT) - 1)]
        value = source[word >> SHIFT]
        fr, fi, sr, si = factor[:rows], factor[rows:], value[:rows], value[rows:]
        re, im = fr * sr - fi * si, fr * si + fi * sr
        real = re if real is None else real + re
        imag = im if imag is None else imag + im
    return real, imag


def sums_body(groups, per, entries, me, *refs):
    codes = max(which for _, which in groups) + 1
    code_refs, (table, source), outs = refs[:codes], refs[codes : codes + 2], refs[codes + 2 :]
    rows = table.shape[1] // 2
    for (masks, which), out in zip(groups, outs, strict=True):
        for place, mask in enumerate(masks):
            first = jnp.bitwise_xor(me[0], mask) * per

            def one(i, carry, first=first, place=place, which=which, out=out):
                real, imag = box_sum(first + i, entries, code_refs[which], table, source)
                out[place * per + i, 0:rows] = real.astype(out.dtype)
                out[place * per + i, rows:] = imag.astype(out.dtype)
                return carry

            lax.fori_loop(0, per, one, 0, unroll=2)


def early_body(peers, rows, me, *refs):
    near, outs = refs[:4], refs[4 : 4 + peers]
    padded, summed, top, theta, phi, angles, sems = refs[4 + peers :]
    held = top.shape[0] // 4
    for copy in fetch(list(zip(near, (top, theta, phi, angles), strict=True)), sems):
        copy.wait()
    narrowed = lax.dot_general(top[...], phi[...], NT, preferred_element_type=F32)
    padded[...] = jnp.zeros(padded.shape, F32)
    for k in range(4):
        padded[k, me[0]] = narrowed[k * held : (k + 1) * held]
    for k in range(4):
        full = padded[k].reshape(peers * held, narrowed.shape[1])
        part = split_dot(theta[...], full, (((1,), (0,)), ((), ())))
        summed[k] = part.reshape(peers, rows, narrowed.shape[1])
    low = angles.shape[1]
    half = angles.shape[0] // 2
    for mask, out in enumerate(outs):
        for k in range(4):
            out[k * rows : (k + 1) * rows] = summed[k, jnp.bitwise_xor(me[0], mask)]
        for c in range(half):
            start = 4 * rows + c * low
            out[start : start + low, 0:128] = angles[c]
            out[start : start + low, 128:256] = angles[half + c]


def shift_body(peers, rows, low, me, *refs):
    parts, near = refs[:peers], refs[peers : peers + 3]
    shifted, trig, expand, mix, angles, theta, phi, sems = refs[peers + 3 :]
    for copy in fetch(list(zip(near, (angles, theta, phi), strict=True)), sems):
        copy.wait()
    orders = theta.shape[0]
    line = lax.broadcasted_iota(jnp.int32, (2 * orders, orders), 0)
    column = lax.broadcasted_iota(jnp.int32, (2 * orders, orders), 1)
    for c in range(2):
        pick = (line == 2 * column + c).astype(F32).astype(BF16)
        spread = jnp.dot(pick, theta[...], preferred_element_type=F32)
        expand[c] = spread.astype(BF16)
    size = phi.shape[1]
    mix[0:size, 0:size] = phi[0]
    mix[0:size, size:] = -phi[1]
    mix[size:, 0:size] = phi[1]
    mix[size:, size:] = phi[0]
    children = angles.shape[0]
    half = children // 2
    for c in range(children):
        cosine, sine = jnp.cos(angles[c]), jnp.sin(angles[c])
        for b in range(2):
            re = parts[0][2 * b * rows : (2 * b + 1) * rows]
            im = parts[0][(2 * b + 1) * rows : (2 * b + 2) * rows]
            for part in parts[1:]:
                re = re + part[2 * b * rows : (2 * b + 1) * rows]
                im = im + part[(2 * b + 1) * rows : (2 * b + 2) * rows]
            shifted[b * children + c, 0] = re * cosine - im * sine
            shifted[b * children + c, 1] = re * sine + im * cosine
    for mask, part in enumerate(parts):
        for c in range(half):
            start = 4 * rows + c * low
            for side in range(2):
                angle = part[start : start + low, side * 128 : side * 128 + 128]
                place = jnp.bitwise_xor(me[0], mask)
                trig[0, side * half + c, place] = jnp.cos(angle)
                trig[1, side * half + c, place] = jnp.sin(angle)


def join(owns, got):
    def body(*refs):
        first = 0
        count = len(owns)
        for own, out in zip(refs[:count], refs[count + 1 :], strict=True):
            size = own.shape[0]
            out[...] = (own[...] + refs[count][first : first + size].astype(F32)).astype(BF16)
            first += size

    return kernel_call(body, [struct(a.shape, BF16) for a in owns], [], [*owns, got], "join")


def upper_body(peers, entries, me, code, own, far, table, shifted, phi, *refs):
    outs, (pool, whole) = refs[:peers], refs[peers:]
    boxes, _, rows, _ = own.shape
    pool[0:boxes] = own[...].astype(F32)
    pool[boxes:] = far[...].astype(F32)
    step = min(16, rows)
    per = boxes // peers

    def one(box, carry):
        for r in range(0, rows, step):
            span = slice(r, r + step)
            real, imag = shifted[box, 0, span], shifted[box, 1, span]
            for entry in range(entries):
                word = code[entry, box]
                offset, place = word & ((1 << SHIFT) - 1), word >> SHIFT
                fr, fi = table[offset, 0, span].astype(F32), table[offset, 1, span].astype(F32)
                sr, si = pool[place, 0, span], pool[place, 1, span]
                real = real + (fr * sr - fi * si)
                imag = imag + (fr * si + fi * sr)
            whole[box, 0, span] = real
            whole[box, 1, span] = imag
        return carry

    lax.fori_loop(0, boxes, one, 0)
    for mask in range(peers):
        first = jnp.bitwise_xor(me[0], mask) * per
        for i in range(per):
            for c in range(2):
                incoming = whole[first + i, c].astype(BF16)
                narrow = lax.dot_general(incoming, phi[...], NT, preferred_element_type=F32)
                outs[mask][i, c * rows : (c + 1) * rows] = narrow.astype(BF16)


def final_body(peers, me, *refs):
    ups, lows = refs[:peers], refs[peers : 2 * peers]
    trig, theta, mix, expand, out, rows_up, rows_low, pattern = refs[2 * peers :]
    children, rows = trig.shape[1], trig.shape[2]
    high_rows, low_rows = rows_up.shape[2], rows_low.shape[3]
    for mask in range(peers):
        place = jnp.bitwise_xor(me[0], mask)
        for c in range(2):
            rows_up[c, place] = ups[mask][0, c * high_rows : (c + 1) * high_rows].astype(F32)
            for k in range(children):
                piece = lows[mask][k, c * low_rows : (c + 1) * low_rows]
                rows_low[k, c, place] = piece.astype(F32)
    coarse = []
    for c in range(2):
        full = rows_up[c].reshape(peers * high_rows, 128).astype(BF16)
        coarse.append(jnp.dot(theta[...], full, preferred_element_type=F32))
    for k in range(children):
        cosine, sine = trig[0, k], trig[1, k]
        real = coarse[0] * cosine - coarse[1] * sine + rows_low[k, 0].reshape(rows, 128)
        imag = coarse[0] * sine + coarse[1] * cosine + rows_low[k, 1].reshape(rows, 128)
        pattern[k * rows : (k + 1) * rows, 0:128] = real.astype(BF16)
        pattern[k * rows : (k + 1) * rows, 128:256] = imag.astype(BF16)
    for k in range(0, children, 2):
        block = pattern[k * rows : (k + 2) * rows]
        turned = lax.dot_general(block, mix[...], NT, preferred_element_type=F32)
        one, two = turned[:rows], turned[rows:]
        stacked = jnp.concatenate(
            [
                jnp.concatenate([one[:, :128], two[:, :128]], axis=1),
                jnp.concatenate([one[:, 128:], two[:, 128:]], axis=1),
            ],
            axis=0,
        )
        both = jnp.concatenate([expand[0], expand[1]], axis=1)
        result = split_dot(both, stacked, (((1,), (0,)), ((), ())))
        size = expand.shape[1]
        out[k * size : (k + 1) * size] = result[:, :128]
        out[(k + 1) * size : (k + 2) * size] = result[:, 128:]


def struct(shape, dtype):
    return jax.ShapeDtypeStruct(shape, dtype)


def per_device(
    top_patterns,
    theta_upper,
    phi_upper,
    angles_upper,
    table_upper,
    outgoing_upper,
    list_upper,
    offset_upper,
    theta_lower,
    phi_lower,
    angles_lower,
    table_lower,
    outgoing_lower,
    list_lower,
    offset_lower,
    switch_theta,
    switch_phi,
):
    peers = lax.axis_size("angle")
    home = lax.axis_index("box")
    me = lax.axis_index("angle").astype(jnp.int32).reshape(1)
    far_mask = lax.axis_size("box") // 2
    boxes, _, low, lanes = outgoing_lower.shape
    per = boxes // peers
    entries = list_lower.shape[1]
    upper_boxes, _, rows, wide = outgoing_upper.shape
    upper_per = upper_boxes // peers

    other = list_lower.T // boxes != home
    spot = list_lower.T % boxes
    ask_code = (jnp.where(other, spot, boxes) << SHIFT) + offset_lower.T
    own_code = (jnp.where(other, boxes, spot) << SHIFT) + offset_lower.T
    upper_spot = list_upper % upper_boxes + jnp.where(list_upper // upper_boxes != home, upper_boxes, 0)
    upper_code = ((upper_spot << SHIFT) + offset_upper).T
    ask_code, own_code, upper_code = lax.optimization_barrier((ask_code, own_code, upper_code))
    far_upper = swap(outgoing_upper, "box", far_mask)
    far_code = swap(ask_code, "box", 1)

    places = table_lower.shape[0]
    table, source = kernel_call(
        widen_body,
        [struct((places, 2 * low, lanes), F32), struct((boxes + 1, 2 * low, lanes), F32)],
        [],
        [table_lower.reshape(-1, 2 * low, lanes), outgoing_lower.reshape(-1, 2 * low, lanes)],
        "widen",
        scratch=[
            pltpu.VMEM((places, 2 * low, lanes), BF16),
            pltpu.VMEM((boxes, 2 * low, lanes), BF16),
            pltpu.SemaphoreType.DMA((3,)),
        ],
        held=2,
    )
    outer, inner = list(range(peers - 1, peers // 2 - 1, -1)), list(range(peers // 2 - 1, -1, -1))

    def sums(groups, outs, codes, order, name):
        return kernel_call(
            functools.partial(sums_body, groups, per, entries),
            outs,
            [order, *codes],
            [table, source],
            name,
        )

    own_shape = struct((per, 2 * low, lanes), F32)
    far_shape = struct((len(outer) * per, 2 * low, lanes), BF16)
    (first,) = sums([(tuple(outer), 0)], [far_shape], [far_code], me, "sums_first")
    got_outer = swap(first, "box", 1)

    children = angles_lower.shape[0]
    part_rows = 4 * rows + children * low // 2
    held = top_patterns.shape[2]
    top = top_patterns.reshape(4 * held, -1)
    parts = kernel_call(
        functools.partial(early_body, peers, rows),
        [struct((part_rows, wide), F32)] * peers,
        [after(me, first)],
        [top, theta_upper, phi_upper, angles_lower],
        "early",
        scratch=[
            pltpu.VMEM((4, peers, held, wide), F32),
            pltpu.VMEM((4, peers, rows, wide), F32),
            *(pltpu.VMEM(a.shape, a.dtype) for a in (top, theta_upper, phi_upper, angles_lower)),
            pltpu.SemaphoreType.DMA((4,)),
        ],
        held=4,
    )
    order = after(me, parts[0])
    parts = [swap(part, "angle", mask) if mask else part for mask, part in enumerate(parts)]
    second, *own_outer = sums(
        [(tuple(inner), 0)] + [((mask,), 1) for mask in outer],
        [far_shape] + [own_shape] * len(outer),
        [far_code, own_code],
        order,
        "sums_second",
    )
    orders, angles = switch_theta.shape
    azimuths = switch_phi.shape[1]
    shifted, trig, expand, mix = kernel_call(
        functools.partial(shift_body, peers, rows, low),
        [
            struct((upper_boxes, 2, rows, wide), F32),
            struct((2, children, peers, low, lanes), F32),
            struct((2, 2 * orders, angles), BF16),
            struct((2 * azimuths, 2 * azimuths), BF16),
        ],
        [after(me, second)],
        [*parts, angles_upper, switch_theta, switch_phi],
        "shift",
        scratch=[
            *(pltpu.VMEM(a.shape, a.dtype) for a in (angles_upper, switch_theta, switch_phi)),
            pltpu.SemaphoreType.DMA((3,)),
        ],
        held=3,
    )
    got_inner = swap(after(second, trig), "box", 1)
    trig = trig.reshape(2, children, peers * low, lanes)
    lows = dict(zip(outer, join(own_outer, got_outer), strict=True))
    own_inner = sums(
        [((mask,), 0) for mask in inner],
        [own_shape] * len(inner),
        [own_code],
        after(me, lows[outer[0]]),
        "sums_third",
    )
    ups = kernel_call(
        functools.partial(upper_body, peers, entries),
        [struct((upper_per, 2 * rows, lanes), BF16)] * peers,
        [after(me, own_inner[0]), upper_code],
        [outgoing_upper, far_upper, table_upper, shifted, phi_lower],
        "upper",
        scratch=[
            pltpu.VMEM((2 * upper_boxes, 2, rows, wide), F32),
            pltpu.VMEM((upper_boxes, 2, rows, wide), F32),
        ],
    )
    ups = [swap(value, "angle", mask) if mask else value for mask, value in enumerate(ups)]
    lows.update(zip(inner, join(own_inner, got_inner), strict=True))
    lows = [swap(lows[mask], "angle", mask) if mask else lows[mask] for mask in range(peers)]

    whole = lambda shape: pl.BlockSpec(shape, lambda b: (0,) * len(shape))
    out = pl.pallas_call(
        functools.partial(final_body, peers),
        out_shape=struct((per * 2 * orders, azimuths), F32),
        grid=(upper_per,),
        in_specs=[SM]
        + [pl.BlockSpec((1, 2 * rows, lanes), lambda b: (b, 0, 0))] * peers
        + [pl.BlockSpec((children, 2 * low, lanes), lambda b: (b, 0, 0))] * peers
        + [whole(trig.shape), whole(theta_lower.shape), whole(mix.shape), whole(expand.shape)],
        out_specs=pl.BlockSpec((children * 2 * orders, azimuths), lambda b: (b, 0)),
        scratch_shapes=[
            pltpu.VMEM((2, peers, rows, lanes), F32),
            pltpu.VMEM((children, 2, peers, low, lanes), F32),
            pltpu.VMEM((children * peers * low, 2 * lanes), BF16),
        ],
        compiler_params=pltpu.CompilerParams(vmem_limit_bytes=16 << 20),
        name="expand",
    )(me, *ups, *lows, trig, theta_lower, mix, expand)
    out = out.reshape(per, orders, 2, azimuths)
    return jnp.transpose(out, (0, 2, 1, 3)).reshape(per, 2, orders * azimuths)


def solution(mesh):
    return jax.shard_map(
        per_device,
        mesh=mesh,
        in_specs=(
            P("box", None, "angle", None),
            P(),
            P(),
            P(None, "angle", None),
            P(None, None, "angle", None),
            P("box", None, "angle", None),
            P("box", None),
            P("box", None),
            P(),
            P(),
            P(None, "angle", None),
            P(None, None, "angle", None),
            P("box", None, "angle", None),
            P("box", None),
            P("box", None),
            P(),
            P(),
        ),
        out_specs=P(("box", "angle"), None, None),
        check_vma=False,
    )
```

```python
import functools

import jax
import jax.numpy as jnp
from jax import lax
from jax.experimental import pallas as pl
from jax.experimental.pallas import tpu as pltpu
from jax.sharding import PartitionSpec as P

F32, BF16 = jnp.float32, jnp.bfloat16
VM = pl.BlockSpec(memory_space=pltpu.VMEM)
SM = pl.BlockSpec(memory_space=pltpu.SMEM)
HB = pl.BlockSpec(memory_space=pltpu.HBM)
SHIFT = 9
NT = (((1,), (1,)), ((), ()))


def swap(value, axis, mask):
    pairs = [(source, source ^ mask) for source in range(lax.axis_size(axis))]
    return lax.ppermute(value, axis, pairs)


def after(value, *others):
    return lax.optimization_barrier((value, *others))[0]


def kernel_call(body, outs, scalars, arrays, name, scratch=(), held=0, vmem=6 << 20, away=0):
    near = len(arrays) - held
    return pl.pallas_call(
        body,
        out_shape=outs,
        in_specs=[SM] * len(scalars) + [VM] * near + [HB] * held,
        out_specs=[VM] * (len(outs) - away) + [HB] * away,
        scratch_shapes=list(scratch),
        compiler_params=pltpu.CompilerParams(vmem_limit_bytes=vmem),
        cost_estimate=pl.CostEstimate(flops=4000000000, bytes_accessed=1, transcendentals=0),
        name=name,
    )(*scalars, *arrays)


def fetch(pairs, sems):
    copies = [pltpu.make_async_copy(a, b, sems.at[k]) for k, (a, b) in enumerate(pairs)]
    for copy in copies:
        copy.start()
    return copies


def split_dot(left, value, dims):
    high = value.astype(BF16)
    low = (value - high.astype(F32)).astype(BF16)
    return lax.dot_general(left, high, dims, preferred_element_type=F32) + lax.dot_general(
        left, low, dims, preferred_element_type=F32
    )


def box_sum(box, entries, code, table, source):
    rows = table.shape[1] // 2
    real = imag = None
    for entry in range(entries):
        word = code[entry, box]
        factor = table[word & ((1 << SHIFT) - 1)]
        value = source[word >> SHIFT]
        fr, fi, sr, si = factor[:rows], factor[rows:], value[:rows], value[rows:]
        re, im = fr * sr - fi * si, fr * si + fi * sr
        real = re if real is None else real + re
        imag = im if imag is None else imag + im
    return real, imag


def sums_body(groups, per, entries, me, *refs):
    codes = max(which for _, which in groups) + 1
    code_refs, (table, source), outs = refs[:codes], refs[codes : codes + 2], refs[codes + 2 :]
    rows = table.shape[1] // 2
    for (masks, which), out in zip(groups, outs, strict=True):
        for place, mask in enumerate(masks):
            first = jnp.bitwise_xor(me[0], mask) * per

            def one(i, carry, first=first, place=place, which=which, out=out):
                real, imag = box_sum(first + i, entries, code_refs[which], table, source)
                out[place * per + i, 0:rows] = real.astype(out.dtype)
                out[place * per + i, rows:] = imag.astype(out.dtype)
                return carry

            lax.fori_loop(0, per, one, 0, unroll=2)


def first_body(groups, per, entries, me, code, table, source, out, *refs):
    table_out, source_out, table_in, source_in, wide_table, wide_source, sems, back = refs
    count, total = source.shape[0], table.shape[0]
    step = -(-total // 4)
    spans = [(k, min(k + step, total)) for k in range(0, total, step)]
    pairs = [(source, source_in)]
    pairs += [(table.at[lo:hi], table_in.at[lo:hi]) for lo, hi in spans]
    copies = fetch(pairs, sems)
    copies[0].wait()
    wide_source[0:count] = source_in[...].astype(F32)
    wide_source[count] = jnp.zeros(source.shape[1:], F32)
    for copy, (lo, hi) in zip(copies[1:], spans, strict=True):
        copy.wait()
        wide_table[lo:hi] = table_in[lo:hi].astype(F32)
    copies = fetch([(wide_table, table_out), (wide_source, source_out)], back)
    sums_body(groups, per, entries, me, code, wide_table, wide_source, out)
    for copy in copies:
        copy.wait()


def early_body(peers, rows, me, *refs):
    near, outs = refs[:4], refs[4 : 4 + peers]
    padded, summed, top, theta, phi, angles, sems = refs[4 + peers :]
    held = top.shape[0] // 4
    for copy in fetch(list(zip(near, (top, theta, phi, angles), strict=True)), sems):
        copy.wait()
    narrowed = lax.dot_general(top[...], phi[...], NT, preferred_element_type=F32)
    padded[...] = jnp.zeros(padded.shape, F32)
    for k in range(4):
        padded[k, me[0]] = narrowed[k * held : (k + 1) * held]
    for k in range(4):
        full = padded[k].reshape(peers * held, narrowed.shape[1])
        part = split_dot(theta[...], full, (((1,), (0,)), ((), ())))
        summed[k] = part.reshape(peers, rows, narrowed.shape[1])
    low = angles.shape[1]
    half = angles.shape[0] // 2
    for mask, out in enumerate(outs):
        for k in range(4):
            out[k * rows : (k + 1) * rows] = summed[k, jnp.bitwise_xor(me[0], mask)]
        for c in range(half):
            start = 4 * rows + c * low
            out[start : start + low, 0:128] = angles[c]
            out[start : start + low, 128:256] = angles[half + c]


def shift_body(peers, rows, low, me, *refs):
    parts, near = refs[:peers], refs[peers : peers + 3]
    shifted, trig, expand, mix, angles, theta, phi, sems = refs[peers + 3 :]
    for copy in fetch(list(zip(near, (angles, theta, phi), strict=True)), sems):
        copy.wait()
    orders = theta.shape[0]
    line = lax.broadcasted_iota(jnp.int32, (2 * orders, orders), 0)
    column = lax.broadcasted_iota(jnp.int32, (2 * orders, orders), 1)
    for c in range(2):
        pick = (line == 2 * column + c).astype(F32).astype(BF16)
        spread = jnp.dot(pick, theta[...], preferred_element_type=F32)
        expand[c] = spread.astype(BF16)
    size = phi.shape[1]
    mix[0:size, 0:size] = phi[0]
    mix[0:size, size:] = -phi[1]
    mix[size:, 0:size] = phi[1]
    mix[size:, size:] = phi[0]
    children = angles.shape[0]
    half = children // 2
    for c in range(children):
        cosine, sine = jnp.cos(angles[c]), jnp.sin(angles[c])
        for b in range(2):
            re = parts[0][2 * b * rows : (2 * b + 1) * rows]
            im = parts[0][(2 * b + 1) * rows : (2 * b + 2) * rows]
            for part in parts[1:]:
                re = re + part[2 * b * rows : (2 * b + 1) * rows]
                im = im + part[(2 * b + 1) * rows : (2 * b + 2) * rows]
            shifted[b * children + c, 0] = re * cosine - im * sine
            shifted[b * children + c, 1] = re * sine + im * cosine
    for mask, part in enumerate(parts):
        for c in range(half):
            start = 4 * rows + c * low
            for side in range(2):
                angle = part[start : start + low, side * 128 : side * 128 + 128]
                place = jnp.bitwise_xor(me[0], mask)
                trig[0, side * half + c, place] = jnp.cos(angle)
                trig[1, side * half + c, place] = jnp.sin(angle)


def join(owns, got):
    def body(*refs):
        first = 0
        count = len(owns)
        for own, out in zip(refs[:count], refs[count + 1 :], strict=True):
            size = own.shape[0]
            out[...] = (own[...] + refs[count][first : first + size].astype(F32)).astype(BF16)
            first += size

    return kernel_call(body, [struct(a.shape, BF16) for a in owns], [], [*owns, got], "join")


def upper_body(peers, entries, me, home, ids, offsets, own, far, table, shifted, phi, *refs):
    outs, (pool, whole) = refs[:peers], refs[peers:]
    boxes, _, rows, _ = own.shape
    pool[0:boxes] = own[...].astype(F32)
    pool[boxes:] = far[...].astype(F32)
    step = min(16, rows)
    per = boxes // peers

    def one(box, carry):
        for r in range(0, rows, step):
            span = slice(r, r + step)
            real, imag = shifted[box, 0, span], shifted[box, 1, span]
            for entry in range(entries):
                offset, ident = offsets[box, entry], ids[box, entry]
                place = lax.rem(ident, boxes)
                place = jnp.where(ident - place == home[0] * boxes, place, place + boxes)
                fr, fi = table[offset, 0, span].astype(F32), table[offset, 1, span].astype(F32)
                sr, si = pool[place, 0, span], pool[place, 1, span]
                real = real + (fr * sr - fi * si)
                imag = imag + (fr * si + fi * sr)
            whole[box, 0, span] = real
            whole[box, 1, span] = imag
        return carry

    lax.fori_loop(0, boxes, one, 0)
    for mask in range(peers):
        first = jnp.bitwise_xor(me[0], mask) * per
        for i in range(per):
            for c in range(2):
                incoming = whole[first + i, c].astype(BF16)
                narrow = lax.dot_general(incoming, phi[...], NT, preferred_element_type=F32)
                outs[mask][i, c * rows : (c + 1) * rows] = narrow.astype(BF16)


def final_body(peers, parents, me, *refs):
    ups, lows = refs[:peers], refs[peers : 2 * peers]
    trig, theta, mix, expand, out, rows_up, rows_low, pattern, ready, sems = refs[2 * peers :]
    children, rows = trig.shape[1], trig.shape[2]
    high_rows, low_rows = rows_up.shape[3], rows_low.shape[3]
    both = jnp.concatenate([expand[0], expand[1]], axis=1)
    size = both.shape[0]
    block_rows = children * size
    copies = []
    for mask in range(peers):
        place = jnp.bitwise_xor(me[0], mask)
        for c in range(2):
            for b in range(parents):
                rows_up[b, c, place] = ups[mask][b, c * high_rows : (c + 1) * high_rows].astype(F32)
            rows_low[:, c, place] = lows[mask][:, c * low_rows : (c + 1) * low_rows].astype(F32)
    for b in range(parents):
        coarse = []
        for c in range(2):
            full = rows_up[b, c].reshape(peers * high_rows, 128).astype(BF16)
            coarse.append(jnp.dot(theta[...], full, preferred_element_type=F32))
        for k in range(children):
            cosine, sine = trig[0, k], trig[1, k]
            box = b * children + k
            real = coarse[0] * cosine - coarse[1] * sine + rows_low[box, 0].reshape(rows, 128)
            imag = coarse[0] * sine + coarse[1] * cosine + rows_low[box, 1].reshape(rows, 128)
            pattern[k * rows : (k + 1) * rows, 0:128] = real.astype(BF16)
            pattern[k * rows : (k + 1) * rows, 128:256] = imag.astype(BF16)
        for k in range(0, children, 2):
            block = pattern[k * rows : (k + 2) * rows]
            turned = lax.dot_general(block, mix[...], NT, preferred_element_type=F32)
            one, two = turned[:rows], turned[rows:]
            stacked = jnp.concatenate(
                [
                    jnp.concatenate([one[:, :128], two[:, :128]], axis=1),
                    jnp.concatenate([one[:, 128:], two[:, 128:]], axis=1),
                ],
                axis=0,
            )
            result = split_dot(both, stacked, (((1,), (0,)), ((), ())))
            start = b * block_rows + k * size
            ready[start : start + size] = result[:, :128]
            ready[start + size : start + 2 * size] = result[:, 128:]
        span = pl.ds(b * block_rows, block_rows)
        copies += fetch([(ready.at[span], out.at[span])], sems.at[pl.ds(b, 1)])
    for copy in copies:
        copy.wait()


def struct(shape, dtype):
    return jax.ShapeDtypeStruct(shape, dtype)


def per_device(
    top_patterns,
    theta_upper,
    phi_upper,
    angles_upper,
    table_upper,
    outgoing_upper,
    list_upper,
    offset_upper,
    theta_lower,
    phi_lower,
    angles_lower,
    table_lower,
    outgoing_lower,
    list_lower,
    offset_lower,
    switch_theta,
    switch_phi,
):
    peers = lax.axis_size("angle")
    home = lax.axis_index("box")
    me = lax.axis_index("angle").astype(jnp.int32).reshape(1)
    far_mask = lax.axis_size("box") // 2
    boxes, _, low, lanes = outgoing_lower.shape
    per = boxes // peers
    entries = list_lower.shape[1]
    upper_boxes, _, rows, wide = outgoing_upper.shape
    upper_per = upper_boxes // peers

    other = list_lower.T // boxes != home
    spot = list_lower.T % boxes
    ask_code = (jnp.where(other, spot, boxes) << SHIFT) + offset_lower.T
    own_code = (jnp.where(other, boxes, spot) << SHIFT) + offset_lower.T
    far_code = swap(ask_code, "box", 1)
    far_upper = swap(outgoing_upper, "box", far_mask)

    places = table_lower.shape[0]
    outer, inner = list(range(peers - 1, peers // 2 - 1, -1)), list(range(peers // 2 - 1, -1, -1))

    def sums(groups, outs, codes, order, name):
        return kernel_call(
            functools.partial(sums_body, groups, per, entries),
            outs,
            [order, *codes],
            [table, source],
            name,
        )

    own_shape = struct((per, 2 * low, lanes), F32)
    far_shape = struct((len(outer) * per, 2 * low, lanes), BF16)
    first, table, source = kernel_call(
        functools.partial(first_body, [(tuple(outer), 0)], per, entries),
        [
            far_shape,
            struct((places, 2 * low, lanes), F32),
            struct((boxes + 1, 2 * low, lanes), F32),
        ],
        [me, far_code],
        [table_lower.reshape(-1, 2 * low, lanes), outgoing_lower.reshape(-1, 2 * low, lanes)],
        "sums_first",
        scratch=[
            pltpu.VMEM((places, 2 * low, lanes), BF16),
            pltpu.VMEM((boxes, 2 * low, lanes), BF16),
            pltpu.VMEM((places, 2 * low, lanes), F32),
            pltpu.VMEM((boxes + 1, 2 * low, lanes), F32),
            pltpu.SemaphoreType.DMA((5,)),
            pltpu.SemaphoreType.DMA((2,)),
        ],
        held=2,
        away=2,
        vmem=53 << 20,
    )
    got_outer = swap(first, "box", 1)

    children = angles_lower.shape[0]
    part_rows = 4 * rows + children * low // 2
    held = top_patterns.shape[2]
    top = top_patterns.reshape(4 * held, -1)
    parts = kernel_call(
        functools.partial(early_body, peers, rows),
        [struct((part_rows, wide), F32)] * peers,
        [after(me, first)],
        [top, theta_upper, phi_upper, angles_lower],
        "early",
        scratch=[
            pltpu.VMEM((4, peers, held, wide), F32),
            pltpu.VMEM((4, peers, rows, wide), F32),
            *(pltpu.VMEM(a.shape, a.dtype) for a in (top, theta_upper, phi_upper, angles_lower)),
            pltpu.SemaphoreType.DMA((4,)),
        ],
        held=4,
    )
    order = after(me, parts[0])
    parts = [swap(part, "angle", mask) if mask else part for mask, part in enumerate(parts)]
    second, *own_outer = sums(
        [(tuple(inner), 0)] + [((mask,), 1) for mask in outer],
        [far_shape] + [own_shape] * len(outer),
        [far_code, own_code],
        order,
        "sums_second",
    )
    orders, angles = switch_theta.shape
    azimuths = switch_phi.shape[1]
    shifted, trig, expand, mix = kernel_call(
        functools.partial(shift_body, peers, rows, low),
        [
            struct((upper_boxes, 2, rows, wide), F32),
            struct((2, children, peers, low, lanes), F32),
            struct((2, 2 * orders, angles), BF16),
            struct((2 * azimuths, 2 * azimuths), BF16),
        ],
        [after(me, second)],
        [*parts, angles_upper, switch_theta, switch_phi],
        "shift",
        scratch=[
            *(pltpu.VMEM(a.shape, a.dtype) for a in (angles_upper, switch_theta, switch_phi)),
            pltpu.SemaphoreType.DMA((3,)),
        ],
        held=3,
    )
    got_inner = swap(after(second, trig), "box", 1)
    trig = trig.reshape(2, children, peers * low, lanes)
    lows = dict(zip(outer, join(own_outer, got_outer), strict=True))
    own_inner = sums(
        [((mask,), 0) for mask in inner],
        [own_shape] * len(inner),
        [own_code],
        after(me, lows[outer[0]]),
        "sums_third",
    )
    ups = kernel_call(
        functools.partial(upper_body, peers, entries),
        [struct((upper_per, 2 * rows, lanes), BF16)] * peers,
        [after(me, own_inner[0]), home.astype(jnp.int32).reshape(1), list_upper, offset_upper],
        [outgoing_upper, far_upper, table_upper, shifted, phi_lower],
        "upper",
        scratch=[
            pltpu.VMEM((2 * upper_boxes, 2, rows, wide), F32),
            pltpu.VMEM((upper_boxes, 2, rows, wide), F32),
        ],
    )
    own_inner = [after(own_inner[0], ups[0]), *own_inner[1:]]
    ups = [swap(value, "angle", mask) if mask else value for mask, value in enumerate(ups)]
    lows.update(zip(inner, join(own_inner, got_inner), strict=True))
    lows = [swap(lows[mask], "angle", mask) if mask else lows[mask] for mask in range(peers)]

    (out,) = kernel_call(
        functools.partial(final_body, peers, upper_per),
        [struct((per * 2 * orders, azimuths), F32)],
        [me],
        [*ups, *lows, trig, theta_lower, mix, expand],
        "expand",
        scratch=[
            pltpu.VMEM((upper_per, 2, peers, rows, lanes), F32),
            pltpu.VMEM((per, 2, peers, low, lanes), F32),
            pltpu.VMEM((children * peers * low, 2 * lanes), BF16),
            pltpu.VMEM((per * 2 * orders, azimuths), F32),
            pltpu.SemaphoreType.DMA((upper_per,)),
        ],
        away=1,
        vmem=12 << 20,
    )
    out = out.reshape(per, orders, 2, azimuths)
    return jnp.transpose(out, (0, 2, 1, 3)).reshape(per, 2, orders * azimuths)


def solution(mesh):
    return jax.shard_map(
        per_device,
        mesh=mesh,
        in_specs=(
            P("box", None, "angle", None),
            P(),
            P(),
            P(None, "angle", None),
            P(None, None, "angle", None),
            P("box", None, "angle", None),
            P("box", None),
            P("box", None),
            P(),
            P(),
            P(None, "angle", None),
            P(None, None, "angle", None),
            P("box", None, "angle", None),
            P("box", None),
            P("box", None),
            P(),
            P(),
        ),
        out_specs=P(("box", "angle"), None, None),
        check_vma=False,
    )
```

```python
import functools

import jax
import jax.numpy as jnp
from jax import lax
from jax.experimental import pallas as pl
from jax.experimental.pallas import tpu as pltpu
from jax.sharding import PartitionSpec as P

F32, BF16 = jnp.float32, jnp.bfloat16
VM = pl.BlockSpec(memory_space=pltpu.VMEM)
SM = pl.BlockSpec(memory_space=pltpu.SMEM)
HB = pl.BlockSpec(memory_space=pltpu.HBM)
SHIFT = 9
NT = (((1,), (1,)), ((), ()))


def swap(value, axis, mask):
    pairs = [(source, source ^ mask) for source in range(lax.axis_size(axis))]
    return lax.ppermute(value, axis, pairs)


def after(value, *others):
    return lax.optimization_barrier((value, *others))[0]


def kernel_call(body, outs, scalars, arrays, name, scratch=(), held=0, vmem=6 << 20, away=0, flops=4 << 30):
    near = len(arrays) - held
    return pl.pallas_call(
        body,
        out_shape=outs,
        in_specs=[SM] * len(scalars) + [VM] * near + [HB] * held,
        out_specs=[VM] * (len(outs) - away) + [HB] * away,
        scratch_shapes=list(scratch),
        compiler_params=pltpu.CompilerParams(vmem_limit_bytes=vmem),
        cost_estimate=pl.CostEstimate(flops=flops, bytes_accessed=1, transcendentals=0),
        name=name,
    )(*scalars, *arrays)


def fetch(pairs, sems):
    copies = [pltpu.make_async_copy(a, b, sems.at[k]) for k, (a, b) in enumerate(pairs)]
    for copy in copies:
        copy.start()
    return copies


def split_dot(left, value, dims):
    high = value.astype(BF16)
    low = (value - high.astype(F32)).astype(BF16)
    return lax.dot_general(left, high, dims, preferred_element_type=F32) + lax.dot_general(
        left, low, dims, preferred_element_type=F32
    )


def box_sum(box, entries, code, table, source):
    rows = table.shape[1] // 2
    real = imag = None
    for entry in range(entries):
        word = code[entry, box]
        factor = table[word & ((1 << SHIFT) - 1)]
        value = source[word >> SHIFT]
        fr, fi, sr, si = factor[:rows], factor[rows:], value[:rows], value[rows:]
        re, im = fr * sr - fi * si, fr * si + fi * sr
        real = re if real is None else real + re
        imag = im if imag is None else imag + im
    return real, imag


def sums_body(groups, per, entries, me, *refs):
    codes = max(which for _, which in groups) + 1
    code_refs, (table, source), outs = refs[:codes], refs[codes : codes + 2], refs[codes + 2 :]
    rows = table.shape[1] // 2
    for (masks, which), out in zip(groups, outs, strict=True):
        for place, mask in enumerate(masks):
            first = jnp.bitwise_xor(me[0], mask) * per

            def one(i, carry, first=first, place=place, which=which, out=out):
                real, imag = box_sum(first + i, entries, code_refs[which], table, source)
                out[place * per + i, 0:rows] = real.astype(out.dtype)
                out[place * per + i, rows:] = imag.astype(out.dtype)
                return carry

            lax.fori_loop(0, per, one, 0, unroll=2)


def first_body(groups, per, entries, me, code, table, source, out, *refs):
    table_out, source_out, table_in, source_in, wide_table, wide_source, sems, back = refs
    count, total = source.shape[0], table.shape[0]
    step = -(-total // 4)
    spans = [(k, min(k + step, total)) for k in range(0, total, step)]
    pairs = [(source, source_in)]
    pairs += [(table.at[lo:hi], table_in.at[lo:hi]) for lo, hi in spans]
    copies = fetch(pairs, sems)
    copies[0].wait()
    wide_source[0:count] = source_in[...].astype(F32)
    wide_source[count] = jnp.zeros(source.shape[1:], F32)
    for copy, (lo, hi) in zip(copies[1:], spans, strict=True):
        copy.wait()
        wide_table[lo:hi] = table_in[lo:hi].astype(F32)
    copies = fetch([(wide_table, table_out), (wide_source, source_out)], back)
    sums_body(groups, per, entries, me, code, wide_table, wide_source, out)
    for copy in copies:
        copy.wait()


def early_body(peers, rows, me, *refs):
    near, outs = refs[:4], refs[4 : 4 + peers]
    padded, summed, top, theta, phi, angles, sems = refs[4 + peers :]
    held = top.shape[0] // 4
    for copy in fetch(list(zip(near, (top, theta, phi, angles), strict=True)), sems):
        copy.wait()
    narrowed = lax.dot_general(top[...], phi[...], NT, preferred_element_type=F32)
    padded[...] = jnp.zeros(padded.shape, F32)
    for k in range(4):
        padded[k, me[0]] = narrowed[k * held : (k + 1) * held]
    for k in range(4):
        full = padded[k].reshape(peers * held, narrowed.shape[1])
        part = split_dot(theta[...], full, (((1,), (0,)), ((), ())))
        summed[k] = part.reshape(peers, rows, narrowed.shape[1])
    low = angles.shape[1]
    half = angles.shape[0] // 2
    for mask, out in enumerate(outs):
        for k in range(4):
            out[k * rows : (k + 1) * rows] = summed[k, jnp.bitwise_xor(me[0], mask)]
        for c in range(half):
            start = 4 * rows + c * low
            out[start : start + low, 0:128] = angles[c]
            out[start : start + low, 128:256] = angles[half + c]


def shift_body(peers, rows, low, me, *refs):
    parts, near = refs[:peers], refs[peers : peers + 3]
    shifted, trig, expand, mix, angles, theta, phi, sems = refs[peers + 3 :]
    for copy in fetch(list(zip(near, (angles, theta, phi), strict=True)), sems):
        copy.wait()
    orders = theta.shape[0]
    line = lax.broadcasted_iota(jnp.int32, (2 * orders, orders), 0)
    column = lax.broadcasted_iota(jnp.int32, (2 * orders, orders), 1)
    for c in range(2):
        pick = (line == 2 * column + c).astype(F32).astype(BF16)
        spread = jnp.dot(pick, theta[...], preferred_element_type=F32)
        expand[c] = spread.astype(BF16)
    size = phi.shape[1]
    mix[0:size, 0:size] = phi[0]
    mix[0:size, size:] = -phi[1]
    mix[size:, 0:size] = phi[1]
    mix[size:, size:] = phi[0]
    children = angles.shape[0]
    half = children // 2
    for c in range(children):
        cosine, sine = jnp.cos(angles[c]), jnp.sin(angles[c])
        for b in range(2):
            re = parts[0][2 * b * rows : (2 * b + 1) * rows]
            im = parts[0][(2 * b + 1) * rows : (2 * b + 2) * rows]
            for part in parts[1:]:
                re = re + part[2 * b * rows : (2 * b + 1) * rows]
                im = im + part[(2 * b + 1) * rows : (2 * b + 2) * rows]
            shifted[b * children + c, 0] = re * cosine - im * sine
            shifted[b * children + c, 1] = re * sine + im * cosine
    for mask, part in enumerate(parts):
        for c in range(half):
            start = 4 * rows + c * low
            for side in range(2):
                angle = part[start : start + low, side * 128 : side * 128 + 128]
                place = jnp.bitwise_xor(me[0], mask)
                trig[0, side * half + c, place] = jnp.cos(angle)
                trig[1, side * half + c, place] = jnp.sin(angle)


def join(owns, got, extra=None):
    shapes = [struct(a.shape, BF16) for a in owns]
    if extra is not None:
        shapes[0] = struct((owns[0].shape[0] + extra.shape[0], *extra.shape[1:]), BF16)

    def body(*refs):
        first = 0
        count = len(owns)
        outs = refs[-count:]
        for own, out in zip(refs[:count], outs, strict=True):
            size = own.shape[0]
            out[0:size] = (own[...] + refs[count][first : first + size].astype(F32)).astype(BF16)
            first += size
        if extra is not None:
            outs[0][owns[0].shape[0] :] = refs[count + 1][...]

    more = [] if extra is None else [extra]
    return kernel_call(body, shapes, [], [*owns, got, *more], "join", flops=1)


def upper_body(peers, entries, me, home, ids, offsets, own, far, table, shifted, phi, *refs):
    outs, (pool, whole) = refs[:peers], refs[peers:]
    boxes, _, rows, _ = own.shape
    pool[0:boxes] = own[...].astype(F32)
    pool[boxes:] = far[...].astype(F32)
    step = min(16, rows)
    per = boxes // peers

    def one(box, carry):
        for r in range(0, rows, step):
            span = slice(r, r + step)
            real, imag = shifted[box, 0, span], shifted[box, 1, span]
            for entry in range(entries):
                offset, ident = offsets[box, entry], ids[box, entry]
                place = lax.rem(ident, boxes)
                place = jnp.where(ident - place == home[0] * boxes, place, place + boxes)
                fr, fi = table[offset, 0, span].astype(F32), table[offset, 1, span].astype(F32)
                sr, si = pool[place, 0, span], pool[place, 1, span]
                real = real + (fr * sr - fi * si)
                imag = imag + (fr * si + fi * sr)
            whole[box, 0, span] = real
            whole[box, 1, span] = imag
        return carry

    lax.fori_loop(0, boxes, one, 0)
    for mask in range(peers):
        first = jnp.bitwise_xor(me[0], mask) * per
        for i in range(per):
            for c in range(2):
                incoming = whole[first + i, c].astype(BF16)
                narrow = lax.dot_general(incoming, phi[...], NT, preferred_element_type=F32)
                outs[mask][i, c * rows : (c + 1) * rows] = narrow.astype(BF16)


def place_body(*refs):
    count = len(refs) // 2
    for low, out in zip(refs[:count], refs[count:], strict=True):
        out[...] = low[...].astype(F32)


def final_body(peers, parents, me, *refs):
    ups, lows = list(refs[: peers - 1]), refs[peers - 1 : 2 * peers - 1]
    ups.insert(1, None)
    trig, theta, mix, expand, out, rows_up, rows_low, pattern, ready, sems = refs[2 * peers - 1 :]
    children, rows = trig.shape[1], trig.shape[2]
    high_rows, low_rows = rows_up.shape[3], rows_low.shape[3]
    both = jnp.concatenate([expand[0], expand[1]], axis=1)
    size = both.shape[0]
    block_rows = children * size
    copies = []
    for mask in range(peers):
        place = jnp.bitwise_xor(me[0], mask)
        for c in range(2):
            for b in range(parents):
                if mask == 1:
                    piece = lows[1][parents * children + 2 * b + c]
                else:
                    piece = ups[mask][b, c * high_rows : (c + 1) * high_rows]
                rows_up[b, c, place] = piece.astype(F32)
            piece = lows[mask][0 : parents * children, c * low_rows : (c + 1) * low_rows]
            rows_low[:, c, place] = piece.astype(F32)
    for b in range(parents):
        coarse = []
        for c in range(2):
            full = rows_up[b, c].reshape(peers * high_rows, 128).astype(BF16)
            coarse.append(jnp.dot(theta[...], full, preferred_element_type=F32))
        for k in range(children):
            cosine, sine = trig[0, k], trig[1, k]
            box = b * children + k
            real = coarse[0] * cosine - coarse[1] * sine + rows_low[box, 0].reshape(rows, 128)
            imag = coarse[0] * sine + coarse[1] * cosine + rows_low[box, 1].reshape(rows, 128)
            pattern[k * rows : (k + 1) * rows, 0:128] = real.astype(BF16)
            pattern[k * rows : (k + 1) * rows, 128:256] = imag.astype(BF16)
        for k in range(0, children, 2):
            block = pattern[k * rows : (k + 2) * rows]
            turned = lax.dot_general(block, mix[...], NT, preferred_element_type=F32)
            one, two = turned[:rows], turned[rows:]
            stacked = jnp.concatenate(
                [
                    jnp.concatenate([one[:, :128], two[:, :128]], axis=1),
                    jnp.concatenate([one[:, 128:], two[:, 128:]], axis=1),
                ],
                axis=0,
            )
            result = split_dot(both, stacked, (((1,), (0,)), ((), ())))
            start = b * block_rows + k * size
            ready[start : start + size] = result[:, :128]
            ready[start + size : start + 2 * size] = result[:, 128:]
        span = pl.ds(b * block_rows, block_rows)
        copies += fetch([(ready.at[span], out.at[span])], sems.at[pl.ds(b, 1)])
    for copy in copies:
        copy.wait()


def struct(shape, dtype):
    return jax.ShapeDtypeStruct(shape, dtype)


def per_device(
    top_patterns,
    theta_upper,
    phi_upper,
    angles_upper,
    table_upper,
    outgoing_upper,
    list_upper,
    offset_upper,
    theta_lower,
    phi_lower,
    angles_lower,
    table_lower,
    outgoing_lower,
    list_lower,
    offset_lower,
    switch_theta,
    switch_phi,
):
    peers = lax.axis_size("angle")
    home = lax.axis_index("box")
    me = lax.axis_index("angle").astype(jnp.int32).reshape(1)
    far_mask = lax.axis_size("box") // 2
    boxes, _, low, lanes = outgoing_lower.shape
    per = boxes // peers
    entries = list_lower.shape[1]
    upper_boxes, _, rows, wide = outgoing_upper.shape
    upper_per = upper_boxes // peers

    other = list_lower.T // boxes != home
    spot = list_lower.T % boxes
    ask_code = (jnp.where(other, spot, boxes) << SHIFT) + offset_lower.T
    own_code = (jnp.where(other, boxes, spot) << SHIFT) + offset_lower.T
    far_code = swap(ask_code, "box", 1)
    far_upper = swap(outgoing_upper, "box", far_mask)

    places = table_lower.shape[0]
    outer, inner = list(range(peers - 1, peers // 2 - 1, -1)), list(range(peers // 2 - 1, -1, -1))

    def sums(groups, outs, codes, order, name, flops=4 << 30):
        return kernel_call(
            functools.partial(sums_body, groups, per, entries),
            outs,
            [order, *codes],
            [table, source],
            name,
            flops=flops,
        )

    own_shape = struct((per, 2 * low, lanes), F32)
    far_shape = struct((len(outer) * per, 2 * low, lanes), BF16)
    first, table, source = kernel_call(
        functools.partial(first_body, [(tuple(outer), 0)], per, entries),
        [
            far_shape,
            struct((places, 2 * low, lanes), F32),
            struct((boxes + 1, 2 * low, lanes), F32),
        ],
        [me, far_code],
        [table_lower.reshape(-1, 2 * low, lanes), outgoing_lower.reshape(-1, 2 * low, lanes)],
        "sums_first",
        scratch=[
            pltpu.VMEM((places, 2 * low, lanes), BF16),
            pltpu.VMEM((boxes, 2 * low, lanes), BF16),
            pltpu.VMEM((places, 2 * low, lanes), F32),
            pltpu.VMEM((boxes + 1, 2 * low, lanes), F32),
            pltpu.SemaphoreType.DMA((5,)),
            pltpu.SemaphoreType.DMA((2,)),
        ],
        held=2,
        away=2,
        vmem=53 << 20,
    )
    got_outer = swap(first, "box", 1)

    children = angles_lower.shape[0]
    part_rows = 4 * rows + children * low // 2
    held = top_patterns.shape[2]
    top = top_patterns.reshape(4 * held, -1)
    parts = kernel_call(
        functools.partial(early_body, peers, rows),
        [struct((part_rows, wide), F32)] * peers,
        [after(me, first)],
        [top, theta_upper, phi_upper, angles_lower],
        "early",
        scratch=[
            pltpu.VMEM((4, peers, held, wide), F32),
            pltpu.VMEM((4, peers, rows, wide), F32),
            *(pltpu.VMEM(a.shape, a.dtype) for a in (top, theta_upper, phi_upper, angles_lower)),
            pltpu.SemaphoreType.DMA((4,)),
        ],
        held=4,
    )
    order = after(me, parts[0])
    parts = [swap(part, "angle", mask) if mask else part for mask, part in enumerate(parts)]
    (second,) = sums([(tuple(inner), 0)], [far_shape], [far_code], order, "sums_second")
    got_inner = swap(after(second, parts[1]), "box", 1)
    own_outer = sums(
        [((mask,), 0) for mask in outer],
        [own_shape] * len(outer),
        [own_code],
        after(me, second),
        "sums_third",
    )
    lows = dict(zip(outer, join(own_outer, got_outer), strict=True))
    orders, angles = switch_theta.shape
    azimuths = switch_phi.shape[1]
    shifted, trig, expand, mix = kernel_call(
        functools.partial(shift_body, peers, rows, low),
        [
            struct((upper_boxes, 2, rows, wide), F32),
            struct((2, children, peers, low, lanes), F32),
            struct((2, 2 * orders, angles), BF16),
            struct((2 * azimuths, 2 * azimuths), BF16),
        ],
        [after(me, lows[outer[0]])],
        [*parts, angles_upper, switch_theta, switch_phi],
        "shift",
        scratch=[
            *(pltpu.VMEM(a.shape, a.dtype) for a in (angles_upper, switch_theta, switch_phi)),
            pltpu.SemaphoreType.DMA((3,)),
        ],
        held=3,
    )
    trig = trig.reshape(2, children, peers * low, lanes)
    own_inner = sums(
        [((mask,), 0) for mask in inner],
        [own_shape] * len(inner),
        [own_code],
        after(me, trig),
        "sums_fourth",
    )
    ups = kernel_call(
        functools.partial(upper_body, peers, entries),
        [struct((upper_per, 2 * rows, lanes), BF16)] * peers,
        [after(me, own_inner[0]), home.astype(jnp.int32).reshape(1), list_upper, offset_upper],
        [outgoing_upper, far_upper, table_upper, shifted, phi_lower],
        "upper",
        scratch=[
            pltpu.VMEM((2 * upper_boxes, 2, rows, wide), F32),
            pltpu.VMEM((upper_boxes, 2, rows, wide), F32),
        ],
    )
    own_inner = [after(own_inner[0], ups[0]), *own_inner[1:]]
    near = ups[1].reshape(-1, 2 * low, lanes)
    lows.update(zip(inner, join(own_inner, got_inner, near), strict=True))
    ups = [swap(ups[mask], "angle", mask) if mask else ups[0] for mask in range(peers) if mask != 1]
    lows = [swap(lows[mask], "angle", mask) if mask else lows[mask] for mask in range(peers)]

    arrived = kernel_call(
        place_body,
        [struct(lows[mask].shape, F32) for mask in outer],
        [],
        [lows[mask] for mask in outer],
        "place",
    )
    lows = [*lows[: len(inner)], *reversed(arrived)]
    (out,) = kernel_call(
        functools.partial(final_body, peers, upper_per),
        [struct((per * 2 * orders, azimuths), F32)],
        [me],
        [*ups, *lows, trig, theta_lower, mix, expand],
        "expand",
        scratch=[
            pltpu.VMEM((upper_per, 2, peers, rows, lanes), F32),
            pltpu.VMEM((per, 2, peers, low, lanes), F32),
            pltpu.VMEM((children * peers * low, 2 * lanes), BF16),
            pltpu.VMEM((per * 2 * orders, azimuths), F32),
            pltpu.SemaphoreType.DMA((upper_per,)),
        ],
        away=1,
        vmem=12 << 20,
    )
    out = out.reshape(per, orders, 2, azimuths)
    return jnp.transpose(out, (0, 2, 1, 3)).reshape(per, 2, orders * azimuths)


def solution(mesh):
    return jax.shard_map(
        per_device,
        mesh=mesh,
        in_specs=(
            P("box", None, "angle", None),
            P(),
            P(),
            P(None, "angle", None),
            P(None, None, "angle", None),
            P("box", None, "angle", None),
            P("box", None),
            P("box", None),
            P(),
            P(),
            P(None, "angle", None),
            P(None, None, "angle", None),
            P("box", None, "angle", None),
            P("box", None),
            P("box", None),
            P(),
            P(),
        ),
        out_specs=P(("box", "angle"), None, None),
        check_vma=False,
    )
```

```python
import functools

import jax
import jax.numpy as jnp
from jax import lax
from jax.experimental import pallas as pl
from jax.experimental.pallas import tpu as pltpu
from jax.sharding import PartitionSpec as P

F32, BF16 = jnp.float32, jnp.bfloat16
VM = pl.BlockSpec(memory_space=pltpu.VMEM)
SM = pl.BlockSpec(memory_space=pltpu.SMEM)
HB = pl.BlockSpec(memory_space=pltpu.HBM)
SHIFT = 9
NT = (((1,), (1,)), ((), ()))


def swap(value, axis, mask):
    pairs = [(source, source ^ mask) for source in range(lax.axis_size(axis))]
    return lax.ppermute(value, axis, pairs)


COSTS = {"join": 0, "sums_third": 0, "shift": 0, "sums_fourth": 0, "upper_near": 0}


def after(value, *others):
    return lax.optimization_barrier((value, *others))[0]


def kernel_call(body, outs, scalars, arrays, name, scratch=(), held=0, vmem=6 << 20, away=0):
    near = len(arrays) - held
    return pl.pallas_call(
        body,
        out_shape=outs,
        in_specs=[SM] * len(scalars) + [VM] * near + [HB] * held,
        out_specs=[VM] * (len(outs) - away) + [HB] * away,
        scratch_shapes=list(scratch),
        compiler_params=pltpu.CompilerParams(vmem_limit_bytes=vmem),
        cost_estimate=pl.CostEstimate(flops=COSTS.get(name, 4) << 30, bytes_accessed=1, transcendentals=0),
        name=name,
    )(*scalars, *arrays)


def fetch(pairs, sems):
    copies = [pltpu.make_async_copy(a, b, sems.at[k]) for k, (a, b) in enumerate(pairs)]
    for copy in copies:
        copy.start()
    return copies


def split_dot(left, value, dims):
    high = value.astype(BF16)
    low = (value - high.astype(F32)).astype(BF16)
    return lax.dot_general(left, high, dims, preferred_element_type=F32) + lax.dot_general(
        left, low, dims, preferred_element_type=F32
    )


def box_sum(box, entries, code, table, source):
    rows = table.shape[1] // 2
    real = imag = None
    for entry in range(entries):
        word = code[entry, box]
        factor = table[word & ((1 << SHIFT) - 1)]
        value = source[word >> SHIFT]
        fr, fi, sr, si = factor[:rows], factor[rows:], value[:rows], value[rows:]
        re, im = fr * sr - fi * si, fr * si + fi * sr
        real = re if real is None else real + re
        imag = im if imag is None else imag + im
    return real, imag


def sums_body(groups, per, entries, me, *refs):
    codes = max(which for _, which in groups) + 1
    code_refs, (table, source), outs = refs[:codes], refs[codes : codes + 2], refs[codes + 2 :]
    rows = table.shape[1] // 2
    for (masks, which), out in zip(groups, outs, strict=True):
        for place, mask in enumerate(masks):
            first = jnp.bitwise_xor(me[0], mask) * per

            def one(i, carry, first=first, place=place, which=which, out=out):
                real, imag = box_sum(first + i, entries, code_refs[which], table, source)
                out[place * per + i, 0:rows] = real.astype(out.dtype)
                out[place * per + i, rows:] = imag.astype(out.dtype)
                return carry

            lax.fori_loop(0, per, one, 0, unroll=2)


def first_body(groups, per, entries, me, code, table, source, out, *refs):
    table_out, source_out, table_in, source_in, wide_table, wide_source, sems, back = refs
    count, total = source.shape[0], table.shape[0]
    step = -(-total // 4)
    spans = [(k, min(k + step, total)) for k in range(0, total, step)]
    pairs = [(source, source_in)]
    pairs += [(table.at[lo:hi], table_in.at[lo:hi]) for lo, hi in spans]
    copies = fetch(pairs, sems)
    copies[0].wait()
    wide_source[0:count] = source_in[...].astype(F32)
    wide_source[count] = jnp.zeros(source.shape[1:], F32)
    for copy, (lo, hi) in zip(copies[1:], spans, strict=True):
        copy.wait()
        wide_table[lo:hi] = table_in[lo:hi].astype(F32)
    copies = fetch([(wide_table, table_out), (wide_source, source_out)], back)
    sums_body(groups, per, entries, me, code, wide_table, wide_source, out)
    for copy in copies:
        copy.wait()


def early_body(peers, rows, me, *refs):
    near, outs = refs[:4], refs[4 : 4 + peers]
    padded, summed, top, theta, phi, angles, sems = refs[4 + peers :]
    held = top.shape[0] // 4
    for copy in fetch(list(zip(near, (top, theta, phi, angles), strict=True)), sems):
        copy.wait()
    narrowed = lax.dot_general(top[...], phi[...], NT, preferred_element_type=F32)
    padded[...] = jnp.zeros(padded.shape, F32)
    for k in range(4):
        padded[k, me[0]] = narrowed[k * held : (k + 1) * held]
    for k in range(4):
        full = padded[k].reshape(peers * held, narrowed.shape[1])
        part = split_dot(theta[...], full, (((1,), (0,)), ((), ())))
        summed[k] = part.reshape(peers, rows, narrowed.shape[1])
    low = angles.shape[1]
    half = angles.shape[0] // 2
    for mask, out in enumerate(outs):
        for k in range(4):
            out[k * rows : (k + 1) * rows] = summed[k, jnp.bitwise_xor(me[0], mask)]
        for c in range(half):
            start = 4 * rows + c * low
            out[start : start + low, 0:128] = angles[c]
            out[start : start + low, 128:256] = angles[half + c]


def shift_body(peers, rows, low, me, *refs):
    parts, near = refs[:peers], refs[peers : peers + 3]
    shifted, trig, expand, mix, angles, theta, phi, sems = refs[peers + 3 :]
    for copy in fetch(list(zip(near, (angles, theta, phi), strict=True)), sems):
        copy.wait()
    orders = theta.shape[0]
    line = lax.broadcasted_iota(jnp.int32, (2 * orders, orders), 0)
    column = lax.broadcasted_iota(jnp.int32, (2 * orders, orders), 1)
    for c in range(2):
        pick = (line == 2 * column + c).astype(F32).astype(BF16)
        spread = jnp.dot(pick, theta[...], preferred_element_type=F32)
        expand[c] = spread.astype(BF16)
    size = phi.shape[1]
    mix[0:size, 0:size] = phi[0]
    mix[0:size, size:] = -phi[1]
    mix[size:, 0:size] = phi[1]
    mix[size:, size:] = phi[0]
    children = angles.shape[0]
    half = children // 2
    for c in range(children):
        cosine, sine = jnp.cos(angles[c]), jnp.sin(angles[c])
        for b in range(2):
            re = parts[0][2 * b * rows : (2 * b + 1) * rows]
            im = parts[0][(2 * b + 1) * rows : (2 * b + 2) * rows]
            for part in parts[1:]:
                re = re + part[2 * b * rows : (2 * b + 1) * rows]
                im = im + part[(2 * b + 1) * rows : (2 * b + 2) * rows]
            shifted[b * children + c, 0] = re * cosine - im * sine
            shifted[b * children + c, 1] = re * sine + im * cosine
    for mask, part in enumerate(parts):
        for c in range(half):
            start = 4 * rows + c * low
            for side in range(2):
                angle = part[start : start + low, side * 128 : side * 128 + 128]
                place = jnp.bitwise_xor(me[0], mask)
                trig[0, side * half + c, place] = jnp.cos(angle)
                trig[1, side * half + c, place] = jnp.sin(angle)


def join(owns, got, extra=None):
    shapes = [struct(a.shape, BF16) for a in owns]
    if extra is not None:
        shapes[0] = struct((owns[0].shape[0] + extra.shape[0], *extra.shape[1:]), BF16)

    def body(*refs):
        first = 0
        count = len(owns)
        outs = refs[-count:]
        for own, out in zip(refs[:count], outs, strict=True):
            size = own.shape[0]
            out[0:size] = (own[...] + refs[count][first : first + size].astype(F32)).astype(BF16)
            first += size
        if extra is not None:
            outs[0][owns[0].shape[0] :] = refs[count + 1][...]

    more = [] if extra is None else [extra]
    return kernel_call(body, shapes, [], [*owns, got, *more], "join")


def upper_body(masks, peers, entries, me, home, ids, offsets, own, far, table, shifted, phi, *refs):
    outs, pool = refs[: len(masks)], refs[-1]
    boxes, _, rows, _ = own.shape
    pool[0:boxes] = own[...].astype(F32)
    pool[boxes:] = far[...].astype(F32)
    spans = [slice(r, r + 8) for r in range(0, rows, 8)]
    per = boxes // peers
    for mask, out in zip(masks, outs, strict=True):
        first = jnp.bitwise_xor(me[0], mask) * per

        def one(i, carry, first=first, out=out):
            box = first + i
            real = [shifted[box, 0, span] for span in spans]
            imag = [shifted[box, 1, span] for span in spans]
            for entry in range(entries):
                offset, ident = offsets[box, entry], ids[box, entry]
                place = lax.rem(ident, boxes)
                place = jnp.where(ident - place == home[0] * boxes, place, place + boxes)
                for k, span in enumerate(spans):
                    fr, fi = table[offset, 0, span].astype(F32), table[offset, 1, span].astype(F32)
                    sr, si = pool[place, 0, span], pool[place, 1, span]
                    real[k] = real[k] + (fr * sr - fi * si)
                    imag[k] = imag[k] + (fr * si + fi * sr)
            incoming = jnp.concatenate([*real, *imag], axis=0).astype(BF16)
            narrow = lax.dot_general(incoming, phi[...], NT, preferred_element_type=F32)
            out[i] = narrow.astype(BF16)
            return carry

        lax.fori_loop(0, per, one, 0)


def place_body(*refs):
    count = len(refs) // 2
    for low, out in zip(refs[:count], refs[count:], strict=True):
        out[...] = low[...].astype(F32)


def final_body(peers, parents, me, *refs):
    ups, lows = list(refs[: peers - 1]), refs[peers - 1 : 2 * peers - 1]
    ups.insert(1, None)
    trig, theta, mix, expand, out, rows_up, rows_low, pattern, ready, sems = refs[2 * peers - 1 :]
    children, rows = trig.shape[1], trig.shape[2]
    high_rows, low_rows = rows_up.shape[3], rows_low.shape[3]
    both = jnp.concatenate([expand[0], expand[1]], axis=1)
    size = both.shape[0]
    block_rows = children * size
    copies = []
    for mask in range(peers):
        place = jnp.bitwise_xor(me[0], mask)
        for c in range(2):
            for b in range(parents):
                if mask == 1:
                    piece = lows[1][parents * children + 2 * b + c]
                else:
                    piece = ups[mask][b, c * high_rows : (c + 1) * high_rows]
                rows_up[b, c, place] = piece.astype(F32)
            piece = lows[mask][0 : parents * children, c * low_rows : (c + 1) * low_rows]
            rows_low[:, c, place] = piece.astype(F32)
    for b in range(parents):
        coarse = []
        for c in range(2):
            full = rows_up[b, c].reshape(peers * high_rows, 128).astype(BF16)
            coarse.append(jnp.dot(theta[...], full, preferred_element_type=F32))
        for k in range(children):
            cosine, sine = trig[0, k], trig[1, k]
            box = b * children + k
            real = coarse[0] * cosine - coarse[1] * sine + rows_low[box, 0].reshape(rows, 128)
            imag = coarse[0] * sine + coarse[1] * cosine + rows_low[box, 1].reshape(rows, 128)
            pattern[k * rows : (k + 1) * rows, 0:128] = real.astype(BF16)
            pattern[k * rows : (k + 1) * rows, 128:256] = imag.astype(BF16)
        for k in range(0, children, 2):
            block = pattern[k * rows : (k + 2) * rows]
            turned = lax.dot_general(block, mix[...], NT, preferred_element_type=F32)
            one, two = turned[:rows], turned[rows:]
            stacked = jnp.concatenate(
                [
                    jnp.concatenate([one[:, :128], two[:, :128]], axis=1),
                    jnp.concatenate([one[:, 128:], two[:, 128:]], axis=1),
                ],
                axis=0,
            )
            result = split_dot(both, stacked, (((1,), (0,)), ((), ())))
            start = b * block_rows + k * size
            ready[start : start + size] = result[:, :128]
            ready[start + size : start + 2 * size] = result[:, 128:]
        span = pl.ds(b * block_rows, block_rows)
        copies += fetch([(ready.at[span], out.at[span])], sems.at[pl.ds(b, 1)])
    for copy in copies:
        copy.wait()


def struct(shape, dtype):
    return jax.ShapeDtypeStruct(shape, dtype)


def per_device(
    top_patterns,
    theta_upper,
    phi_upper,
    angles_upper,
    table_upper,
    outgoing_upper,
    list_upper,
    offset_upper,
    theta_lower,
    phi_lower,
    angles_lower,
    table_lower,
    outgoing_lower,
    list_lower,
    offset_lower,
    switch_theta,
    switch_phi,
):
    peers = lax.axis_size("angle")
    home = lax.axis_index("box")
    me = lax.axis_index("angle").astype(jnp.int32).reshape(1)
    far_mask = lax.axis_size("box") // 2
    boxes, _, low, lanes = outgoing_lower.shape
    per = boxes // peers
    entries = list_lower.shape[1]
    upper_boxes, _, rows, wide = outgoing_upper.shape
    upper_per = upper_boxes // peers

    other = list_lower.T // boxes != home
    spot = list_lower.T % boxes
    ask_code = (jnp.where(other, spot, boxes) << SHIFT) + offset_lower.T
    own_code = (jnp.where(other, boxes, spot) << SHIFT) + offset_lower.T
    far_code = swap(ask_code, "box", 1)
    far_upper = swap(outgoing_upper, "box", far_mask)

    places = table_lower.shape[0]
    outer, inner = list(range(peers - 1, peers // 2 - 1, -1)), list(range(peers // 2 - 1, -1, -1))

    def sums(groups, outs, codes, order, name):
        return kernel_call(
            functools.partial(sums_body, groups, per, entries),
            outs,
            [order, *codes],
            [table, source],
            name,
        )

    own_shape = struct((per, 2 * low, lanes), F32)
    far_shape = struct((len(outer) * per, 2 * low, lanes), BF16)
    first, table, source = kernel_call(
        functools.partial(first_body, [(tuple(outer), 0)], per, entries),
        [
            far_shape,
            struct((places, 2 * low, lanes), F32),
            struct((boxes + 1, 2 * low, lanes), F32),
        ],
        [me, far_code],
        [table_lower.reshape(-1, 2 * low, lanes), outgoing_lower.reshape(-1, 2 * low, lanes)],
        "sums_first",
        scratch=[
            pltpu.VMEM((places, 2 * low, lanes), BF16),
            pltpu.VMEM((boxes, 2 * low, lanes), BF16),
            pltpu.VMEM((places, 2 * low, lanes), F32),
            pltpu.VMEM((boxes + 1, 2 * low, lanes), F32),
            pltpu.SemaphoreType.DMA((5,)),
            pltpu.SemaphoreType.DMA((2,)),
        ],
        held=2,
        away=2,
        vmem=53 << 20,
    )
    got_outer = swap(first, "box", 1)

    children = angles_lower.shape[0]
    part_rows = 4 * rows + children * low // 2
    held = top_patterns.shape[2]
    top = top_patterns.reshape(4 * held, -1)
    parts = kernel_call(
        functools.partial(early_body, peers, rows),
        [struct((part_rows, wide), F32)] * peers,
        [after(me, first)],
        [top, theta_upper, phi_upper, angles_lower],
        "early",
        scratch=[
            pltpu.VMEM((4, peers, held, wide), F32),
            pltpu.VMEM((4, peers, rows, wide), F32),
            *(pltpu.VMEM(a.shape, a.dtype) for a in (top, theta_upper, phi_upper, angles_lower)),
            pltpu.SemaphoreType.DMA((4,)),
        ],
        held=4,
    )
    order = after(me, parts[0])
    parts = [swap(part, "angle", mask) if mask else part for mask, part in enumerate(parts)]
    (second,) = sums([(tuple(inner), 0)], [far_shape], [far_code], order, "sums_second")
    got_inner = swap(after(second, parts[1]), "box", 1)
    own_outer = sums(
        [((mask,), 0) for mask in outer],
        [own_shape] * len(outer),
        [own_code],
        after(me, second),
        "sums_third",
    )
    lows = dict(zip(outer, join(own_outer, got_outer), strict=True))
    orders, angles = switch_theta.shape
    azimuths = switch_phi.shape[1]
    shifted, trig, expand, mix = kernel_call(
        functools.partial(shift_body, peers, rows, low),
        [
            struct((upper_boxes, 2, rows, wide), F32),
            struct((2, children, peers, low, lanes), F32),
            struct((2, 2 * orders, angles), BF16),
            struct((2 * azimuths, 2 * azimuths), BF16),
        ],
        [after(me, lows[outer[0]])],
        [*parts, angles_upper, switch_theta, switch_phi],
        "shift",
        scratch=[
            *(pltpu.VMEM(a.shape, a.dtype) for a in (angles_upper, switch_theta, switch_phi)),
            pltpu.SemaphoreType.DMA((3,)),
        ],
        held=3,
    )
    trig = trig.reshape(2, children, peers * low, lanes)
    def upper(masks, order, name):
        return kernel_call(
            functools.partial(upper_body, masks, peers, entries),
            [struct((upper_per, 2 * rows, lanes), BF16)] * len(masks),
            [order, home.astype(jnp.int32).reshape(1), list_upper, offset_upper],
            [outgoing_upper, far_upper, table_upper, shifted, phi_lower],
            name,
            scratch=[pltpu.VMEM((2 * upper_boxes, 2, rows, wide), F32)],
        )

    ups = dict(zip(outer, upper(outer, me, "upper_far"), strict=True))
    own_inner = sums(
        [((mask,), 0) for mask in inner],
        [own_shape] * len(inner),
        [own_code],
        after(me, ups[outer[0]]),
        "sums_fourth",
    )
    ups.update(zip(inner, upper(inner, after(me, own_inner[0]), "upper_near"), strict=True))
    near = ups[1].reshape(-1, 2 * low, lanes)
    lows.update(zip(inner, join(own_inner, got_inner, near), strict=True))
    ups = [swap(ups[mask], "angle", mask) if mask else ups[0] for mask in range(peers) if mask != 1]
    lows = [swap(lows[mask], "angle", mask) if mask else lows[mask] for mask in range(peers)]

    arrived = kernel_call(
        place_body,
        [struct(lows[mask].shape, F32) for mask in outer],
        [],
        [lows[mask] for mask in outer],
        "place",
    )
    lows = [*lows[: len(inner)], *reversed(arrived)]
    (out,) = kernel_call(
        functools.partial(final_body, peers, upper_per),
        [struct((per * 2 * orders, azimuths), F32)],
        [me],
        [*ups, *lows, trig, theta_lower, mix, expand],
        "expand",
        scratch=[
            pltpu.VMEM((upper_per, 2, peers, rows, lanes), F32),
            pltpu.VMEM((per, 2, peers, low, lanes), F32),
            pltpu.VMEM((children * peers * low, 2 * lanes), BF16),
            pltpu.VMEM((per * 2 * orders, azimuths), F32),
            pltpu.SemaphoreType.DMA((upper_per,)),
        ],
        away=1,
        vmem=12 << 20,
    )
    out = out.reshape(per, orders, 2, azimuths)
    return jnp.transpose(out, (0, 2, 1, 3)).reshape(per, 2, orders * azimuths)


def solution(mesh):
    return jax.shard_map(
        per_device,
        mesh=mesh,
        in_specs=(
            P("box", None, "angle", None),
            P(),
            P(),
            P(None, "angle", None),
            P(None, None, "angle", None),
            P("box", None, "angle", None),
            P("box", None),
            P("box", None),
            P(),
            P(),
            P(None, "angle", None),
            P(None, None, "angle", None),
            P("box", None, "angle", None),
            P("box", None),
            P("box", None),
            P(),
            P(),
        ),
        out_specs=P(("box", "angle"), None, None),
        check_vma=False,
    )
```

```python
import functools

import jax
import jax.numpy as jnp
from jax import lax
from jax.experimental import pallas as pl
from jax.experimental.pallas import tpu as pltpu
from jax.sharding import PartitionSpec as P

F32, BF16 = jnp.float32, jnp.bfloat16
VM = pl.BlockSpec(memory_space=pltpu.VMEM)
SM = pl.BlockSpec(memory_space=pltpu.SMEM)
HB = pl.BlockSpec(memory_space=pltpu.HBM)
SHIFT = 9
NT = (((1,), (1,)), ((), ()))


def swap(value, axis, mask):
    pairs = [(source, source ^ mask) for source in range(lax.axis_size(axis))]
    return lax.ppermute(value, axis, pairs)


COSTS = {"join": 0, "sums_third": 0, "shift": 0, "close_peers": 0, "close_self": 0}


def after(value, *others):
    return lax.optimization_barrier((value, *others))[0]


def kernel_call(body, outs, scalars, arrays, name, scratch=(), held=0, vmem=6 << 20, away=0):
    near = len(arrays) - held
    return pl.pallas_call(
        body,
        out_shape=outs,
        in_specs=[SM] * len(scalars) + [VM] * near + [HB] * held,
        out_specs=[VM] * (len(outs) - away) + [HB] * away,
        scratch_shapes=list(scratch),
        compiler_params=pltpu.CompilerParams(vmem_limit_bytes=vmem),
        cost_estimate=pl.CostEstimate(flops=COSTS.get(name, 4) << 30, bytes_accessed=1, transcendentals=0),
        name=name,
    )(*scalars, *arrays)


def fetch(pairs, sems):
    copies = [pltpu.make_async_copy(a, b, sems.at[k]) for k, (a, b) in enumerate(pairs)]
    for copy in copies:
        copy.start()
    return copies


def split_dot(left, value, dims):
    high = value.astype(BF16)
    low = (value - high.astype(F32)).astype(BF16)
    return lax.dot_general(left, high, dims, preferred_element_type=F32) + lax.dot_general(
        left, low, dims, preferred_element_type=F32
    )


def box_sum(box, entries, code, table, source):
    rows = table.shape[1] // 2
    real = imag = None
    for entry in range(entries):
        word = code[entry, box]
        factor = table[word & ((1 << SHIFT) - 1)]
        value = source[word >> SHIFT]
        fr, fi, sr, si = factor[:rows], factor[rows:], value[:rows], value[rows:]
        re, im = fr * sr - fi * si, fr * si + fi * sr
        real = re if real is None else real + re
        imag = im if imag is None else imag + im
    return real, imag


def sums_body(groups, per, entries, me, *refs):
    codes = max(which for _, which in groups) + 1
    code_refs, (table, source), outs = refs[:codes], refs[codes : codes + 2], refs[codes + 2 :]
    rows = table.shape[1] // 2
    for (masks, which), out in zip(groups, outs, strict=True):
        for place, mask in enumerate(masks):
            first = jnp.bitwise_xor(me[0], mask) * per

            def one(i, carry, first=first, place=place, which=which, out=out):
                real, imag = box_sum(first + i, entries, code_refs[which], table, source)
                out[place * per + i, 0:rows] = real.astype(out.dtype)
                out[place * per + i, rows:] = imag.astype(out.dtype)
                return carry

            lax.fori_loop(0, per, one, 0, unroll=2)


def first_body(groups, per, entries, me, code, table, source, out, *refs):
    table_out, source_out, table_in, source_in, wide_table, wide_source, sems, back = refs
    count, total = source.shape[0], table.shape[0]
    step = -(-total // 4)
    spans = [(k, min(k + step, total)) for k in range(0, total, step)]
    pairs = [(source, source_in)]
    pairs += [(table.at[lo:hi], table_in.at[lo:hi]) for lo, hi in spans]
    copies = fetch(pairs, sems)
    copies[0].wait()
    wide_source[0:count] = source_in[...].astype(F32)
    wide_source[count] = jnp.zeros(source.shape[1:], F32)
    for copy, (lo, hi) in zip(copies[1:], spans, strict=True):
        copy.wait()
        wide_table[lo:hi] = table_in[lo:hi].astype(F32)
    copies = fetch([(wide_table, table_out), (wide_source, source_out)], back)
    sums_body(groups, per, entries, me, code, wide_table, wide_source, out)
    for copy in copies:
        copy.wait()


def early_body(peers, rows, me, *refs):
    near, outs = refs[:4], refs[4 : 4 + peers]
    padded, summed, top, theta, phi, angles, sems = refs[4 + peers :]
    held = top.shape[0] // 4
    for copy in fetch(list(zip(near, (top, theta, phi, angles), strict=True)), sems):
        copy.wait()
    narrowed = lax.dot_general(top[...], phi[...], NT, preferred_element_type=F32)
    padded[...] = jnp.zeros(padded.shape, F32)
    for k in range(4):
        padded[k, me[0]] = narrowed[k * held : (k + 1) * held]
    for k in range(4):
        full = padded[k].reshape(peers * held, narrowed.shape[1])
        part = split_dot(theta[...], full, (((1,), (0,)), ((), ())))
        summed[k] = part.reshape(peers, rows, narrowed.shape[1])
    low = angles.shape[1]
    half = angles.shape[0] // 2
    for mask, out in enumerate(outs):
        for k in range(4):
            out[k * rows : (k + 1) * rows] = summed[k, jnp.bitwise_xor(me[0], mask)]
        for c in range(half):
            start = 4 * rows + c * low
            out[start : start + low, 0:128] = angles[c]
            out[start : start + low, 128:256] = angles[half + c]


def shift_body(peers, rows, low, me, *refs):
    parts, near = refs[:peers], refs[peers : peers + 2]
    shifted, trig, mix, angles, phi, sems = refs[peers + 2 :]
    for copy in fetch(list(zip(near, (angles, phi), strict=True)), sems):
        copy.wait()
    size = phi.shape[1]
    mix[0:size, 0:size] = phi[0]
    mix[0:size, size:] = -phi[1]
    mix[size:, 0:size] = phi[1]
    mix[size:, size:] = phi[0]
    children = angles.shape[0]
    half = children // 2
    for c in range(children):
        cosine, sine = jnp.cos(angles[c]), jnp.sin(angles[c])
        for b in range(2):
            re = parts[0][2 * b * rows : (2 * b + 1) * rows]
            im = parts[0][(2 * b + 1) * rows : (2 * b + 2) * rows]
            for part in parts[1:]:
                re = re + part[2 * b * rows : (2 * b + 1) * rows]
                im = im + part[(2 * b + 1) * rows : (2 * b + 2) * rows]
            shifted[b * children + c, 0] = re * cosine - im * sine
            shifted[b * children + c, 1] = re * sine + im * cosine
    for mask, part in enumerate(parts):
        for c in range(half):
            start = 4 * rows + c * low
            for side in range(2):
                angle = part[start : start + low, side * 128 : side * 128 + 128]
                place = jnp.bitwise_xor(me[0], mask)
                trig[0, side * half + c, place] = jnp.cos(angle)
                trig[1, side * half + c, place] = jnp.sin(angle)


def join(owns, got):
    def body(*refs):
        first = 0
        count = len(owns)
        for own, out in zip(refs[:count], refs[count + 1 :], strict=True):
            size = own.shape[0]
            out[...] = (own[...] + refs[count][first : first + size].astype(F32)).astype(BF16)
            first += size

    return kernel_call(body, [struct(a.shape, BF16) for a in owns], [], [*owns, got], "join")


def close_body(masks, firsts, per, entries, me, code, table, source, got, *refs):
    count = len(masks)
    rows = table.shape[1] // 2
    for mask, begin, piece, out in zip(masks, firsts, refs[:count], refs[count:], strict=True):
        first = jnp.bitwise_xor(me[0], mask) * per

        def one(i, carry, first=first, begin=begin, out=out):
            real, imag = box_sum(first + i, entries, code, table, source)
            real = real + got[begin + i, 0:rows].astype(F32)
            imag = imag + got[begin + i, rows:].astype(F32)
            out[i, 0:rows] = real.astype(BF16)
            out[i, rows:] = imag.astype(BF16)
            return carry

        lax.fori_loop(0, per, one, 0, unroll=2)
        out[per:] = piece[...]


def upper_body(masks, peers, entries, me, home, ids, offsets, own, far, table, shifted, phi, *refs):
    outs, pool = refs[: len(masks)], refs[-1]
    boxes, _, rows, _ = own.shape
    pool[0:boxes] = own[...].astype(F32)
    pool[boxes:] = far[...].astype(F32)
    spans = [slice(r, r + 8) for r in range(0, rows, 8)]
    per = boxes // peers
    for mask, out in zip(masks, outs, strict=True):
        first = jnp.bitwise_xor(me[0], mask) * per

        def one(i, carry, first=first, out=out):
            box = first + i
            real = [shifted[box, 0, span] for span in spans]
            imag = [shifted[box, 1, span] for span in spans]
            for entry in range(entries):
                offset, ident = offsets[box, entry], ids[box, entry]
                place = lax.rem(ident, boxes)
                place = jnp.where(ident - place == home[0] * boxes, place, place + boxes)
                for k, span in enumerate(spans):
                    fr, fi = table[offset, 0, span].astype(F32), table[offset, 1, span].astype(F32)
                    sr, si = pool[place, 0, span], pool[place, 1, span]
                    real[k] = real[k] + (fr * sr - fi * si)
                    imag[k] = imag[k] + (fr * si + fi * sr)
            incoming = jnp.concatenate([*real, *imag], axis=0).astype(BF16)
            narrow = lax.dot_general(incoming, phi[...], NT, preferred_element_type=F32)
            out[i] = narrow.astype(BF16)
            return carry

        lax.fori_loop(0, per, one, 0)


def place_body(*refs):
    count = len(refs) // 2
    for low, out in zip(refs[:count], refs[count:], strict=True):
        out[...] = low[...].astype(F32)


def final_body(peers, parents, me, *refs):
    near = peers // 2
    ups, lows = refs[:near], refs[near : near + peers]
    trig, theta, mix, expand, out, rows_up, rows_low, turned, ready, sems = refs[near + peers :]
    children, rows = trig.shape[1], trig.shape[2]
    high_rows, low_rows = rows_up.shape[3], rows_low.shape[3]
    orders = expand.shape[0]
    boxes = parents * children
    for mask in range(peers):
        place = jnp.bitwise_xor(me[0], mask)
        for c in range(2):
            for b in range(parents):
                if mask < near:
                    piece = lows[mask][boxes + 2 * b + c]
                else:
                    piece = ups[mask - near][b, c * high_rows : (c + 1) * high_rows]
                rows_up[b, c, place] = piece.astype(F32)
            piece = lows[mask][0:boxes, c * low_rows : (c + 1) * low_rows]
            rows_low[:, c, place] = piece.astype(F32)
    copies = []
    for b in range(parents):
        coarse = []
        for c in range(2):
            full = rows_up[b, c].reshape(peers * high_rows, 128).astype(BF16)
            coarse.append(jnp.dot(theta[...], full, preferred_element_type=F32))
        for k in range(children):
            cosine, sine = trig[0, k], trig[1, k]
            box = b * children + k
            real = coarse[0] * cosine - coarse[1] * sine + rows_low[box, 0].reshape(rows, 128)
            imag = coarse[0] * sine + coarse[1] * cosine + rows_low[box, 1].reshape(rows, 128)
            pattern = jnp.concatenate([real.astype(BF16), imag.astype(BF16)], axis=1)
            half = jnp.dot(expand[...], pattern, preferred_element_type=F32)
            high = half.astype(BF16)
            turned[k * orders : (k + 1) * orders] = high
            low = (half - high.astype(F32)).astype(BF16)
            turned[(children + k) * orders : (children + k + 1) * orders] = low
        both = lax.dot_general(turned[...], mix[...], NT, preferred_element_type=F32)
        size = children * orders
        result = both[:size] + both[size:]
        start = b * 2 * size
        ready[pl.ds(start, size, stride=2)] = result[:, :128]
        ready[pl.ds(start + 1, size, stride=2)] = result[:, 128:]
        span = pl.ds(start, 2 * size)
        copies += fetch([(ready.at[span], out.at[span])], sems.at[pl.ds(b, 1)])
    for copy in copies:
        copy.wait()


def struct(shape, dtype):
    return jax.ShapeDtypeStruct(shape, dtype)


def per_device(
    top_patterns,
    theta_upper,
    phi_upper,
    angles_upper,
    table_upper,
    outgoing_upper,
    list_upper,
    offset_upper,
    theta_lower,
    phi_lower,
    angles_lower,
    table_lower,
    outgoing_lower,
    list_lower,
    offset_lower,
    switch_theta,
    switch_phi,
):
    peers = lax.axis_size("angle")
    home = lax.axis_index("box")
    me = lax.axis_index("angle").astype(jnp.int32).reshape(1)
    far_mask = lax.axis_size("box") // 2
    boxes, _, low, lanes = outgoing_lower.shape
    per = boxes // peers
    entries = list_lower.shape[1]
    upper_boxes, _, rows, wide = outgoing_upper.shape
    upper_per = upper_boxes // peers

    other = list_lower.T // boxes != home
    spot = list_lower.T % boxes
    ask_code = (jnp.where(other, spot, boxes) << SHIFT) + offset_lower.T
    own_code = (jnp.where(other, boxes, spot) << SHIFT) + offset_lower.T
    far_code = swap(ask_code, "box", 1)
    far_upper = swap(outgoing_upper, "box", far_mask)

    places = table_lower.shape[0]
    outer, inner = list(range(peers - 1, peers // 2 - 1, -1)), list(range(peers // 2 - 1, -1, -1))

    def sums(groups, outs, codes, order, name):
        return kernel_call(
            functools.partial(sums_body, groups, per, entries),
            outs,
            [order, *codes],
            [table, source],
            name,
        )

    own_shape = struct((per, 2 * low, lanes), F32)
    far_shape = struct((len(outer) * per, 2 * low, lanes), BF16)
    first, table, source = kernel_call(
        functools.partial(first_body, [(tuple(outer), 0)], per, entries),
        [
            far_shape,
            struct((places, 2 * low, lanes), F32),
            struct((boxes + 1, 2 * low, lanes), F32),
        ],
        [me, far_code],
        [table_lower.reshape(-1, 2 * low, lanes), outgoing_lower.reshape(-1, 2 * low, lanes)],
        "sums_first",
        scratch=[
            pltpu.VMEM((places, 2 * low, lanes), BF16),
            pltpu.VMEM((boxes, 2 * low, lanes), BF16),
            pltpu.VMEM((places, 2 * low, lanes), F32),
            pltpu.VMEM((boxes + 1, 2 * low, lanes), F32),
            pltpu.SemaphoreType.DMA((5,)),
            pltpu.SemaphoreType.DMA((2,)),
        ],
        held=2,
        away=2,
        vmem=53 << 20,
    )
    got_outer = swap(first, "box", 1)

    children = angles_lower.shape[0]
    part_rows = 4 * rows + children * low // 2
    held = top_patterns.shape[2]
    top = top_patterns.reshape(4 * held, -1)
    parts = kernel_call(
        functools.partial(early_body, peers, rows),
        [struct((part_rows, wide), F32)] * peers,
        [after(me, first)],
        [top, theta_upper, phi_upper, angles_lower],
        "early",
        scratch=[
            pltpu.VMEM((4, peers, held, wide), F32),
            pltpu.VMEM((4, peers, rows, wide), F32),
            *(pltpu.VMEM(a.shape, a.dtype) for a in (top, theta_upper, phi_upper, angles_lower)),
            pltpu.SemaphoreType.DMA((4,)),
        ],
        held=4,
    )
    order = after(me, parts[0])
    parts = [swap(part, "angle", mask) if mask else part for mask, part in enumerate(parts)]
    (second,) = sums([(tuple(inner), 0)], [far_shape], [far_code], order, "sums_second")
    got_inner = swap(after(second, parts[1]), "box", 1)
    own_outer = sums(
        [((mask,), 0) for mask in outer],
        [own_shape] * len(outer),
        [own_code],
        after(me, second),
        "sums_third",
    )
    lows = dict(zip(outer, join(own_outer, got_outer), strict=True))
    orders = switch_theta.shape[0]
    azimuths = switch_phi.shape[1]
    shifted, trig, mix = kernel_call(
        functools.partial(shift_body, peers, rows, low),
        [
            struct((upper_boxes, 2, rows, wide), F32),
            struct((2, children, peers, low, lanes), F32),
            struct((2 * azimuths, 2 * azimuths), BF16),
        ],
        [after(me, lows[outer[0]])],
        [*parts, angles_upper, switch_phi],
        "shift",
        scratch=[
            *(pltpu.VMEM(a.shape, a.dtype) for a in (angles_upper, switch_phi)),
            pltpu.SemaphoreType.DMA((2,)),
        ],
        held=2,
    )
    trig = trig.reshape(2, children, peers * low, lanes)
    ups = kernel_call(
        functools.partial(upper_body, outer + inner, peers, entries),
        [struct((upper_per, 2 * rows, lanes), BF16)] * peers,
        [me, home.astype(jnp.int32).reshape(1), list_upper, offset_upper],
        [outgoing_upper, far_upper, table_upper, shifted, phi_lower],
        "upper",
        scratch=[pltpu.VMEM((2 * upper_boxes, 2, rows, wide), F32)],
    )
    ups = dict(zip(outer + inner, ups, strict=True))
    order = after(me, ups[0])
    behind = {mask: ups.pop(mask).reshape(-1, 2 * low, lanes) for mask in inner}
    for masks, name in ((inner[:-1], "close_peers"), (inner[-1:], "close_self")):
        close = kernel_call(
            functools.partial(close_body, masks, [per * inner.index(m) for m in masks], per, entries),
            [struct((per + behind[0].shape[0], 2 * low, lanes), BF16)] * len(masks),
            [order, own_code],
            [table, source, got_inner, *(behind[mask] for mask in masks)],
            name,
        )
        lows.update(zip(masks, close, strict=True))
        order = after(me, close[0])
    ups = [swap(ups[mask], "angle", mask) for mask in reversed(outer)]
    lows = [swap(lows[mask], "angle", mask) if mask else lows[mask] for mask in range(peers)]

    arrived = kernel_call(
        place_body,
        [struct(lows[mask].shape, F32) for mask in outer],
        [],
        [lows[mask] for mask in outer],
        "place",
    )
    lows = [*lows[: len(inner)], *reversed(arrived)]
    (out,) = kernel_call(
        functools.partial(final_body, peers, upper_per),
        [struct((per * 2 * orders, azimuths), F32)],
        [me],
        [*ups, *lows, trig, theta_lower, mix, switch_theta],
        "expand",
        scratch=[
            pltpu.VMEM((upper_per, 2, peers, rows, lanes), F32),
            pltpu.VMEM((per, 2, peers, low, lanes), F32),
            pltpu.VMEM((2 * children * orders, 2 * lanes), BF16),
            pltpu.VMEM((per * 2 * orders + 8, azimuths), F32),
            pltpu.SemaphoreType.DMA((upper_per,)),
        ],
        away=1,
        vmem=12 << 20,
    )
    out = out.reshape(per, orders, 2, azimuths)
    return jnp.transpose(out, (0, 2, 1, 3)).reshape(per, 2, orders * azimuths)


def solution(mesh):
    return jax.shard_map(
        per_device,
        mesh=mesh,
        in_specs=(
            P("box", None, "angle", None),
            P(),
            P(),
            P(None, "angle", None),
            P(None, None, "angle", None),
            P("box", None, "angle", None),
            P("box", None),
            P("box", None),
            P(),
            P(),
            P(None, "angle", None),
            P(None, None, "angle", None),
            P("box", None, "angle", None),
            P("box", None),
            P("box", None),
            P(),
            P(),
        ),
        out_specs=P(("box", "angle"), None, None),
        check_vma=False,
    )
```

```python
import functools

import jax
import jax.numpy as jnp
from jax import lax
from jax.experimental import pallas as pl
from jax.experimental.pallas import tpu as pltpu
from jax.sharding import PartitionSpec as P

F32, BF16 = jnp.float32, jnp.bfloat16
VM = pl.BlockSpec(memory_space=pltpu.VMEM)
SM = pl.BlockSpec(memory_space=pltpu.SMEM)
HB = pl.BlockSpec(memory_space=pltpu.HBM)
SHIFT = 9
NT = (((1,), (1,)), ((), ()))


def swap(value, axis, mask):
    pairs = [(source, source ^ mask) for source in range(lax.axis_size(axis))]
    return lax.ppermute(value, axis, pairs)


COSTS = {"join": 0, "sums_third": 0, "shift": 0, "close_peers": 0, "close_self": 0}


def after(value, *others):
    return lax.optimization_barrier((value, *others))[0]


def kernel_call(body, outs, scalars, arrays, name, scratch=(), held=0, vmem=6 << 20, away=0):
    near = len(arrays) - held
    return pl.pallas_call(
        body,
        out_shape=outs,
        in_specs=[SM] * len(scalars) + [VM] * near + [HB] * held,
        out_specs=[VM] * (len(outs) - away) + [HB] * away,
        scratch_shapes=list(scratch),
        compiler_params=pltpu.CompilerParams(vmem_limit_bytes=vmem),
        cost_estimate=pl.CostEstimate(flops=COSTS.get(name, 4) << 30, bytes_accessed=1, transcendentals=0),
        name=name,
    )(*scalars, *arrays)


def fetch(pairs, sems):
    copies = [pltpu.make_async_copy(a, b, sems.at[k]) for k, (a, b) in enumerate(pairs)]
    for copy in copies:
        copy.start()
    return copies


def split_dot(left, value, dims):
    high = value.astype(BF16)
    low = (value - high.astype(F32)).astype(BF16)
    return lax.dot_general(left, high, dims, preferred_element_type=F32) + lax.dot_general(
        left, low, dims, preferred_element_type=F32
    )


def box_sum(box, entries, code, table, source):
    rows = table.shape[1] // 2
    real = imag = None
    for entry in range(entries):
        word = code[entry, box]
        factor = table[word & ((1 << SHIFT) - 1)]
        value = source[word >> SHIFT]
        fr, fi, sr, si = factor[:rows], factor[rows:], value[:rows], value[rows:]
        re, im = fr * sr - fi * si, fr * si + fi * sr
        real = re if real is None else real + re
        imag = im if imag is None else imag + im
    return real, imag


def sums_body(groups, per, entries, me, *refs):
    codes = max(which for _, which in groups) + 1
    code_refs, (table, source), outs = refs[:codes], refs[codes : codes + 2], refs[codes + 2 :]
    rows = table.shape[1] // 2
    for (masks, which), out in zip(groups, outs, strict=True):
        for place, mask in enumerate(masks):
            first = jnp.bitwise_xor(me[0], mask) * per

            def one(i, carry, first=first, place=place, which=which, out=out):
                real, imag = box_sum(first + i, entries, code_refs[which], table, source)
                out[place * per + i, 0:rows] = real.astype(out.dtype)
                out[place * per + i, rows:] = imag.astype(out.dtype)
                return carry

            lax.fori_loop(0, per, one, 0, unroll=2)


def first_body(groups, per, entries, me, code, table, source, *refs):
    outs = refs[: len(groups)]
    table_out, source_out, table_in, source_in, wide_table, wide_source, sems, back = refs[len(groups) :]
    count, total = source.shape[0], table.shape[0]
    step = -(-total // 4)
    spans = [(k, min(k + step, total)) for k in range(0, total, step)]
    pairs = [(source, source_in)]
    pairs += [(table.at[lo:hi], table_in.at[lo:hi]) for lo, hi in spans]
    copies = fetch(pairs, sems)
    copies[0].wait()
    wide_source[0:count] = source_in[...].astype(F32)
    wide_source[count] = jnp.zeros(source.shape[1:], F32)
    for copy, (lo, hi) in zip(copies[1:], spans, strict=True):
        copy.wait()
        wide_table[lo:hi] = table_in[lo:hi].astype(F32)
    copies = fetch([(wide_table, table_out), (wide_source, source_out)], back)
    sums_body(groups, per, entries, me, code, wide_table, wide_source, *outs)
    for copy in copies:
        copy.wait()


def early_body(peers, rows, me, *refs):
    near, outs = refs[:4], refs[4 : 4 + peers]
    padded, summed, top, theta, phi, angles, sems = refs[4 + peers :]
    held = top.shape[0] // 4
    for copy in fetch(list(zip(near, (top, theta, phi, angles), strict=True)), sems):
        copy.wait()
    narrowed = lax.dot_general(top[...], phi[...], NT, preferred_element_type=F32)
    padded[...] = jnp.zeros(padded.shape, F32)
    for k in range(4):
        padded[k, me[0]] = narrowed[k * held : (k + 1) * held]
    for k in range(4):
        full = padded[k].reshape(peers * held, narrowed.shape[1])
        part = split_dot(theta[...], full, (((1,), (0,)), ((), ())))
        summed[k] = part.reshape(peers, rows, narrowed.shape[1])
    low = angles.shape[1]
    half = angles.shape[0] // 2
    for mask, out in enumerate(outs):
        for k in range(4):
            out[k * rows : (k + 1) * rows] = summed[k, jnp.bitwise_xor(me[0], mask)]
        for c in range(half):
            start = 4 * rows + c * low
            out[start : start + low, 0:128] = angles[c]
            out[start : start + low, 128:256] = angles[half + c]


def shift_body(peers, rows, low, me, *refs):
    parts, near = refs[:peers], refs[peers : peers + 4]
    shifted, trig, mix, low_out, switch_out, angles, phi, theta, switch, sems = refs[peers + 4 :]
    for copy in fetch(list(zip(near, (angles, phi, theta, switch), strict=True)), sems):
        copy.wait()
    low_out[...] = theta[...]
    switch_out[...] = switch[...]
    size = phi.shape[1]
    mix[0:size, 0:size] = phi[0]
    mix[0:size, size:] = -phi[1]
    mix[size:, 0:size] = phi[1]
    mix[size:, size:] = phi[0]
    children = angles.shape[0]
    half = children // 2
    for c in range(children):
        cosine, sine = jnp.cos(angles[c]), jnp.sin(angles[c])
        for b in range(2):
            re = parts[0][2 * b * rows : (2 * b + 1) * rows]
            im = parts[0][(2 * b + 1) * rows : (2 * b + 2) * rows]
            for part in parts[1:]:
                re = re + part[2 * b * rows : (2 * b + 1) * rows]
                im = im + part[(2 * b + 1) * rows : (2 * b + 2) * rows]
            shifted[b * children + c, 0] = re * cosine - im * sine
            shifted[b * children + c, 1] = re * sine + im * cosine
    for mask, part in enumerate(parts):
        for c in range(half):
            start = 4 * rows + c * low
            for side in range(2):
                angle = part[start : start + low, side * 128 : side * 128 + 128]
                place = jnp.bitwise_xor(me[0], mask)
                trig[0, side * half + c, place] = jnp.cos(angle)
                trig[1, side * half + c, place] = jnp.sin(angle)


def join(owns, got):
    def body(*refs):
        first = 0
        count = len(owns)
        for own, out in zip(refs[:count], refs[count + 1 :], strict=True):
            size = own.shape[0]
            out[...] = (own[...] + refs[count][first : first + size].astype(F32)).astype(BF16)
            first += size

    return kernel_call(body, [struct(a.shape, BF16) for a in owns], [], [*owns, got], "join")


def close_body(masks, firsts, per, entries, me, code, table, source, got, *refs):
    count = len(masks)
    rows = table.shape[1] // 2
    for mask, begin, piece, out in zip(masks, firsts, refs[:count], refs[count:], strict=True):
        first = jnp.bitwise_xor(me[0], mask) * per

        def one(i, carry, first=first, begin=begin, out=out):
            real, imag = box_sum(first + i, entries, code, table, source)
            real = real + got[begin + i, 0:rows].astype(F32)
            imag = imag + got[begin + i, rows:].astype(F32)
            out[i, 0:rows] = real.astype(BF16)
            out[i, rows:] = imag.astype(BF16)
            return carry

        lax.fori_loop(0, per, one, 0, unroll=2)
        out[per:] = piece[...]


def upper_body(masks, peers, entries, me, home, ids, offsets, own, far, table, shifted, phi, *refs):
    outs, pool = refs[: len(masks)], refs[-1]
    boxes, _, rows, _ = own.shape
    pool[0:boxes] = own[...].astype(F32)
    pool[boxes:] = far[...].astype(F32)
    spans = [slice(r, r + 8) for r in range(0, rows, 8)]
    per = boxes // peers
    for mask, out in zip(masks, outs, strict=True):
        first = jnp.bitwise_xor(me[0], mask) * per

        def one(i, carry, first=first, out=out):
            box = first + i
            real = [shifted[box, 0, span] for span in spans]
            imag = [shifted[box, 1, span] for span in spans]
            for entry in range(entries):
                offset, ident = offsets[box, entry], ids[box, entry]
                if boxes & (boxes - 1):
                    place = lax.rem(ident, boxes)
                else:
                    place = ident & (boxes - 1)
                place = jnp.where(ident - place == home[0] * boxes, place, place + boxes)
                for k, span in enumerate(spans):
                    fr, fi = table[offset, 0, span].astype(F32), table[offset, 1, span].astype(F32)
                    sr, si = pool[place, 0, span], pool[place, 1, span]
                    real[k] = real[k] + (fr * sr - fi * si)
                    imag[k] = imag[k] + (fr * si + fi * sr)
            incoming = jnp.concatenate([*real, *imag], axis=0).astype(BF16)
            narrow = lax.dot_general(incoming, phi[...], NT, preferred_element_type=F32)
            out[i] = narrow.astype(BF16)
            return carry

        lax.fori_loop(0, per, one, 0)


def place_body(*refs):
    count = len(refs) // 2
    for low, out in zip(refs[:count], refs[count:], strict=True):
        out[...] = low[...].astype(F32)


def final_body(peers, parents, me, *refs):
    near = peers // 2
    ups, lows = refs[:near], refs[near : near + peers]
    trig, theta, mix, expand, out, rows_up, rows_low, turned, ready, sems = refs[near + peers :]
    children, rows = trig.shape[1], trig.shape[2]
    high_rows, low_rows = rows_up.shape[3], rows_low.shape[3]
    orders = expand.shape[0]
    boxes = parents * children
    for mask in range(peers):
        place = jnp.bitwise_xor(me[0], mask)
        for c in range(2):
            for b in range(parents):
                if mask < near:
                    piece = lows[mask][boxes + 2 * b + c]
                else:
                    piece = ups[mask - near][b, c * high_rows : (c + 1) * high_rows]
                rows_up[b, c, place] = piece.astype(F32)
            piece = lows[mask][0:boxes, c * low_rows : (c + 1) * low_rows]
            rows_low[:, c, place] = piece.astype(F32)
    copies = []
    for b in range(parents):
        coarse = []
        for c in range(2):
            full = rows_up[b, c].reshape(peers * high_rows, 128).astype(BF16)
            coarse.append(jnp.dot(theta[...], full, preferred_element_type=F32))
        for k in range(children):
            cosine, sine = trig[0, k], trig[1, k]
            box = b * children + k
            real = coarse[0] * cosine - coarse[1] * sine + rows_low[box, 0].reshape(rows, 128)
            imag = coarse[0] * sine + coarse[1] * cosine + rows_low[box, 1].reshape(rows, 128)
            pattern = jnp.concatenate([real.astype(BF16), imag.astype(BF16)], axis=1)
            half = jnp.dot(expand[...], pattern, preferred_element_type=F32)
            high = half.astype(BF16)
            turned[k * orders : (k + 1) * orders] = high
            low = (half - high.astype(F32)).astype(BF16)
            turned[(children + k) * orders : (children + k + 1) * orders] = low
        both = lax.dot_general(turned[...], mix[...], NT, preferred_element_type=F32)
        size = children * orders
        result = both[:size] + both[size:]
        start = b * 2 * size
        ready[pl.ds(start, size, stride=2)] = result[:, :128]
        ready[pl.ds(start + 1, size, stride=2)] = result[:, 128:]
        span = pl.ds(start, 2 * size)
        copies += fetch([(ready.at[span], out.at[span])], sems.at[pl.ds(b, 1)])
    for copy in copies:
        copy.wait()


def struct(shape, dtype):
    return jax.ShapeDtypeStruct(shape, dtype)


def per_device(
    top_patterns,
    theta_upper,
    phi_upper,
    angles_upper,
    table_upper,
    outgoing_upper,
    list_upper,
    offset_upper,
    theta_lower,
    phi_lower,
    angles_lower,
    table_lower,
    outgoing_lower,
    list_lower,
    offset_lower,
    switch_theta,
    switch_phi,
):
    peers = lax.axis_size("angle")
    home = lax.axis_index("box")
    me = lax.axis_index("angle").astype(jnp.int32).reshape(1)
    far_mask = lax.axis_size("box") // 2
    boxes, _, low, lanes = outgoing_lower.shape
    per = boxes // peers
    entries = list_lower.shape[1]
    upper_boxes, _, rows, wide = outgoing_upper.shape
    upper_per = upper_boxes // peers

    other = list_lower.T // boxes != home
    spot = list_lower.T % boxes
    ask_code = (jnp.where(other, spot, boxes) << SHIFT) + offset_lower.T
    own_code = (jnp.where(other, boxes, spot) << SHIFT) + offset_lower.T
    far_code = swap(ask_code, "box", 1)
    far_upper = swap(outgoing_upper, "box", far_mask)

    places = table_lower.shape[0]
    outer, inner = list(range(peers - 1, peers // 2 - 1, -1)), list(range(peers // 2 - 1, -1, -1))

    def sums(groups, outs, codes, order, name):
        return kernel_call(
            functools.partial(sums_body, groups, per, entries),
            outs,
            [order, *codes],
            [table, source],
            name,
        )

    own_shape = struct((per, 2 * low, lanes), F32)
    far_shape = struct((len(outer) * per, 2 * low, lanes), BF16)
    *first, table, source = kernel_call(
        functools.partial(first_body, [((mask,), 0) for mask in outer], per, entries),
        [
            *[struct((per, 2 * low, lanes), BF16)] * len(outer),
            struct((places, 2 * low, lanes), F32),
            struct((boxes + 1, 2 * low, lanes), F32),
        ],
        [me, far_code],
        [table_lower.reshape(-1, 2 * low, lanes), outgoing_lower.reshape(-1, 2 * low, lanes)],
        "sums_first",
        scratch=[
            pltpu.VMEM((places, 2 * low, lanes), BF16),
            pltpu.VMEM((boxes, 2 * low, lanes), BF16),
            pltpu.VMEM((places, 2 * low, lanes), F32),
            pltpu.VMEM((boxes + 1, 2 * low, lanes), F32),
            pltpu.SemaphoreType.DMA((5,)),
            pltpu.SemaphoreType.DMA((2,)),
        ],
        held=2,
        away=2,
        vmem=53 << 20,
    )
    got_outer = [swap(value, "box", 1) for value in first]

    children = angles_lower.shape[0]
    part_rows = 4 * rows + children * low // 2
    held = top_patterns.shape[2]
    top = top_patterns.reshape(4 * held, -1)
    parts = kernel_call(
        functools.partial(early_body, peers, rows),
        [struct((part_rows, wide), F32)] * peers,
        [after(me, first[0])],
        [top, theta_upper, phi_upper, angles_lower],
        "early",
        scratch=[
            pltpu.VMEM((4, peers, held, wide), F32),
            pltpu.VMEM((4, peers, rows, wide), F32),
            *(pltpu.VMEM(a.shape, a.dtype) for a in (top, theta_upper, phi_upper, angles_lower)),
            pltpu.SemaphoreType.DMA((4,)),
        ],
        held=4,
    )
    order = after(me, parts[0])
    parts = [swap(part, "angle", mask) if mask else part for mask, part in enumerate(parts)]
    own_outer = sums(
        [((mask,), 0) for mask in outer],
        [own_shape] * len(outer),
        [own_code],
        order,
        "sums_third",
    )
    lows = {}
    for mask, own, got in list(zip(outer, own_outer, got_outer, strict=True))[: len(outer) // 2]:
        (lows[mask],) = join([own], got)
    (second,) = sums([(tuple(inner), 0)], [far_shape], [far_code], after(me, lows[outer[0]]), "sums_second")
    got_inner = swap(second, "box", 1)
    orders = switch_theta.shape[0]
    azimuths = switch_phi.shape[1]
    shifted, trig, mix, theta_low, theta_switch = kernel_call(
        functools.partial(shift_body, peers, rows, low),
        [
            struct((upper_boxes, 2, rows, wide), F32),
            struct((2, children, peers, low, lanes), F32),
            struct((2 * azimuths, 2 * azimuths), BF16),
            struct(theta_lower.shape, BF16),
            struct(switch_theta.shape, BF16),
        ],
        [after(me, second)],
        [*parts, angles_upper, switch_phi, theta_lower, switch_theta],
        "shift",
        scratch=[
            *(pltpu.VMEM(a.shape, a.dtype) for a in (angles_upper, switch_phi, theta_lower, switch_theta)),
            pltpu.SemaphoreType.DMA((4,)),
        ],
        held=4,
    )
    for mask, own, got in list(zip(outer, own_outer, got_outer, strict=True))[len(outer) // 2 :]:
        (lows[mask],) = join([after(own, trig)], got)
    trig = trig.reshape(2, children, peers * low, lanes)
    ups = kernel_call(
        functools.partial(upper_body, outer + inner, peers, entries),
        [struct((upper_per, 2 * rows, lanes), BF16)] * peers,
        [after(me, lows[outer[-1]]), home.astype(jnp.int32).reshape(1), list_upper, offset_upper],
        [outgoing_upper, far_upper, table_upper, shifted, phi_lower],
        "upper",
        scratch=[pltpu.VMEM((2 * upper_boxes, 2, rows, wide), F32)],
    )
    ups = dict(zip(outer + inner, ups, strict=True))
    order = after(me, ups[0])
    behind = {mask: ups.pop(mask).reshape(-1, 2 * low, lanes) for mask in inner}
    for masks, name in ((inner[:-1], "close_peers"), (inner[-1:], "close_self")):
        close = kernel_call(
            functools.partial(close_body, masks, [per * inner.index(m) for m in masks], per, entries),
            [struct((per + behind[0].shape[0], 2 * low, lanes), BF16)] * len(masks),
            [order, own_code],
            [table, source, got_inner, *(behind[mask] for mask in masks)],
            name,
        )
        lows.update(zip(masks, close, strict=True))
        order = after(me, close[0])
    ups = [swap(ups[mask], "angle", mask) for mask in reversed(outer)]
    lows = [swap(lows[mask], "angle", mask) if mask else lows[mask] for mask in range(peers)]

    arrived = kernel_call(
        place_body,
        [struct(lows[mask].shape, F32) for mask in outer],
        [],
        [lows[mask] for mask in outer],
        "place",
    )
    lows = [*lows[: len(inner)], *reversed(arrived)]
    (out,) = kernel_call(
        functools.partial(final_body, peers, upper_per),
        [struct((per * 2 * orders, azimuths), F32)],
        [me],
        [*ups, *lows, trig, theta_low, mix, theta_switch],
        "expand",
        scratch=[
            pltpu.VMEM((upper_per, 2, peers, rows, lanes), F32),
            pltpu.VMEM((per, 2, peers, low, lanes), F32),
            pltpu.VMEM((2 * children * orders, 2 * lanes), BF16),
            pltpu.VMEM((per * 2 * orders + 8, azimuths), F32),
            pltpu.SemaphoreType.DMA((upper_per,)),
        ],
        away=1,
        vmem=12 << 20,
    )
    out = out.reshape(per, orders, 2, azimuths)
    return jnp.transpose(out, (0, 2, 1, 3)).reshape(per, 2, orders * azimuths)


def solution(mesh):
    return jax.shard_map(
        per_device,
        mesh=mesh,
        in_specs=(
            P("box", None, "angle", None),
            P(),
            P(),
            P(None, "angle", None),
            P(None, None, "angle", None),
            P("box", None, "angle", None),
            P("box", None),
            P("box", None),
            P(),
            P(),
            P(None, "angle", None),
            P(None, None, "angle", None),
            P("box", None, "angle", None),
            P("box", None),
            P("box", None),
            P(),
            P(),
        ),
        out_specs=P(("box", "angle"), None, None),
        check_vma=False,
    )
```

```python
import functools

import jax
import jax.numpy as jnp
from jax import lax
from jax.experimental import pallas as pl
from jax.experimental.pallas import tpu as pltpu
from jax.sharding import PartitionSpec as P

F32, BF16 = jnp.float32, jnp.bfloat16
VM = pl.BlockSpec(memory_space=pltpu.VMEM)
SM = pl.BlockSpec(memory_space=pltpu.SMEM)
HB = pl.BlockSpec(memory_space=pltpu.HBM)
SHIFT = 9
NT = (((1,), (1,)), ((), ()))


def swap(value, axis, mask):
    pairs = [(source, source ^ mask) for source in range(lax.axis_size(axis))]
    return lax.ppermute(value, axis, pairs)


COSTS = {"join": 0, "sums_third": 0, "shift": 0, "close_peers": 0, "close_self": 0}


def after(value, *others):
    return lax.optimization_barrier((value, *others))[0]


def kernel_call(body, outs, scalars, arrays, name, scratch=(), held=0, vmem=6 << 20, away=0):
    near = len(arrays) - held
    return pl.pallas_call(
        body,
        out_shape=outs,
        in_specs=[SM] * len(scalars) + [VM] * near + [HB] * held,
        out_specs=[VM] * (len(outs) - away) + [HB] * away,
        scratch_shapes=list(scratch),
        compiler_params=pltpu.CompilerParams(vmem_limit_bytes=vmem),
        cost_estimate=pl.CostEstimate(flops=COSTS.get(name, 4) << 30, bytes_accessed=1, transcendentals=0),
        name=name,
    )(*scalars, *arrays)


def fetch(pairs, sems):
    copies = [pltpu.make_async_copy(a, b, sems.at[k]) for k, (a, b) in enumerate(pairs)]
    for copy in copies:
        copy.start()
    return copies


def split_dot(left, value, dims):
    high = value.astype(BF16)
    low = (value - high.astype(F32)).astype(BF16)
    return lax.dot_general(left, high, dims, preferred_element_type=F32) + lax.dot_general(
        left, low, dims, preferred_element_type=F32
    )


def box_sum(box, entries, code, table, source):
    rows = table.shape[1] // 2
    real = imag = None
    for entry in range(entries):
        word = code[entry, box]
        factor = table[word & ((1 << SHIFT) - 1)]
        value = source[word >> SHIFT]
        fr, fi, sr, si = factor[:rows], factor[rows:], value[:rows], value[rows:]
        re, im = fr * sr - fi * si, fr * si + fi * sr
        real = re if real is None else real + re
        imag = im if imag is None else imag + im
    return real, imag


def sums_body(groups, per, entries, me, *refs):
    codes = max(which for _, which in groups) + 1
    code_refs, (table, source), outs = refs[:codes], refs[codes : codes + 2], refs[codes + 2 :]
    rows = table.shape[1] // 2
    for (masks, which), out in zip(groups, outs, strict=True):
        for place, mask in enumerate(masks):
            first = jnp.bitwise_xor(me[0], mask) * per

            def one(i, carry, first=first, place=place, which=which, out=out):
                real, imag = box_sum(first + i, entries, code_refs[which], table, source)
                out[place * per + i, 0:rows] = real.astype(out.dtype)
                out[place * per + i, rows:] = imag.astype(out.dtype)
                return carry

            lax.fori_loop(0, per, one, 0, unroll=2)


def first_body(groups, per, entries, me, code, table, source, *refs):
    outs = refs[: len(groups)]
    table_out, source_out, table_in, source_in, wide_table, wide_source, sems, back = refs[len(groups) :]
    count, total = source.shape[0], table.shape[0]
    step = -(-total // 4)
    spans = [(k, min(k + step, total)) for k in range(0, total, step)]
    pairs = [(source, source_in)]
    pairs += [(table.at[lo:hi], table_in.at[lo:hi]) for lo, hi in spans]
    copies = fetch(pairs, sems)
    copies[0].wait()
    wide_source[0:count] = source_in[...].astype(F32)
    wide_source[count] = jnp.zeros(source.shape[1:], F32)
    for copy, (lo, hi) in zip(copies[1:], spans, strict=True):
        copy.wait()
        wide_table[lo:hi] = table_in[lo:hi].astype(F32)
    copies = fetch([(wide_table, table_out), (wide_source, source_out)], back)
    sums_body(groups, per, entries, me, code, wide_table, wide_source, *outs)
    for copy in copies:
        copy.wait()


def early_body(peers, rows, me, *refs):
    near, outs = refs[:4], refs[4 : 4 + peers]
    padded, summed, top, theta, phi, angles, sems = refs[4 + peers :]
    held = top.shape[0] // 4
    for copy in fetch(list(zip(near, (top, theta, phi, angles), strict=True)), sems):
        copy.wait()
    narrowed = lax.dot_general(top[...], phi[...], NT, preferred_element_type=F32)
    padded[...] = jnp.zeros(padded.shape, F32)
    for k in range(4):
        padded[k, me[0]] = narrowed[k * held : (k + 1) * held]
    for k in range(4):
        full = padded[k].reshape(peers * held, narrowed.shape[1])
        part = split_dot(theta[...], full, (((1,), (0,)), ((), ())))
        summed[k] = part.reshape(peers, rows, narrowed.shape[1])
    low = angles.shape[1]
    half = angles.shape[0] // 2
    for mask, out in enumerate(outs):
        for k in range(4):
            out[k * rows : (k + 1) * rows] = summed[k, jnp.bitwise_xor(me[0], mask)]
        for c in range(half):
            start = 4 * rows + c * low
            out[start : start + low, 0:128] = angles[c]
            out[start : start + low, 128:256] = angles[half + c]


def shift_body(peers, rows, low, me, *refs):
    parts, near = refs[:peers], refs[peers : peers + 4]
    shifted, trig, mix, low_out, switch_out, angles, phi, theta, switch, sems = refs[peers + 4 :]
    for copy in fetch(list(zip(near, (angles, phi, theta, switch), strict=True)), sems):
        copy.wait()
    low_out[...] = theta[...]
    switch_out[...] = switch[...]
    size = phi.shape[1]
    mix[0:size, 0:size] = phi[0]
    mix[0:size, size:] = -phi[1]
    mix[size:, 0:size] = phi[1]
    mix[size:, size:] = phi[0]
    children = angles.shape[0]
    half = children // 2
    for c in range(children):
        cosine, sine = jnp.cos(angles[c]), jnp.sin(angles[c])
        for b in range(2):
            re = parts[0][2 * b * rows : (2 * b + 1) * rows]
            im = parts[0][(2 * b + 1) * rows : (2 * b + 2) * rows]
            for part in parts[1:]:
                re = re + part[2 * b * rows : (2 * b + 1) * rows]
                im = im + part[(2 * b + 1) * rows : (2 * b + 2) * rows]
            shifted[b * children + c, 0] = re * cosine - im * sine
            shifted[b * children + c, 1] = re * sine + im * cosine
    for mask, part in enumerate(parts):
        for c in range(half):
            start = 4 * rows + c * low
            for side in range(2):
                angle = part[start : start + low, side * 128 : side * 128 + 128]
                place = jnp.bitwise_xor(me[0], mask)
                trig[0, side * half + c, place] = jnp.cos(angle)
                trig[1, side * half + c, place] = jnp.sin(angle)


def join(owns, got):
    def body(*refs):
        first = 0
        count = len(owns)
        for own, out in zip(refs[:count], refs[count + 1 :], strict=True):
            size = own.shape[0]
            out[...] = (own[...] + refs[count][first : first + size].astype(F32)).astype(BF16)
            first += size

    return kernel_call(body, [struct(a.shape, BF16) for a in owns], [], [*owns, got], "join")


def close_body(masks, firsts, per, entries, me, code, table, source, got, *refs):
    count = len(masks)
    rows = table.shape[1] // 2
    for mask, begin, piece, out in zip(masks, firsts, refs[:count], refs[count:], strict=True):
        first = jnp.bitwise_xor(me[0], mask) * per

        def one(i, carry, first=first, begin=begin, out=out):
            real, imag = box_sum(first + i, entries, code, table, source)
            real = real + got[begin + i, 0:rows].astype(F32)
            imag = imag + got[begin + i, rows:].astype(F32)
            out[i, 0:rows] = real.astype(BF16)
            out[i, rows:] = imag.astype(BF16)
            return carry

        lax.fori_loop(0, per, one, 0, unroll=2)
        out[per:] = piece[...]


def upper_body(masks, peers, entries, me, home, ids, offsets, own, far, table, shifted, phi, *refs):
    outs, (pool, rounded) = refs[: len(masks)], refs[len(masks) :]
    boxes, _, rows, wide = own.shape
    pool[0:boxes] = own[...].astype(F32)
    pool[boxes:] = far[...].astype(F32)
    spans = [slice(r, r + 8) for r in range(0, rows, 8)]
    per = boxes // peers
    for turn, mask in enumerate(masks):
        first = jnp.bitwise_xor(me[0], mask) * per

        def one(i, carry, first=first, turn=turn):
            box = first + i
            real = [shifted[box, 0, span] for span in spans]
            imag = [shifted[box, 1, span] for span in spans]
            for entry in range(entries):
                offset, ident = offsets[box, entry], ids[box, entry]
                if boxes & (boxes - 1):
                    place = lax.rem(ident, boxes)
                else:
                    place = ident & (boxes - 1)
                place = jnp.where(ident - place == home[0] * boxes, place, place + boxes)
                for k, span in enumerate(spans):
                    fr, fi = table[offset, 0, span].astype(F32), table[offset, 1, span].astype(F32)
                    sr, si = pool[place, 0, span], pool[place, 1, span]
                    real[k] = real[k] + (fr * sr - fi * si)
                    imag[k] = imag[k] + (fr * si + fi * sr)
            rounded[turn * per + i] = jnp.concatenate([*real, *imag], axis=0).astype(BF16)
            return carry

        lax.fori_loop(0, per, one, 0)
    for turn, out in enumerate(outs):
        incoming = rounded[turn * per : (turn + 1) * per].reshape(per * 2 * rows, wide)
        narrow = lax.dot_general(incoming, phi[...], NT, preferred_element_type=F32)
        out[...] = narrow.astype(BF16).reshape(out.shape)


def place_body(*refs):
    count = len(refs) // 2
    for low, out in zip(refs[:count], refs[count:], strict=True):
        out[...] = low[...].astype(F32)


def final_body(peers, parents, me, *refs):
    near = peers // 2
    ups, lows = refs[:near], refs[near : near + peers]
    trig, theta, mix, expand, out, rows_up, rows_low, turned, ready, sems = refs[near + peers :]
    children, rows = trig.shape[1], trig.shape[2]
    high_rows, low_rows = rows_up.shape[3], rows_low.shape[3]
    orders = expand.shape[0]
    boxes = parents * children
    for mask in range(peers):
        place = jnp.bitwise_xor(me[0], mask)
        for c in range(2):
            for b in range(parents):
                if mask < near:
                    piece = lows[mask][boxes + 2 * b + c]
                else:
                    piece = ups[mask - near][b, c * high_rows : (c + 1) * high_rows]
                rows_up[b, c, place] = piece.astype(F32)
            piece = lows[mask][0:boxes, c * low_rows : (c + 1) * low_rows]
            rows_low[:, c, place] = piece.astype(F32)
    copies = []
    for b in range(parents):
        coarse = []
        for c in range(2):
            full = rows_up[b, c].reshape(peers * high_rows, 128).astype(BF16)
            coarse.append(jnp.dot(theta[...], full, preferred_element_type=F32))
        for k in range(children):
            cosine, sine = trig[0, k], trig[1, k]
            box = b * children + k
            real = coarse[0] * cosine - coarse[1] * sine + rows_low[box, 0].reshape(rows, 128)
            imag = coarse[0] * sine + coarse[1] * cosine + rows_low[box, 1].reshape(rows, 128)
            pattern = jnp.concatenate([real.astype(BF16), imag.astype(BF16)], axis=1)
            half = jnp.dot(expand[...], pattern, preferred_element_type=F32)
            high = half.astype(BF16)
            turned[k * orders : (k + 1) * orders] = high
            low = (half - high.astype(F32)).astype(BF16)
            turned[(children + k) * orders : (children + k + 1) * orders] = low
        both = lax.dot_general(turned[...], mix[...], NT, preferred_element_type=F32)
        size = children * orders
        result = both[:size] + both[size:]
        start = b * 2 * size
        ready[pl.ds(start, size, stride=2)] = result[:, :128]
        ready[pl.ds(start + 1, size, stride=2)] = result[:, 128:]
        span = pl.ds(start, 2 * size)
        copies += fetch([(ready.at[span], out.at[span])], sems.at[pl.ds(b, 1)])
    for copy in copies:
        copy.wait()


def struct(shape, dtype):
    return jax.ShapeDtypeStruct(shape, dtype)


def per_device(
    top_patterns,
    theta_upper,
    phi_upper,
    angles_upper,
    table_upper,
    outgoing_upper,
    list_upper,
    offset_upper,
    theta_lower,
    phi_lower,
    angles_lower,
    table_lower,
    outgoing_lower,
    list_lower,
    offset_lower,
    switch_theta,
    switch_phi,
):
    peers = lax.axis_size("angle")
    home = lax.axis_index("box")
    me = lax.axis_index("angle").astype(jnp.int32).reshape(1)
    far_mask = lax.axis_size("box") // 2
    boxes, _, low, lanes = outgoing_lower.shape
    per = boxes // peers
    entries = list_lower.shape[1]
    upper_boxes, _, rows, wide = outgoing_upper.shape
    upper_per = upper_boxes // peers

    other = list_lower.T // boxes != home
    spot = list_lower.T % boxes
    ask_code = (jnp.where(other, spot, boxes) << SHIFT) + offset_lower.T
    own_code = (jnp.where(other, boxes, spot) << SHIFT) + offset_lower.T
    far_code = swap(ask_code, "box", 1)
    far_upper = swap(outgoing_upper, "box", far_mask)

    places = table_lower.shape[0]
    outer, inner = list(range(peers - 1, peers // 2 - 1, -1)), list(range(peers // 2 - 1, -1, -1))

    def sums(groups, outs, codes, order, name):
        return kernel_call(
            functools.partial(sums_body, groups, per, entries),
            outs,
            [order, *codes],
            [table, source],
            name,
        )

    own_shape = struct((per, 2 * low, lanes), F32)
    far_shape = struct((len(outer) * per, 2 * low, lanes), BF16)
    *first, table, source = kernel_call(
        functools.partial(first_body, [((mask,), 0) for mask in outer], per, entries),
        [
            *[struct((per, 2 * low, lanes), BF16)] * len(outer),
            struct((places, 2 * low, lanes), F32),
            struct((boxes + 1, 2 * low, lanes), F32),
        ],
        [me, far_code],
        [table_lower.reshape(-1, 2 * low, lanes), outgoing_lower.reshape(-1, 2 * low, lanes)],
        "sums_first",
        scratch=[
            pltpu.VMEM((places, 2 * low, lanes), BF16),
            pltpu.VMEM((boxes, 2 * low, lanes), BF16),
            pltpu.VMEM((places, 2 * low, lanes), F32),
            pltpu.VMEM((boxes + 1, 2 * low, lanes), F32),
            pltpu.SemaphoreType.DMA((5,)),
            pltpu.SemaphoreType.DMA((2,)),
        ],
        held=2,
        away=2,
        vmem=53 << 20,
    )
    got_outer = [swap(value, "box", 1) for value in first]

    children = angles_lower.shape[0]
    part_rows = 4 * rows + children * low // 2
    held = top_patterns.shape[2]
    top = top_patterns.reshape(4 * held, -1)
    parts = kernel_call(
        functools.partial(early_body, peers, rows),
        [struct((part_rows, wide), F32)] * peers,
        [after(me, first[0])],
        [top, theta_upper, phi_upper, angles_lower],
        "early",
        scratch=[
            pltpu.VMEM((4, peers, held, wide), F32),
            pltpu.VMEM((4, peers, rows, wide), F32),
            *(pltpu.VMEM(a.shape, a.dtype) for a in (top, theta_upper, phi_upper, angles_lower)),
            pltpu.SemaphoreType.DMA((4,)),
        ],
        held=4,
    )
    order = after(me, parts[0])
    parts = [swap(part, "angle", mask) if mask in outer else part for mask, part in enumerate(parts)]
    own_outer = sums(
        [((mask,), 0) for mask in outer],
        [own_shape] * len(outer),
        [own_code],
        order,
        "sums_third",
    )
    lows = {}
    for mask, own, got in list(zip(outer, own_outer, got_outer, strict=True))[: len(outer) // 2]:
        (lows[mask],) = join([own], got)
    (second,) = sums([(tuple(inner), 0)], [far_shape], [far_code], after(me, lows[outer[0]]), "sums_second")
    got_inner = swap(second, "box", 1)
    late = after(parts[1], second)
    parts = [parts[0]] + [swap(late if mask == 1 else parts[mask], "angle", mask) for mask in inner[-2::-1]] + [*parts[len(inner) :]]
    orders = switch_theta.shape[0]
    azimuths = switch_phi.shape[1]
    shifted, trig, mix, theta_low, theta_switch = kernel_call(
        functools.partial(shift_body, peers, rows, low),
        [
            struct((upper_boxes, 2, rows, wide), F32),
            struct((2, children, peers, low, lanes), F32),
            struct((2 * azimuths, 2 * azimuths), BF16),
            struct(theta_lower.shape, BF16),
            struct(switch_theta.shape, BF16),
        ],
        [after(me, second)],
        [*parts, angles_upper, switch_phi, theta_lower, switch_theta],
        "shift",
        scratch=[
            *(pltpu.VMEM(a.shape, a.dtype) for a in (angles_upper, switch_phi, theta_lower, switch_theta)),
            pltpu.SemaphoreType.DMA((4,)),
        ],
        held=4,
    )
    for mask, own, got in list(zip(outer, own_outer, got_outer, strict=True))[len(outer) // 2 :]:
        (lows[mask],) = join([after(own, trig)], got)
    trig = trig.reshape(2, children, peers * low, lanes)
    ups = kernel_call(
        functools.partial(upper_body, outer + inner, peers, entries),
        [struct((upper_per, 2 * rows, lanes), BF16)] * peers,
        [after(me, lows[outer[-1]]), home.astype(jnp.int32).reshape(1), list_upper, offset_upper],
        [outgoing_upper, far_upper, table_upper, shifted, phi_lower],
        "upper",
        scratch=[
            pltpu.VMEM((2 * upper_boxes, 2, rows, wide), F32),
            pltpu.VMEM((upper_boxes, 2 * rows, wide), BF16),
        ],
    )
    ups = dict(zip(outer + inner, ups, strict=True))
    order = after(me, ups[0])
    behind = {mask: ups.pop(mask).reshape(-1, 2 * low, lanes) for mask in inner}
    for masks, name in ((inner[:-1], "close_peers"), (inner[-1:], "close_self")):
        close = kernel_call(
            functools.partial(close_body, masks, [per * inner.index(m) for m in masks], per, entries),
            [struct((per + behind[0].shape[0], 2 * low, lanes), BF16)] * len(masks),
            [order, own_code],
            [table, source, got_inner, *(behind[mask] for mask in masks)],
            name,
        )
        lows.update(zip(masks, close, strict=True))
        order = after(me, close[0])
    ups = [swap(ups[mask], "angle", mask) for mask in reversed(outer)]
    lows = [swap(lows[mask], "angle", mask) if mask else lows[mask] for mask in range(peers)]

    arrived = kernel_call(
        place_body,
        [struct(lows[mask].shape, F32) for mask in outer],
        [],
        [lows[mask] for mask in outer],
        "place",
    )
    lows = [*lows[: len(inner)], *reversed(arrived)]
    (out,) = kernel_call(
        functools.partial(final_body, peers, upper_per),
        [struct((per * 2 * orders, azimuths), F32)],
        [me],
        [*ups, *lows, trig, theta_low, mix, theta_switch],
        "expand",
        scratch=[
            pltpu.VMEM((upper_per, 2, peers, rows, lanes), F32),
            pltpu.VMEM((per, 2, peers, low, lanes), F32),
            pltpu.VMEM((2 * children * orders, 2 * lanes), BF16),
            pltpu.VMEM((per * 2 * orders + 8, azimuths), F32),
            pltpu.SemaphoreType.DMA((upper_per,)),
        ],
        away=1,
        vmem=12 << 20,
    )
    out = out.reshape(per, orders, 2, azimuths)
    return jnp.transpose(out, (0, 2, 1, 3)).reshape(per, 2, orders * azimuths)


def solution(mesh):
    return jax.shard_map(
        per_device,
        mesh=mesh,
        in_specs=(
            P("box", None, "angle", None),
            P(),
            P(),
            P(None, "angle", None),
            P(None, None, "angle", None),
            P("box", None, "angle", None),
            P("box", None),
            P("box", None),
            P(),
            P(),
            P(None, "angle", None),
            P(None, None, "angle", None),
            P("box", None, "angle", None),
            P("box", None),
            P("box", None),
            P(),
            P(),
        ),
        out_specs=P(("box", "angle"), None, None),
        check_vma=False,
    )
```

```python
import functools

import jax
import jax.numpy as jnp
from jax import lax
from jax.experimental import pallas as pl
from jax.experimental.pallas import tpu as pltpu
from jax.sharding import PartitionSpec as P

F32, BF16 = jnp.float32, jnp.bfloat16
VM = pl.BlockSpec(memory_space=pltpu.VMEM)
SM = pl.BlockSpec(memory_space=pltpu.SMEM)
HB = pl.BlockSpec(memory_space=pltpu.HBM)
SHIFT = 9
NT = (((1,), (1,)), ((), ()))


def swap(value, axis, mask):
    pairs = [(source, source ^ mask) for source in range(lax.axis_size(axis))]
    return lax.ppermute(value, axis, pairs)


COSTS = {"join": 0, "sums_third": 0, "sums_second": 0, "shift": 0, "upper": 1, "close_peers": 0, "close_self": 0}


def after(value, *others):
    return lax.optimization_barrier((value, *others))[0]


def kernel_call(body, outs, scalars, arrays, name, scratch=(), held=0, vmem=6 << 20, away=0):
    near = len(arrays) - held
    return pl.pallas_call(
        body,
        out_shape=outs,
        in_specs=[SM] * len(scalars) + [VM] * near + [HB] * held,
        out_specs=[VM] * (len(outs) - away) + [HB] * away,
        scratch_shapes=list(scratch),
        compiler_params=pltpu.CompilerParams(vmem_limit_bytes=vmem),
        cost_estimate=pl.CostEstimate(flops=COSTS.get(name, 4) << 30, bytes_accessed=1, transcendentals=0),
        name=name,
    )(*scalars, *arrays)


def fetch(pairs, sems):
    copies = [pltpu.make_async_copy(a, b, sems.at[k]) for k, (a, b) in enumerate(pairs)]
    for copy in copies:
        copy.start()
    return copies


def split_dot(left, value, dims):
    high = value.astype(BF16)
    low = (value - high.astype(F32)).astype(BF16)
    return lax.dot_general(left, high, dims, preferred_element_type=F32) + lax.dot_general(
        left, low, dims, preferred_element_type=F32
    )


def box_sum(box, entries, code, table, source):
    rows = table.shape[1] // 2
    real = imag = None
    for entry in range(entries):
        word = code[entry, box]
        factor = table[word & ((1 << SHIFT) - 1)]
        value = source[word >> SHIFT]
        fr, fi, sr, si = factor[:rows], factor[rows:], value[:rows], value[rows:]
        re, im = fr * sr - fi * si, fr * si + fi * sr
        real = re if real is None else real + re
        imag = im if imag is None else imag + im
    return real, imag


def sums_body(groups, per, entries, me, *refs):
    codes = max(which for _, which in groups) + 1
    code_refs, (table, source), outs = refs[:codes], refs[codes : codes + 2], refs[codes + 2 :]
    rows = table.shape[1] // 2
    for (masks, which), out in zip(groups, outs, strict=True):
        for place, mask in enumerate(masks):
            first = jnp.bitwise_xor(me[0], mask) * per

            def one(i, carry, first=first, place=place, which=which, out=out):
                real, imag = box_sum(first + i, entries, code_refs[which], table, source)
                out[place * per + i, 0:rows] = real.astype(out.dtype)
                out[place * per + i, rows:] = imag.astype(out.dtype)
                return carry

            lax.fori_loop(0, per, one, 0, unroll=2)


def first_body(groups, per, entries, me, code, table, source, *refs):
    outs = refs[: len(groups)]
    table_out, source_out, table_in, source_in, wide_table, wide_source, sems, back = refs[len(groups) :]
    count, total = source.shape[0], table.shape[0]
    step = -(-total // 4)
    spans = [(k, min(k + step, total)) for k in range(0, total, step)]
    pairs = [(source, source_in)]
    pairs += [(table.at[lo:hi], table_in.at[lo:hi]) for lo, hi in spans]
    copies = fetch(pairs, sems)
    copies[0].wait()
    wide_source[0:count] = source_in[...].astype(F32)
    wide_source[count] = jnp.zeros(source.shape[1:], F32)
    for copy, (lo, hi) in zip(copies[1:], spans, strict=True):
        copy.wait()
        wide_table[lo:hi] = table_in[lo:hi].astype(F32)
    copies = fetch([(wide_table, table_out), (wide_source, source_out)], back)
    sums_body(groups, per, entries, me, code, wide_table, wide_source, *outs)
    for copy in copies:
        copy.wait()


def early_body(peers, rows, me, *refs):
    near, outs = refs[:4], refs[4 : 4 + peers]
    padded, summed, top, theta, phi, angles, sems = refs[4 + peers :]
    held = top.shape[0] // 4
    for copy in fetch(list(zip(near, (top, theta, phi, angles), strict=True)), sems):
        copy.wait()
    narrowed = lax.dot_general(top[...], phi[...], NT, preferred_element_type=F32)
    padded[...] = jnp.zeros(padded.shape, F32)
    for k in range(4):
        padded[k, me[0]] = narrowed[k * held : (k + 1) * held]
    for k in range(4):
        full = padded[k].reshape(peers * held, narrowed.shape[1])
        part = split_dot(theta[...], full, (((1,), (0,)), ((), ())))
        summed[k] = part.reshape(peers, rows, narrowed.shape[1])
    low = angles.shape[1]
    half = angles.shape[0] // 2
    for mask, out in enumerate(outs):
        for k in range(4):
            out[k * rows : (k + 1) * rows] = summed[k, jnp.bitwise_xor(me[0], mask)]
        for c in range(half):
            start = 4 * rows + c * low
            out[start : start + low, 0:128] = angles[c]
            out[start : start + low, 128:256] = angles[half + c]


def shift_body(peers, rows, low, me, *refs):
    parts, near = refs[:peers], refs[peers : peers + 4]
    shifted, trig, mix, low_out, switch_out, angles, phi, theta, switch, sems = refs[peers + 4 :]
    for copy in fetch(list(zip(near, (angles, phi, theta, switch), strict=True)), sems):
        copy.wait()
    low_out[...] = theta[...]
    switch_out[...] = switch[...]
    size = phi.shape[1]
    mix[0:size, 0:size] = phi[0]
    mix[0:size, size:] = -phi[1]
    mix[size:, 0:size] = phi[1]
    mix[size:, size:] = phi[0]
    children = angles.shape[0]
    half = children // 2
    for c in range(children):
        cosine, sine = jnp.cos(angles[c]), jnp.sin(angles[c])
        for b in range(2):
            re = parts[0][2 * b * rows : (2 * b + 1) * rows]
            im = parts[0][(2 * b + 1) * rows : (2 * b + 2) * rows]
            for part in parts[1:]:
                re = re + part[2 * b * rows : (2 * b + 1) * rows]
                im = im + part[(2 * b + 1) * rows : (2 * b + 2) * rows]
            shifted[b * children + c, 0] = re * cosine - im * sine
            shifted[b * children + c, 1] = re * sine + im * cosine
    for mask, part in enumerate(parts):
        for c in range(half):
            start = 4 * rows + c * low
            for side in range(2):
                angle = part[start : start + low, side * 128 : side * 128 + 128]
                place = jnp.bitwise_xor(me[0], mask)
                trig[0, side * half + c, place] = jnp.cos(angle)
                trig[1, side * half + c, place] = jnp.sin(angle)


def join(owns, got):
    def body(*refs):
        first = 0
        count = len(owns)
        for own, out in zip(refs[:count], refs[count + 1 :], strict=True):
            size = own.shape[0]
            out[...] = (own[...] + refs[count][first : first + size].astype(F32)).astype(BF16)
            first += size

    return kernel_call(body, [struct(a.shape, BF16) for a in owns], [], [*owns, got], "join")


def close_body(masks, per, entries, me, code, table, source, *refs):
    count = len(masks)
    rows = table.shape[1] // 2
    for k, mask in enumerate(masks):
        got, piece, out = refs[k], refs[count + k], refs[2 * count + k]
        first = jnp.bitwise_xor(me[0], mask) * per

        def one(i, carry, first=first, got=got, out=out):
            real, imag = box_sum(first + i, entries, code, table, source)
            real = real + got[i, 0:rows].astype(F32)
            imag = imag + got[i, rows:].astype(F32)
            out[i, 0:rows] = real.astype(BF16)
            out[i, rows:] = imag.astype(BF16)
            return carry

        lax.fori_loop(0, per, one, 0, unroll=2)
        out[per:] = piece[...]


def upper_body(masks, peers, entries, me, home, ids, offsets, own, far, table, shifted, phi, *refs):
    outs, (pool, rounded) = refs[: len(masks)], refs[len(masks) :]
    boxes, _, rows, wide = own.shape
    pool[0:boxes] = own[...].astype(F32)
    pool[boxes:] = far[...].astype(F32)
    spans = [slice(r, r + 8) for r in range(0, rows, 8)]
    per = boxes // peers
    for turn, mask in enumerate(masks):
        first = jnp.bitwise_xor(me[0], mask) * per

        def one(i, carry, first=first, turn=turn):
            box = first + i
            real = [shifted[box, 0, span] for span in spans]
            imag = [shifted[box, 1, span] for span in spans]
            for entry in range(entries):
                offset, ident = offsets[box, entry], ids[box, entry]
                if boxes & (boxes - 1):
                    place = lax.rem(ident, boxes)
                else:
                    place = ident & (boxes - 1)
                place = jnp.where(ident - place == home[0] * boxes, place, place + boxes)
                for k, span in enumerate(spans):
                    fr, fi = table[offset, 0, span].astype(F32), table[offset, 1, span].astype(F32)
                    sr, si = pool[place, 0, span], pool[place, 1, span]
                    real[k] = real[k] + (fr * sr - fi * si)
                    imag[k] = imag[k] + (fr * si + fi * sr)
            rounded[turn * per + i] = jnp.concatenate([*real, *imag], axis=0).astype(BF16)
            return carry

        lax.fori_loop(0, per, one, 0)
    for turn, out in enumerate(outs):
        incoming = rounded[turn * per : (turn + 1) * per].reshape(per * 2 * rows, wide)
        narrow = lax.dot_general(incoming, phi[...], NT, preferred_element_type=F32)
        out[...] = narrow.astype(BF16).reshape(out.shape)


def place_body(*refs):
    count = len(refs) // 2
    for low, out in zip(refs[:count], refs[count:], strict=True):
        out[...] = low[...].astype(F32)


def final_body(peers, parents, me, *refs):
    near = peers // 2
    ups, lows = refs[:near], refs[near : near + peers]
    trig, theta, mix, expand, out, rows_up, rows_low, turned, ready, sems = refs[near + peers :]
    children, rows = trig.shape[1], trig.shape[2]
    high_rows, low_rows = rows_up.shape[3], rows_low.shape[3]
    orders = expand.shape[0]
    boxes = parents * children
    for mask in range(peers):
        place = jnp.bitwise_xor(me[0], mask)
        for c in range(2):
            for b in range(parents):
                if mask < near:
                    piece = lows[mask][boxes + 2 * b + c]
                else:
                    piece = ups[mask - near][b, c * high_rows : (c + 1) * high_rows]
                rows_up[b, c, place] = piece.astype(F32)
            piece = lows[mask][0:boxes, c * low_rows : (c + 1) * low_rows]
            rows_low[:, c, place] = piece.astype(F32)
    copies = []
    for b in range(parents):
        coarse = []
        for c in range(2):
            full = rows_up[b, c].reshape(peers * high_rows, 128).astype(BF16)
            coarse.append(jnp.dot(theta[...], full, preferred_element_type=F32))
        for k in range(children):
            cosine, sine = trig[0, k], trig[1, k]
            box = b * children + k
            real = coarse[0] * cosine - coarse[1] * sine + rows_low[box, 0].reshape(rows, 128)
            imag = coarse[0] * sine + coarse[1] * cosine + rows_low[box, 1].reshape(rows, 128)
            pattern = jnp.concatenate([real.astype(BF16), imag.astype(BF16)], axis=1)
            half = jnp.dot(expand[...], pattern, preferred_element_type=F32)
            high = half.astype(BF16)
            turned[k * orders : (k + 1) * orders] = high
            low = (half - high.astype(F32)).astype(BF16)
            turned[(children + k) * orders : (children + k + 1) * orders] = low
        both = lax.dot_general(turned[...], mix[...], NT, preferred_element_type=F32)
        size = children * orders
        result = both[:size] + both[size:]
        start = b * 2 * size
        ready[pl.ds(start, size, stride=2)] = result[:, :128]
        ready[pl.ds(start + 1, size, stride=2)] = result[:, 128:]
        span = pl.ds(start, 2 * size)
        copies += fetch([(ready.at[span], out.at[span])], sems.at[pl.ds(b, 1)])
    for copy in copies:
        copy.wait()


def struct(shape, dtype):
    return jax.ShapeDtypeStruct(shape, dtype)


def per_device(
    top_patterns,
    theta_upper,
    phi_upper,
    angles_upper,
    table_upper,
    outgoing_upper,
    list_upper,
    offset_upper,
    theta_lower,
    phi_lower,
    angles_lower,
    table_lower,
    outgoing_lower,
    list_lower,
    offset_lower,
    switch_theta,
    switch_phi,
):
    peers = lax.axis_size("angle")
    home = lax.axis_index("box")
    me = lax.axis_index("angle").astype(jnp.int32).reshape(1)
    far_mask = lax.axis_size("box") // 2
    boxes, _, low, lanes = outgoing_lower.shape
    per = boxes // peers
    entries = list_lower.shape[1]
    upper_boxes, _, rows, wide = outgoing_upper.shape
    upper_per = upper_boxes // peers

    other = list_lower.T // boxes != home
    spot = list_lower.T % boxes
    ask_code = (jnp.where(other, spot, boxes) << SHIFT) + offset_lower.T
    own_code = (jnp.where(other, boxes, spot) << SHIFT) + offset_lower.T
    far_code = swap(ask_code, "box", 1)
    far_upper = swap(outgoing_upper, "box", far_mask)

    places = table_lower.shape[0]
    outer, inner = list(range(peers - 1, peers // 2 - 1, -1)), list(range(peers // 2 - 1, -1, -1))

    def sums(groups, outs, codes, order, name):
        return kernel_call(
            functools.partial(sums_body, groups, per, entries),
            outs,
            [order, *codes],
            [table, source],
            name,
        )

    own_shape = struct((per, 2 * low, lanes), F32)
    *first, table, source = kernel_call(
        functools.partial(first_body, [((mask,), 0) for mask in outer], per, entries),
        [
            *[struct((per, 2 * low, lanes), BF16)] * len(outer),
            struct((places, 2 * low, lanes), F32),
            struct((boxes + 1, 2 * low, lanes), F32),
        ],
        [me, far_code],
        [table_lower.reshape(-1, 2 * low, lanes), outgoing_lower.reshape(-1, 2 * low, lanes)],
        "sums_first",
        scratch=[
            pltpu.VMEM((places, 2 * low, lanes), BF16),
            pltpu.VMEM((boxes, 2 * low, lanes), BF16),
            pltpu.VMEM((places, 2 * low, lanes), F32),
            pltpu.VMEM((boxes + 1, 2 * low, lanes), F32),
            pltpu.SemaphoreType.DMA((5,)),
            pltpu.SemaphoreType.DMA((2,)),
        ],
        held=2,
        away=2,
        vmem=53 << 20,
    )
    got_outer = [swap(value, "box", 1) for value in first]

    children = angles_lower.shape[0]
    part_rows = 4 * rows + children * low // 2
    held = top_patterns.shape[2]
    top = top_patterns.reshape(4 * held, -1)
    parts = kernel_call(
        functools.partial(early_body, peers, rows),
        [struct((part_rows, wide), F32)] * peers,
        [after(me, first[0])],
        [top, theta_upper, phi_upper, angles_lower],
        "early",
        scratch=[
            pltpu.VMEM((4, peers, held, wide), F32),
            pltpu.VMEM((4, peers, rows, wide), F32),
            *(pltpu.VMEM(a.shape, a.dtype) for a in (top, theta_upper, phi_upper, angles_lower)),
            pltpu.SemaphoreType.DMA((4,)),
        ],
        held=4,
    )
    order = after(me, parts[0])
    parts = [swap(part, "angle", mask) if mask in outer else part for mask, part in enumerate(parts)]
    own_outer = sums(
        [((mask,), 0) for mask in outer],
        [own_shape] * len(outer),
        [own_code],
        order,
        "sums_third",
    )
    lows = {}
    for mask, own, got in list(zip(outer, own_outer, got_outer, strict=True))[: len(outer) // 2]:
        (lows[mask],) = join([own], got)
    second = sums(
        [((mask,), 0) for mask in inner],
        [struct((per, 2 * low, lanes), BF16)] * len(inner),
        [far_code],
        after(me, lows[outer[0]]),
        "sums_second",
    )
    got_inner = {mask: swap(value, "box", 1) for mask, value in zip(inner, second, strict=True)}
    late = after(parts[1], second[0])
    parts = [parts[0]] + [swap(late if mask == 1 else parts[mask], "angle", mask) for mask in inner[-2::-1]] + [*parts[len(inner) :]]
    orders = switch_theta.shape[0]
    azimuths = switch_phi.shape[1]
    shifted, trig, mix, theta_low, theta_switch = kernel_call(
        functools.partial(shift_body, peers, rows, low),
        [
            struct((upper_boxes, 2, rows, wide), F32),
            struct((2, children, peers, low, lanes), F32),
            struct((2 * azimuths, 2 * azimuths), BF16),
            struct(theta_lower.shape, BF16),
            struct(switch_theta.shape, BF16),
        ],
        [after(me, second[0])],
        [*parts, angles_upper, switch_phi, theta_lower, switch_theta],
        "shift",
        scratch=[
            *(pltpu.VMEM(a.shape, a.dtype) for a in (angles_upper, switch_phi, theta_lower, switch_theta)),
            pltpu.SemaphoreType.DMA((4,)),
        ],
        held=4,
    )
    for mask, own, got in list(zip(outer, own_outer, got_outer, strict=True))[len(outer) // 2 :]:
        (lows[mask],) = join([after(own, trig)], got)
    trig = trig.reshape(2, children, peers * low, lanes)
    ups = kernel_call(
        functools.partial(upper_body, outer + inner, peers, entries),
        [struct((upper_per, 2 * rows, lanes), BF16)] * peers,
        [after(me, lows[outer[-1]]), home.astype(jnp.int32).reshape(1), list_upper, offset_upper],
        [outgoing_upper, far_upper, table_upper, shifted, phi_lower],
        "upper",
        scratch=[
            pltpu.VMEM((2 * upper_boxes, 2, rows, wide), F32),
            pltpu.VMEM((upper_boxes, 2 * rows, wide), BF16),
        ],
    )
    ups = dict(zip(outer + inner, ups, strict=True))
    order = after(me, ups[0])
    behind = {mask: ups.pop(mask).reshape(-1, 2 * low, lanes) for mask in inner}
    for masks, name in ((inner[:-1], "close_peers"), (inner[-1:], "close_self")):
        close = kernel_call(
            functools.partial(close_body, masks, per, entries),
            [struct((per + behind[0].shape[0], 2 * low, lanes), BF16)] * len(masks),
            [order, own_code],
            [table, source, *(got_inner[mask] for mask in masks), *(behind[mask] for mask in masks)],
            name,
        )
        lows.update(zip(masks, close, strict=True))
        order = after(me, close[0])
    ups = [swap(ups[mask], "angle", mask) for mask in reversed(outer)]
    lows = [swap(lows[mask], "angle", mask) if mask else lows[mask] for mask in range(peers)]

    arrived = kernel_call(
        place_body,
        [struct(lows[mask].shape, F32) for mask in outer],
        [],
        [lows[mask] for mask in outer],
        "place",
    )
    lows = [*lows[: len(inner)], *reversed(arrived)]
    (out,) = kernel_call(
        functools.partial(final_body, peers, upper_per),
        [struct((per * 2 * orders, azimuths), F32)],
        [me],
        [*ups, *lows, trig, theta_low, mix, theta_switch],
        "expand",
        scratch=[
            pltpu.VMEM((upper_per, 2, peers, rows, lanes), F32),
            pltpu.VMEM((per, 2, peers, low, lanes), F32),
            pltpu.VMEM((2 * children * orders, 2 * lanes), BF16),
            pltpu.VMEM((per * 2 * orders + 8, azimuths), F32),
            pltpu.SemaphoreType.DMA((upper_per,)),
        ],
        away=1,
        vmem=12 << 20,
    )
    out = out.reshape(per, orders, 2, azimuths)
    return jnp.transpose(out, (0, 2, 1, 3)).reshape(per, 2, orders * azimuths)


def solution(mesh):
    return jax.shard_map(
        per_device,
        mesh=mesh,
        in_specs=(
            P("box", None, "angle", None),
            P(),
            P(),
            P(None, "angle", None),
            P(None, None, "angle", None),
            P("box", None, "angle", None),
            P("box", None),
            P("box", None),
            P(),
            P(),
            P(None, "angle", None),
            P(None, None, "angle", None),
            P("box", None, "angle", None),
            P("box", None),
            P("box", None),
            P(),
            P(),
        ),
        out_specs=P(("box", "angle"), None, None),
        check_vma=False,
    )
```

```python
import functools

import jax
import jax.numpy as jnp
from jax import lax
from jax.experimental import pallas as pl
from jax.experimental.pallas import tpu as pltpu
from jax.sharding import PartitionSpec as P

F32, BF16 = jnp.float32, jnp.bfloat16
VM = pl.BlockSpec(memory_space=pltpu.VMEM)
SM = pl.BlockSpec(memory_space=pltpu.SMEM)
HB = pl.BlockSpec(memory_space=pltpu.HBM)
SHIFT = 9
NT = (((1,), (1,)), ((), ()))


def swap(value, axis, mask):
    pairs = [(source, source ^ mask) for source in range(lax.axis_size(axis))]
    return lax.ppermute(value, axis, pairs)


COSTS = {"join": 0, "sums_third": 0, "shift": 0, "close_self": 0}


def after(value, *others):
    return lax.optimization_barrier((value, *others))[0]


def kernel_call(body, outs, scalars, arrays, name, scratch=(), held=0, vmem=6 << 20, away=0):
    near = len(arrays) - held
    return pl.pallas_call(
        body,
        out_shape=outs,
        in_specs=[SM] * len(scalars) + [VM] * near + [HB] * held,
        out_specs=[VM] * (len(outs) - away) + [HB] * away,
        scratch_shapes=list(scratch),
        compiler_params=pltpu.CompilerParams(vmem_limit_bytes=vmem),
        cost_estimate=pl.CostEstimate(flops=COSTS.get(name, 4) << 30, bytes_accessed=1, transcendentals=0),
        name=name,
    )(*scalars, *arrays)


def fetch(pairs, sems):
    copies = [pltpu.make_async_copy(a, b, sems.at[k]) for k, (a, b) in enumerate(pairs)]
    for copy in copies:
        copy.start()
    return copies


def split_dot(left, value, dims):
    high = value.astype(BF16)
    low = (value - high.astype(F32)).astype(BF16)
    return lax.dot_general(left, high, dims, preferred_element_type=F32) + lax.dot_general(
        left, low, dims, preferred_element_type=F32
    )


def box_sum(box, entries, code, table, source):
    rows = table.shape[1] // 2
    real = imag = None
    for entry in range(entries):
        word = code[entry, box]
        factor = table[word & ((1 << SHIFT) - 1)]
        value = source[word >> SHIFT]
        fr, fi, sr, si = factor[:rows], factor[rows:], value[:rows], value[rows:]
        re, im = fr * sr - fi * si, fr * si + fi * sr
        real = re if real is None else real + re
        imag = im if imag is None else imag + im
    return real, imag


def sums_body(groups, per, entries, me, *refs):
    codes = max(which for _, which in groups) + 1
    code_refs, (table, source), outs = refs[:codes], refs[codes : codes + 2], refs[codes + 2 :]
    rows = table.shape[1] // 2
    for (masks, which), out in zip(groups, outs, strict=True):
        for place, mask in enumerate(masks):
            first = jnp.bitwise_xor(me[0], mask) * per

            def one(i, carry, first=first, place=place, which=which, out=out):
                real, imag = box_sum(first + i, entries, code_refs[which], table, source)
                out[place * per + i, 0:rows] = real.astype(out.dtype)
                out[place * per + i, rows:] = imag.astype(out.dtype)
                return carry

            lax.fori_loop(0, per, one, 0, unroll=2)


def first_body(groups, per, entries, me, code, table, source, *refs):
    outs = refs[: len(groups)]
    table_out, source_out, table_in, source_in, wide_table, wide_source, sems, back = refs[len(groups) :]
    count, total = source.shape[0], table.shape[0]
    step = -(-total // 4)
    spans = [(k, min(k + step, total)) for k in range(0, total, step)]
    pairs = [(source, source_in)]
    pairs += [(table.at[lo:hi], table_in.at[lo:hi]) for lo, hi in spans]
    copies = fetch(pairs, sems)
    copies[0].wait()
    wide_source[0:count] = source_in[...].astype(F32)
    wide_source[count] = jnp.zeros(source.shape[1:], F32)
    for copy, (lo, hi) in zip(copies[1:], spans, strict=True):
        copy.wait()
        wide_table[lo:hi] = table_in[lo:hi].astype(F32)
    copies = fetch([(wide_table, table_out), (wide_source, source_out)], back)
    sums_body(groups, per, entries, me, code, wide_table, wide_source, *outs)
    for copy in copies:
        copy.wait()


def early_body(peers, rows, me, *refs):
    near, outs = refs[:4], refs[4 : 4 + peers]
    padded, summed, top, theta, phi, angles, sems = refs[4 + peers :]
    held = top.shape[0] // 4
    for copy in fetch(list(zip(near, (top, theta, phi, angles), strict=True)), sems):
        copy.wait()
    narrowed = lax.dot_general(top[...], phi[...], NT, preferred_element_type=F32)
    padded[...] = jnp.zeros(padded.shape, F32)
    for k in range(4):
        padded[k, me[0]] = narrowed[k * held : (k + 1) * held]
    for k in range(4):
        full = padded[k].reshape(peers * held, narrowed.shape[1])
        part = split_dot(theta[...], full, (((1,), (0,)), ((), ())))
        summed[k] = part.reshape(peers, rows, narrowed.shape[1])
    low = angles.shape[1]
    half = angles.shape[0] // 2
    for mask, out in enumerate(outs):
        for k in range(4):
            out[k * rows : (k + 1) * rows] = summed[k, jnp.bitwise_xor(me[0], mask)]
        for c in range(half):
            start = 4 * rows + c * low
            out[start : start + low, 0:128] = angles[c]
            out[start : start + low, 128:256] = angles[half + c]


def shift_body(peers, rows, low, me, *refs):
    parts, near = refs[:peers], refs[peers : peers + 4]
    shifted, trig, mix, low_out, switch_out, angles, phi, theta, switch, sems = refs[peers + 4 :]
    for copy in fetch(list(zip(near, (angles, phi, theta, switch), strict=True)), sems):
        copy.wait()
    low_out[...] = theta[...]
    switch_out[...] = switch[...]
    size = phi.shape[1]
    mix[0:size, 0:size] = phi[0]
    mix[0:size, size:] = -phi[1]
    mix[size:, 0:size] = phi[1]
    mix[size:, size:] = phi[0]
    children = angles.shape[0]
    half = children // 2
    for c in range(children):
        cosine, sine = jnp.cos(angles[c]), jnp.sin(angles[c])
        for b in range(2):
            re = parts[0][2 * b * rows : (2 * b + 1) * rows]
            im = parts[0][(2 * b + 1) * rows : (2 * b + 2) * rows]
            for part in parts[1:]:
                re = re + part[2 * b * rows : (2 * b + 1) * rows]
                im = im + part[(2 * b + 1) * rows : (2 * b + 2) * rows]
            shifted[b * children + c, 0] = re * cosine - im * sine
            shifted[b * children + c, 1] = re * sine + im * cosine
    for mask, part in enumerate(parts):
        for c in range(half):
            start = 4 * rows + c * low
            for side in range(2):
                angle = part[start : start + low, side * 128 : side * 128 + 128]
                place = jnp.bitwise_xor(me[0], mask)
                trig[0, side * half + c, place] = jnp.cos(angle)
                trig[1, side * half + c, place] = jnp.sin(angle)


def join(owns, got, extras=()):
    count, more = len(owns), len(extras)
    behind = [extras[k].shape[0] if extras else 0 for k in range(count)]

    def body(*refs):
        first = 0
        for k, (own, out) in enumerate(zip(refs[:count], refs[count + 1 + more :], strict=True)):
            size = own.shape[0]
            out[0:size] = (own[...] + refs[count][first : first + size].astype(F32)).astype(BF16)
            if extras:
                out[size:] = refs[count + 1 + k][...]
            first += size

    shapes = [struct((a.shape[0] + n, *a.shape[1:]), BF16) for a, n in zip(owns, behind, strict=True)]
    return kernel_call(body, shapes, [], [*owns, got, *extras], "join")


def close_body(masks, firsts, per, entries, me, code, table, source, got, *refs):
    count = len(masks)
    rows = table.shape[1] // 2
    for mask, begin, piece, out in zip(masks, firsts, refs[:count], refs[count:], strict=True):
        first = jnp.bitwise_xor(me[0], mask) * per

        def one(i, carry, first=first, begin=begin, out=out):
            real, imag = box_sum(first + i, entries, code, table, source)
            real = real + got[begin + i, 0:rows].astype(F32)
            imag = imag + got[begin + i, rows:].astype(F32)
            out[i, 0:rows] = real.astype(BF16)
            out[i, rows:] = imag.astype(BF16)
            return carry

        lax.fori_loop(0, per, one, 0, unroll=2)
        out[per:] = piece[...]


def upper_body(masks, peers, entries, me, home, ids, offsets, own, far, table, shifted, phi, *refs):
    outs, (pool, rounded) = refs[: len(masks)], refs[len(masks) :]
    boxes, _, rows, wide = own.shape
    pool[0:boxes] = own[...].astype(F32)
    pool[boxes:] = far[...].astype(F32)
    spans = [slice(r, r + 8) for r in range(0, rows, 8)]
    per = boxes // peers
    for turn, mask in enumerate(masks):
        first = jnp.bitwise_xor(me[0], mask) * per

        def one(i, carry, first=first, turn=turn):
            box = first + i
            real = [shifted[box, 0, span] for span in spans]
            imag = [shifted[box, 1, span] for span in spans]
            for entry in range(entries):
                offset, ident = offsets[box, entry], ids[box, entry]
                if boxes & (boxes - 1):
                    place = lax.rem(ident, boxes)
                else:
                    place = ident & (boxes - 1)
                place = jnp.where(ident - place == home[0] * boxes, place, place + boxes)
                for k, span in enumerate(spans):
                    fr, fi = table[offset, 0, span].astype(F32), table[offset, 1, span].astype(F32)
                    sr, si = pool[place, 0, span], pool[place, 1, span]
                    real[k] = real[k] + (fr * sr - fi * si)
                    imag[k] = imag[k] + (fr * si + fi * sr)
            rounded[turn * per + i] = jnp.concatenate([*real, *imag], axis=0).astype(BF16)
            return carry

        lax.fori_loop(0, per, one, 0)
    for turn, out in enumerate(outs):
        incoming = rounded[turn * per : (turn + 1) * per].reshape(per * 2 * rows, wide)
        narrow = lax.dot_general(incoming, phi[...], NT, preferred_element_type=F32)
        out[...] = narrow.astype(BF16).reshape(out.shape)


def place_body(*refs):
    count = len(refs) // 2
    for low, out in zip(refs[:count], refs[count:], strict=True):
        out[...] = low[...].astype(F32)


def final_body(peers, parents, me, *refs):
    near = peers // 2
    ups, lows = refs[:near], refs[near : near + peers]
    trig, theta, mix, expand, out, rows_up, rows_low, turned, ready, sems = refs[near + peers :]
    children, rows = trig.shape[1], trig.shape[2]
    high_rows, low_rows = rows_up.shape[3], rows_low.shape[3]
    orders = expand.shape[0]
    boxes = parents * children
    for mask in range(peers):
        place = jnp.bitwise_xor(me[0], mask)
        for c in range(2):
            for b in range(parents):
                if mask < near:
                    piece = lows[mask][boxes + 2 * b + c]
                else:
                    piece = ups[mask - near][b, c * high_rows : (c + 1) * high_rows]
                rows_up[b, c, place] = piece.astype(F32)
            piece = lows[mask][0:boxes, c * low_rows : (c + 1) * low_rows]
            rows_low[:, c, place] = piece.astype(F32)
    copies = []
    for b in range(parents):
        coarse = []
        for c in range(2):
            full = rows_up[b, c].reshape(peers * high_rows, 128).astype(BF16)
            coarse.append(jnp.dot(theta[...], full, preferred_element_type=F32))
        for k in range(children):
            cosine, sine = trig[0, k], trig[1, k]
            box = b * children + k
            real = coarse[0] * cosine - coarse[1] * sine + rows_low[box, 0].reshape(rows, 128)
            imag = coarse[0] * sine + coarse[1] * cosine + rows_low[box, 1].reshape(rows, 128)
            pattern = jnp.concatenate([real.astype(BF16), imag.astype(BF16)], axis=1)
            half = jnp.dot(expand[...], pattern, preferred_element_type=F32)
            high = half.astype(BF16)
            turned[k * orders : (k + 1) * orders] = high
            low = (half - high.astype(F32)).astype(BF16)
            turned[(children + k) * orders : (children + k + 1) * orders] = low
        both = lax.dot_general(turned[...], mix[...], NT, preferred_element_type=F32)
        size = children * orders
        result = both[:size] + both[size:]
        start = b * 2 * size
        ready[pl.ds(start, size, stride=2)] = result[:, :128]
        ready[pl.ds(start + 1, size, stride=2)] = result[:, 128:]
        span = pl.ds(start, 2 * size)
        copies += fetch([(ready.at[span], out.at[span])], sems.at[pl.ds(b, 1)])
    for copy in copies:
        copy.wait()


def struct(shape, dtype):
    return jax.ShapeDtypeStruct(shape, dtype)


def per_device(
    top_patterns,
    theta_upper,
    phi_upper,
    angles_upper,
    table_upper,
    outgoing_upper,
    list_upper,
    offset_upper,
    theta_lower,
    phi_lower,
    angles_lower,
    table_lower,
    outgoing_lower,
    list_lower,
    offset_lower,
    switch_theta,
    switch_phi,
):
    peers = lax.axis_size("angle")
    home = lax.axis_index("box")
    me = lax.axis_index("angle").astype(jnp.int32).reshape(1)
    far_mask = lax.axis_size("box") // 2
    boxes, _, low, lanes = outgoing_lower.shape
    per = boxes // peers
    entries = list_lower.shape[1]
    upper_boxes, _, rows, wide = outgoing_upper.shape
    upper_per = upper_boxes // peers

    other = list_lower.T // boxes != home
    spot = list_lower.T % boxes
    ask_code = (jnp.where(other, spot, boxes) << SHIFT) + offset_lower.T
    own_code = (jnp.where(other, boxes, spot) << SHIFT) + offset_lower.T
    far_code = swap(ask_code, "box", 1)
    far_upper = swap(outgoing_upper, "box", far_mask)

    places = table_lower.shape[0]
    outer, inner = list(range(peers - 1, peers // 2 - 1, -1)), list(range(peers // 2 - 1, -1, -1))

    def sums(groups, outs, codes, order, name):
        return kernel_call(
            functools.partial(sums_body, groups, per, entries),
            outs,
            [order, *codes],
            [table, source],
            name,
        )

    own_shape = struct((per, 2 * low, lanes), F32)
    far_shape = struct((len(outer) * per, 2 * low, lanes), BF16)
    *first, table, source = kernel_call(
        functools.partial(first_body, [((mask,), 0) for mask in outer], per, entries),
        [
            *[struct((per, 2 * low, lanes), BF16)] * len(outer),
            struct((places, 2 * low, lanes), F32),
            struct((boxes + 1, 2 * low, lanes), F32),
        ],
        [me, far_code],
        [table_lower.reshape(-1, 2 * low, lanes), outgoing_lower.reshape(-1, 2 * low, lanes)],
        "sums_first",
        scratch=[
            pltpu.VMEM((places, 2 * low, lanes), BF16),
            pltpu.VMEM((boxes, 2 * low, lanes), BF16),
            pltpu.VMEM((places, 2 * low, lanes), F32),
            pltpu.VMEM((boxes + 1, 2 * low, lanes), F32),
            pltpu.SemaphoreType.DMA((5,)),
            pltpu.SemaphoreType.DMA((2,)),
        ],
        held=2,
        away=2,
        vmem=53 << 20,
    )
    got_outer = [swap(value, "box", 1) for value in first]

    children = angles_lower.shape[0]
    part_rows = 4 * rows + children * low // 2
    held = top_patterns.shape[2]
    top = top_patterns.reshape(4 * held, -1)
    parts = kernel_call(
        functools.partial(early_body, peers, rows),
        [struct((part_rows, wide), F32)] * peers,
        [after(me, first[0])],
        [top, theta_upper, phi_upper, angles_lower],
        "early",
        scratch=[
            pltpu.VMEM((4, peers, held, wide), F32),
            pltpu.VMEM((4, peers, rows, wide), F32),
            *(pltpu.VMEM(a.shape, a.dtype) for a in (top, theta_upper, phi_upper, angles_lower)),
            pltpu.SemaphoreType.DMA((4,)),
        ],
        held=4,
    )
    order = after(me, parts[0])
    parts = [swap(part, "angle", mask) if mask in outer else part for mask, part in enumerate(parts)]
    own_outer = sums(
        [((mask,), 0) for mask in outer],
        [own_shape] * len(outer),
        [own_code],
        order,
        "sums_third",
    )
    lows = {}
    for mask, own, got in list(zip(outer, own_outer, got_outer, strict=True))[: len(outer) // 2]:
        (lows[mask],) = join([own], got)
    (second,) = sums([(tuple(inner), 0)], [far_shape], [far_code], after(me, lows[outer[0]]), "sums_second")
    got_inner = swap(second, "box", 1)
    late = after(parts[1], second)
    parts = [parts[0]] + [swap(late if mask == 1 else parts[mask], "angle", mask) for mask in inner[-2::-1]] + [*parts[len(inner) :]]
    orders = switch_theta.shape[0]
    azimuths = switch_phi.shape[1]
    shifted, trig, mix, theta_low, theta_switch = kernel_call(
        functools.partial(shift_body, peers, rows, low),
        [
            struct((upper_boxes, 2, rows, wide), F32),
            struct((2, children, peers, low, lanes), F32),
            struct((2 * azimuths, 2 * azimuths), BF16),
            struct(theta_lower.shape, BF16),
            struct(switch_theta.shape, BF16),
        ],
        [after(me, second)],
        [*parts, angles_upper, switch_phi, theta_lower, switch_theta],
        "shift",
        scratch=[
            *(pltpu.VMEM(a.shape, a.dtype) for a in (angles_upper, switch_phi, theta_lower, switch_theta)),
            pltpu.SemaphoreType.DMA((4,)),
        ],
        held=4,
    )
    for mask, own, got in list(zip(outer, own_outer, got_outer, strict=True))[len(outer) // 2 :]:
        (lows[mask],) = join([after(own, trig)], got)
    trig = trig.reshape(2, children, peers * low, lanes)
    ups = kernel_call(
        functools.partial(upper_body, outer + inner, peers, entries),
        [struct((upper_per, 2 * rows, lanes), BF16)] * peers,
        [after(me, lows[outer[-1]]), home.astype(jnp.int32).reshape(1), list_upper, offset_upper],
        [outgoing_upper, far_upper, table_upper, shifted, phi_lower],
        "upper",
        scratch=[
            pltpu.VMEM((2 * upper_boxes, 2, rows, wide), F32),
            pltpu.VMEM((upper_boxes, 2 * rows, wide), BF16),
        ],
    )
    ups = dict(zip(outer + inner, ups, strict=True))
    order = after(me, ups[0])
    behind = {mask: ups.pop(mask).reshape(-1, 2 * low, lanes) for mask in inner}
    own_inner = sums(
        [((mask,), 0) for mask in inner[:-1]],
        [own_shape] * (len(inner) - 1),
        [own_code],
        order,
        "sums_fourth",
    )
    close = join(own_inner, got_inner, [behind[mask] for mask in inner[:-1]])
    lows.update(zip(inner[:-1], close, strict=True))
    (lows[0],) = kernel_call(
        functools.partial(close_body, [0], [per * inner.index(0)], per, entries),
        [struct((per + behind[0].shape[0], 2 * low, lanes), BF16)],
        [after(me, close[0]), own_code],
        [table, source, got_inner, behind[0]],
        "close_self",
    )
    ups = [swap(ups[mask], "angle", mask) for mask in reversed(outer)]
    lows = [swap(lows[mask], "angle", mask) if mask else lows[mask] for mask in range(peers)]

    arrived = kernel_call(
        place_body,
        [struct(lows[mask].shape, F32) for mask in outer],
        [],
        [lows[mask] for mask in outer],
        "place",
    )
    lows = [*lows[: len(inner)], *reversed(arrived)]
    (out,) = kernel_call(
        functools.partial(final_body, peers, upper_per),
        [struct((per * 2 * orders, azimuths), F32)],
        [me],
        [*ups, *lows, trig, theta_low, mix, theta_switch],
        "expand",
        scratch=[
            pltpu.VMEM((upper_per, 2, peers, rows, lanes), F32),
            pltpu.VMEM((per, 2, peers, low, lanes), F32),
            pltpu.VMEM((2 * children * orders, 2 * lanes), BF16),
            pltpu.VMEM((per * 2 * orders + 8, azimuths), F32),
            pltpu.SemaphoreType.DMA((upper_per,)),
        ],
        away=1,
        vmem=12 << 20,
    )
    out = out.reshape(per, orders, 2, azimuths)
    return jnp.transpose(out, (0, 2, 1, 3)).reshape(per, 2, orders * azimuths)


def solution(mesh):
    return jax.shard_map(
        per_device,
        mesh=mesh,
        in_specs=(
            P("box", None, "angle", None),
            P(),
            P(),
            P(None, "angle", None),
            P(None, None, "angle", None),
            P("box", None, "angle", None),
            P("box", None),
            P("box", None),
            P(),
            P(),
            P(None, "angle", None),
            P(None, None, "angle", None),
            P("box", None, "angle", None),
            P("box", None),
            P("box", None),
            P(),
            P(),
        ),
        out_specs=P(("box", "angle"), None, None),
        check_vma=False,
    )
```

```python
import functools

import jax
import jax.numpy as jnp
from jax import lax
from jax.experimental import pallas as pl
from jax.experimental.pallas import tpu as pltpu
from jax.sharding import PartitionSpec as P

F32, BF16 = jnp.float32, jnp.bfloat16
VM = pl.BlockSpec(memory_space=pltpu.VMEM)
SM = pl.BlockSpec(memory_space=pltpu.SMEM)
HB = pl.BlockSpec(memory_space=pltpu.HBM)
SHIFT = 9
NT = (((1,), (1,)), ((), ()))


def swap(value, axis, mask):
    pairs = [(source, source ^ mask) for source in range(lax.axis_size(axis))]
    return lax.ppermute(value, axis, pairs)


COSTS = {"join": 0, "sums_third": 0, "shift": 0, "close_self": 0}


def after(value, *others):
    return lax.optimization_barrier((value, *others))[0]


def kernel_call(body, outs, scalars, arrays, name, scratch=(), held=0, vmem=6 << 20, away=0):
    near = len(arrays) - held
    return pl.pallas_call(
        body,
        out_shape=outs,
        in_specs=[SM] * len(scalars) + [VM] * near + [HB] * held,
        out_specs=[VM] * (len(outs) - away) + [HB] * away,
        scratch_shapes=list(scratch),
        compiler_params=pltpu.CompilerParams(vmem_limit_bytes=vmem),
        cost_estimate=pl.CostEstimate(flops=COSTS.get(name, 4) << 30, bytes_accessed=1, transcendentals=0),
        name=name,
    )(*scalars, *arrays)


def fetch(pairs, sems):
    copies = [pltpu.make_async_copy(a, b, sems.at[k]) for k, (a, b) in enumerate(pairs)]
    for copy in copies:
        copy.start()
    return copies


def split_dot(left, value, dims):
    high = value.astype(BF16)
    low = (value - high.astype(F32)).astype(BF16)
    return lax.dot_general(left, high, dims, preferred_element_type=F32) + lax.dot_general(
        left, low, dims, preferred_element_type=F32
    )


def box_sum(box, entries, code, table, source):
    rows = table.shape[1] // 2
    real = imag = None
    for entry in range(entries):
        word = code[entry, box]
        factor = table[word & ((1 << SHIFT) - 1)]
        value = source[word >> SHIFT]
        fr, fi, sr, si = factor[:rows], factor[rows:], value[:rows], value[rows:]
        re, im = fr * sr - fi * si, fr * si + fi * sr
        real = re if real is None else real + re
        imag = im if imag is None else imag + im
    return real, imag


def sums_body(groups, per, entries, me, *refs):
    codes = max(which for _, which in groups) + 1
    code_refs, (table, source), outs = refs[:codes], refs[codes : codes + 2], refs[codes + 2 :]
    rows = table.shape[1] // 2
    for (masks, which), out in zip(groups, outs, strict=True):
        for place, mask in enumerate(masks):
            first = jnp.bitwise_xor(me[0], mask) * per

            def one(i, carry, first=first, place=place, which=which, out=out):
                real, imag = box_sum(first + i, entries, code_refs[which], table, source)
                out[place * per + i, 0:rows] = real.astype(out.dtype)
                out[place * per + i, rows:] = imag.astype(out.dtype)
                return carry

            lax.fori_loop(0, per, one, 0, unroll=2)


def first_body(groups, per, entries, me, code, table, source, *refs):
    outs = refs[: len(groups)]
    table_out, source_out, table_in, source_in, wide_table, wide_source, sems, back = refs[len(groups) :]
    count, total = source.shape[0], table.shape[0]
    step = -(-total // 4)
    spans = [(k, min(k + step, total)) for k in range(0, total, step)]
    pairs = [(source, source_in)]
    pairs += [(table.at[lo:hi], table_in.at[lo:hi]) for lo, hi in spans]
    copies = fetch(pairs, sems)
    copies[0].wait()
    wide_source[0:count] = source_in[...].astype(F32)
    wide_source[count] = jnp.zeros(source.shape[1:], F32)
    for copy, (lo, hi) in zip(copies[1:], spans, strict=True):
        copy.wait()
        wide_table[lo:hi] = table_in[lo:hi].astype(F32)
    copies = fetch([(wide_table, table_out), (wide_source, source_out)], back)
    sums_body(groups, per, entries, me, code, wide_table, wide_source, *outs)
    for copy in copies:
        copy.wait()


def early_body(peers, rows, me, *refs):
    near, outs = refs[:4], refs[4 : 4 + peers]
    padded, summed, top, theta, phi, angles, sems = refs[4 + peers :]
    held = top.shape[0] // 4
    for copy in fetch(list(zip(near, (top, theta, phi, angles), strict=True)), sems):
        copy.wait()
    narrowed = lax.dot_general(top[...], phi[...], NT, preferred_element_type=F32)
    padded[...] = jnp.zeros(padded.shape, F32)
    for k in range(4):
        padded[k, me[0]] = narrowed[k * held : (k + 1) * held]
    for k in range(4):
        full = padded[k].reshape(peers * held, narrowed.shape[1])
        part = split_dot(theta[...], full, (((1,), (0,)), ((), ())))
        summed[k] = part.reshape(peers, rows, narrowed.shape[1])
    low = angles.shape[1]
    half = angles.shape[0] // 2
    for mask, out in enumerate(outs):
        for k in range(4):
            out[k * rows : (k + 1) * rows] = summed[k, jnp.bitwise_xor(me[0], mask)]
        for c in range(half):
            start = 4 * rows + c * low
            out[start : start + low, 0:128] = angles[c]
            out[start : start + low, 128:256] = angles[half + c]


def shift_body(peers, rows, low, me, *refs):
    parts, near = refs[:peers], refs[peers : peers + 4]
    shifted, trig, mix, low_out, switch_out, angles, phi, theta, switch, sems = refs[peers + 4 :]
    for copy in fetch(list(zip(near, (angles, phi, theta, switch), strict=True)), sems):
        copy.wait()
    low_out[...] = theta[...]
    switch_out[...] = switch[...]
    size = phi.shape[1]
    mix[0:size, 0:size] = phi[0]
    mix[0:size, size:] = -phi[1]
    mix[size:, 0:size] = phi[1]
    mix[size:, size:] = phi[0]
    children = angles.shape[0]
    half = children // 2
    for c in range(children):
        cosine, sine = jnp.cos(angles[c]), jnp.sin(angles[c])
        for b in range(2):
            re = parts[0][2 * b * rows : (2 * b + 1) * rows]
            im = parts[0][(2 * b + 1) * rows : (2 * b + 2) * rows]
            for part in parts[1:]:
                re = re + part[2 * b * rows : (2 * b + 1) * rows]
                im = im + part[(2 * b + 1) * rows : (2 * b + 2) * rows]
            shifted[b * children + c, 0] = re * cosine - im * sine
            shifted[b * children + c, 1] = re * sine + im * cosine
    for mask, part in enumerate(parts):
        for c in range(half):
            start = 4 * rows + c * low
            for side in range(2):
                angle = part[start : start + low, side * 128 : side * 128 + 128]
                place = jnp.bitwise_xor(me[0], mask)
                trig[0, side * half + c, place] = jnp.cos(angle)
                trig[1, side * half + c, place] = jnp.sin(angle)


def join(owns, got, extras=()):
    count, more = len(owns), len(extras)
    behind = [extras[k].shape[0] if extras else 0 for k in range(count)]

    def body(*refs):
        first = 0
        for k, (own, out) in enumerate(zip(refs[:count], refs[count + 1 + more :], strict=True)):
            size = own.shape[0]
            out[0:size] = (own[...] + refs[count][first : first + size].astype(F32)).astype(BF16)
            if extras:
                out[size:] = refs[count + 1 + k][...]
            first += size

    shapes = [struct((a.shape[0] + n, *a.shape[1:]), BF16) for a, n in zip(owns, behind, strict=True)]
    return kernel_call(body, shapes, [], [*owns, got, *extras], "join")


def close_body(masks, firsts, per, entries, me, code, table, source, got, *refs):
    count = len(masks)
    rows = table.shape[1] // 2
    for mask, begin, piece, out in zip(masks, firsts, refs[:count], refs[count:], strict=True):
        first = jnp.bitwise_xor(me[0], mask) * per

        def one(i, carry, first=first, begin=begin, out=out):
            real, imag = box_sum(first + i, entries, code, table, source)
            real = real + got[begin + i, 0:rows].astype(F32)
            imag = imag + got[begin + i, rows:].astype(F32)
            out[i, 0:rows] = real.astype(BF16)
            out[i, rows:] = imag.astype(BF16)
            return carry

        lax.fori_loop(0, per, one, 0, unroll=2)
        out[per:] = piece[...]


def upper_body(masks, peers, entries, me, home, ids, offsets, own, far, table, shifted, phi, *refs):
    outs, (pool, rounded) = refs[: len(masks)], refs[len(masks) :]
    boxes, _, rows, wide = own.shape
    pool[0:boxes] = own[...].astype(F32)
    pool[boxes:] = far[...].astype(F32)
    spans = [slice(r, r + 8) for r in range(0, rows, 8)]
    per = boxes // peers
    for turn, mask in enumerate(masks):
        first = jnp.bitwise_xor(me[0], mask) * per

        def one(i, carry, first=first, turn=turn):
            box = first + i
            real = [shifted[box, 0, span] for span in spans]
            imag = [shifted[box, 1, span] for span in spans]
            for entry in range(entries):
                offset, ident = offsets[box, entry], ids[box, entry]
                if boxes & (boxes - 1):
                    place = lax.rem(ident, boxes)
                else:
                    place = ident & (boxes - 1)
                place = jnp.where(ident - place == home[0] * boxes, place, place + boxes)
                for k, span in enumerate(spans):
                    fr, fi = table[offset, 0, span].astype(F32), table[offset, 1, span].astype(F32)
                    sr, si = pool[place, 0, span], pool[place, 1, span]
                    real[k] = real[k] + (fr * sr - fi * si)
                    imag[k] = imag[k] + (fr * si + fi * sr)
            rounded[turn * per + i] = jnp.concatenate([*real, *imag], axis=0).astype(BF16)
            return carry

        lax.fori_loop(0, per, one, 0)
    for turn, out in enumerate(outs):
        incoming = rounded[turn * per : (turn + 1) * per].reshape(per * 2 * rows, wide)
        narrow = lax.dot_general(incoming, phi[...], NT, preferred_element_type=F32)
        out[...] = narrow.astype(BF16).reshape(out.shape)


def place_body(*refs):
    count = len(refs) // 2
    for low, out in zip(refs[:count], refs[count:], strict=True):
        out[...] = low[...].astype(F32)


def final_body(peers, parents, me, *refs):
    near = peers // 2
    ups, lows = refs[:near], refs[near : near + peers]
    trig, theta, mix, expand, out, rows_up, rows_low, turned, ready, sems = refs[near + peers :]
    children, rows = trig.shape[1], trig.shape[2]
    high_rows, low_rows = rows_up.shape[3], rows_low.shape[3]
    orders = expand.shape[0]
    boxes = parents * children
    for mask in range(peers):
        place = jnp.bitwise_xor(me[0], mask)
        for c in range(2):
            for b in range(parents):
                if mask < near:
                    piece = lows[mask][boxes + 2 * b + c]
                else:
                    piece = ups[mask - near][b, c * high_rows : (c + 1) * high_rows]
                rows_up[b, c, place] = piece.astype(F32)
            piece = lows[mask][0:boxes, c * low_rows : (c + 1) * low_rows]
            rows_low[:, c, place] = piece.astype(F32)
    copies = []
    for b in range(parents):
        coarse = []
        for c in range(2):
            full = rows_up[b, c].reshape(peers * high_rows, 128).astype(BF16)
            coarse.append(jnp.dot(theta[...], full, preferred_element_type=F32))
        for k in range(children):
            cosine, sine = trig[0, k], trig[1, k]
            box = b * children + k
            real = coarse[0] * cosine - coarse[1] * sine + rows_low[box, 0].reshape(rows, 128)
            imag = coarse[0] * sine + coarse[1] * cosine + rows_low[box, 1].reshape(rows, 128)
            pattern = jnp.concatenate([real.astype(BF16), imag.astype(BF16)], axis=1)
            half = jnp.dot(expand[...], pattern, preferred_element_type=F32)
            high = half.astype(BF16)
            turned[k * orders : (k + 1) * orders] = high
            low = (half - high.astype(F32)).astype(BF16)
            turned[(children + k) * orders : (children + k + 1) * orders] = low
        both = lax.dot_general(turned[...], mix[...], NT, preferred_element_type=F32)
        size = children * orders
        result = both[:size] + both[size:]
        start = b * 2 * size
        ready[pl.ds(start, size, stride=2)] = result[:, :128]
        ready[pl.ds(start + 1, size, stride=2)] = result[:, 128:]
        span = pl.ds(start, 2 * size)
        copies += fetch([(ready.at[span], out.at[span])], sems.at[pl.ds(b, 1)])
    for copy in copies:
        copy.wait()


def struct(shape, dtype):
    return jax.ShapeDtypeStruct(shape, dtype)


def per_device(
    top_patterns,
    theta_upper,
    phi_upper,
    angles_upper,
    table_upper,
    outgoing_upper,
    list_upper,
    offset_upper,
    theta_lower,
    phi_lower,
    angles_lower,
    table_lower,
    outgoing_lower,
    list_lower,
    offset_lower,
    switch_theta,
    switch_phi,
):
    peers = lax.axis_size("angle")
    home = lax.axis_index("box")
    me = lax.axis_index("angle").astype(jnp.int32).reshape(1)
    far_mask = lax.axis_size("box") // 2
    boxes, _, low, lanes = outgoing_lower.shape
    per = boxes // peers
    entries = list_lower.shape[1]
    upper_boxes, _, rows, wide = outgoing_upper.shape
    upper_per = upper_boxes // peers

    other = list_lower.T // boxes != home
    spot = list_lower.T % boxes
    ask_code = (jnp.where(other, spot, boxes) << SHIFT) + offset_lower.T
    own_code = (jnp.where(other, boxes, spot) << SHIFT) + offset_lower.T
    far_code = swap(ask_code, "box", 1)
    far_upper = swap(outgoing_upper, "box", far_mask)

    places = table_lower.shape[0]
    outer, inner = list(range(peers - 1, peers // 2 - 1, -1)), list(range(peers // 2 - 1, -1, -1))

    def sums(groups, outs, codes, order, name):
        return kernel_call(
            functools.partial(sums_body, groups, per, entries),
            outs,
            [order, *codes],
            [table, source],
            name,
        )

    own_shape = struct((per, 2 * low, lanes), F32)
    far_shape = struct((len(outer) * per, 2 * low, lanes), BF16)
    *first, table, source = kernel_call(
        functools.partial(first_body, [((mask,), 0) for mask in outer], per, entries),
        [
            *[struct((per, 2 * low, lanes), BF16)] * len(outer),
            struct((places, 2 * low, lanes), F32),
            struct((boxes + 1, 2 * low, lanes), F32),
        ],
        [me, far_code],
        [table_lower.reshape(-1, 2 * low, lanes), outgoing_lower.reshape(-1, 2 * low, lanes)],
        "sums_first",
        scratch=[
            pltpu.VMEM((places, 2 * low, lanes), BF16),
            pltpu.VMEM((boxes, 2 * low, lanes), BF16),
            pltpu.VMEM((places, 2 * low, lanes), F32),
            pltpu.VMEM((boxes + 1, 2 * low, lanes), F32),
            pltpu.SemaphoreType.DMA((5,)),
            pltpu.SemaphoreType.DMA((2,)),
        ],
        held=2,
        away=2,
        vmem=53 << 20,
    )
    got_outer = [swap(value, "box", 1) for value in first]

    children = angles_lower.shape[0]
    part_rows = 4 * rows + children * low // 2
    held = top_patterns.shape[2]
    top = top_patterns.reshape(4 * held, -1)
    parts = kernel_call(
        functools.partial(early_body, peers, rows),
        [struct((part_rows, wide), F32)] * peers,
        [after(me, first[0])],
        [top, theta_upper, phi_upper, angles_lower],
        "early",
        scratch=[
            pltpu.VMEM((4, peers, held, wide), F32),
            pltpu.VMEM((4, peers, rows, wide), F32),
            *(pltpu.VMEM(a.shape, a.dtype) for a in (top, theta_upper, phi_upper, angles_lower)),
            pltpu.SemaphoreType.DMA((4,)),
        ],
        held=4,
    )
    order = after(me, parts[0])
    parts = [swap(part, "angle", mask) if mask in outer else part for mask, part in enumerate(parts)]
    own_outer = sums(
        [((mask,), 0) for mask in outer],
        [own_shape] * len(outer),
        [own_code],
        order,
        "sums_third",
    )
    lows = {}
    for mask, own, got in list(zip(outer, own_outer, got_outer, strict=True))[: len(outer) // 2]:
        (lows[mask],) = join([own], got)
    (second,) = sums([(tuple(inner), 0)], [far_shape], [far_code], after(me, lows[outer[0]]), "sums_second")
    got_inner = swap(after(second, *parts[len(inner) :]), "box", 1)
    late = after(parts[1], second)
    parts = [parts[0]] + [swap(late if mask == 1 else parts[mask], "angle", mask) for mask in inner[-2::-1]] + [*parts[len(inner) :]]
    orders = switch_theta.shape[0]
    azimuths = switch_phi.shape[1]
    shifted, trig, mix, theta_low, theta_switch = kernel_call(
        functools.partial(shift_body, peers, rows, low),
        [
            struct((upper_boxes, 2, rows, wide), F32),
            struct((2, children, peers, low, lanes), F32),
            struct((2 * azimuths, 2 * azimuths), BF16),
            struct(theta_lower.shape, BF16),
            struct(switch_theta.shape, BF16),
        ],
        [after(me, second)],
        [*parts, angles_upper, switch_phi, theta_lower, switch_theta],
        "shift",
        scratch=[
            *(pltpu.VMEM(a.shape, a.dtype) for a in (angles_upper, switch_phi, theta_lower, switch_theta)),
            pltpu.SemaphoreType.DMA((4,)),
        ],
        held=4,
    )
    for mask, own, got in list(zip(outer, own_outer, got_outer, strict=True))[len(outer) // 2 :]:
        (lows[mask],) = join([after(own, trig)], got)
    trig = trig.reshape(2, children, peers * low, lanes)
    ups = kernel_call(
        functools.partial(upper_body, outer + inner, peers, entries),
        [struct((upper_per, 2 * rows, lanes), BF16)] * peers,
        [after(me, lows[outer[-1]]), home.astype(jnp.int32).reshape(1), list_upper, offset_upper],
        [outgoing_upper, far_upper, table_upper, shifted, phi_lower],
        "upper",
        scratch=[
            pltpu.VMEM((2 * upper_boxes, 2, rows, wide), F32),
            pltpu.VMEM((upper_boxes, 2 * rows, wide), BF16),
        ],
    )
    ups = dict(zip(outer + inner, ups, strict=True))
    order = after(me, ups[0])
    behind = {mask: ups.pop(mask).reshape(-1, 2 * low, lanes) for mask in inner}
    own_inner = sums(
        [((mask,), 0) for mask in inner[:-1]],
        [own_shape] * (len(inner) - 1),
        [own_code],
        order,
        "sums_fourth",
    )
    close = join(own_inner, got_inner, [behind[mask] for mask in inner[:-1]])
    lows.update(zip(inner[:-1], close, strict=True))
    (lows[0],) = kernel_call(
        functools.partial(close_body, [0], [per * inner.index(0)], per, entries),
        [struct((per + behind[0].shape[0], 2 * low, lanes), BF16)],
        [after(me, close[0]), own_code],
        [table, source, got_inner, behind[0]],
        "close_self",
    )
    ups = [swap(ups[mask], "angle", mask) for mask in reversed(outer)]
    lows = [swap(lows[mask], "angle", mask) if mask else lows[mask] for mask in range(peers)]

    arrived = kernel_call(
        place_body,
        [struct(lows[mask].shape, F32) for mask in outer],
        [],
        [lows[mask] for mask in outer],
        "place",
    )
    lows = [*lows[: len(inner)], *reversed(arrived)]
    (out,) = kernel_call(
        functools.partial(final_body, peers, upper_per),
        [struct((per * 2 * orders, azimuths), F32)],
        [me],
        [*ups, *lows, trig, theta_low, mix, theta_switch],
        "expand",
        scratch=[
            pltpu.VMEM((upper_per, 2, peers, rows, lanes), F32),
            pltpu.VMEM((per, 2, peers, low, lanes), F32),
            pltpu.VMEM((2 * children * orders, 2 * lanes), BF16),
            pltpu.VMEM((per * 2 * orders + 8, azimuths), F32),
            pltpu.SemaphoreType.DMA((upper_per,)),
        ],
        away=1,
        vmem=12 << 20,
    )
    out = out.reshape(per, orders, 2, azimuths)
    return jnp.transpose(out, (0, 2, 1, 3)).reshape(per, 2, orders * azimuths)


def solution(mesh):
    return jax.shard_map(
        per_device,
        mesh=mesh,
        in_specs=(
            P("box", None, "angle", None),
            P(),
            P(),
            P(None, "angle", None),
            P(None, None, "angle", None),
            P("box", None, "angle", None),
            P("box", None),
            P("box", None),
            P(),
            P(),
            P(None, "angle", None),
            P(None, None, "angle", None),
            P("box", None, "angle", None),
            P("box", None),
            P("box", None),
            P(),
            P(),
        ),
        out_specs=P(("box", "angle"), None, None),
        check_vma=False,
    )
```

```python
import functools

import jax
import jax.numpy as jnp
from jax import lax
from jax.experimental import pallas as pl
from jax.experimental.pallas import tpu as pltpu
from jax.sharding import PartitionSpec as P

F32, BF16 = jnp.float32, jnp.bfloat16
VM = pl.BlockSpec(memory_space=pltpu.VMEM)
SM = pl.BlockSpec(memory_space=pltpu.SMEM)
HB = pl.BlockSpec(memory_space=pltpu.HBM)
SHIFT = 9
NT = (((1,), (1,)), ((), ()))


def swap(value, axis, mask):
    pairs = [(source, source ^ mask) for source in range(lax.axis_size(axis))]
    return lax.ppermute(value, axis, pairs)


COSTS = {"join": 0, "sums_third": 0, "shift": 0}


def after(value, *others):
    return lax.optimization_barrier((value, *others))[0]


def kernel_call(body, outs, scalars, arrays, name, scratch=(), held=0, vmem=6 << 20, away=0):
    near = len(arrays) - held
    return pl.pallas_call(
        body,
        out_shape=outs,
        in_specs=[SM] * len(scalars) + [VM] * near + [HB] * held,
        out_specs=[VM] * (len(outs) - away) + [HB] * away,
        scratch_shapes=list(scratch),
        compiler_params=pltpu.CompilerParams(vmem_limit_bytes=vmem),
        cost_estimate=pl.CostEstimate(flops=COSTS.get(name, 4) << 30, bytes_accessed=1, transcendentals=0),
        name=name,
    )(*scalars, *arrays)


def fetch(pairs, sems):
    copies = [pltpu.make_async_copy(a, b, sems.at[k]) for k, (a, b) in enumerate(pairs)]
    for copy in copies:
        copy.start()
    return copies


def split_dot(left, value, dims):
    high = value.astype(BF16)
    low = (value - high.astype(F32)).astype(BF16)
    return lax.dot_general(left, high, dims, preferred_element_type=F32) + lax.dot_general(
        left, low, dims, preferred_element_type=F32
    )


def box_sum(box, entries, code, table, source):
    rows = table.shape[1] // 2
    real = imag = None
    for entry in range(entries):
        word = code[entry, box]
        factor = table[word & ((1 << SHIFT) - 1)]
        value = source[word >> SHIFT]
        fr, fi, sr, si = factor[:rows], factor[rows:], value[:rows], value[rows:]
        re, im = fr * sr - fi * si, fr * si + fi * sr
        real = re if real is None else real + re
        imag = im if imag is None else imag + im
    return real, imag


def sums_body(groups, per, entries, me, *refs):
    codes = max(which for _, which in groups) + 1
    code_refs, (table, source), outs = refs[:codes], refs[codes : codes + 2], refs[codes + 2 :]
    rows = table.shape[1] // 2
    for (masks, which), out in zip(groups, outs, strict=True):
        for place, mask in enumerate(masks):
            first = jnp.bitwise_xor(me[0], mask) * per

            def one(i, carry, first=first, place=place, which=which, out=out):
                real, imag = box_sum(first + i, entries, code_refs[which], table, source)
                out[place * per + i, 0:rows] = real.astype(out.dtype)
                out[place * per + i, rows:] = imag.astype(out.dtype)
                return carry

            lax.fori_loop(0, per, one, 0, unroll=2)


def first_body(groups, per, entries, me, code, table, source, *refs):
    outs = refs[: len(groups)]
    table_out, source_out, table_in, source_in, wide_table, wide_source, sems, back = refs[len(groups) :]
    count, total = source.shape[0], table.shape[0]
    step = -(-total // 4)
    spans = [(k, min(k + step, total)) for k in range(0, total, step)]
    pairs = [(source, source_in)]
    pairs += [(table.at[lo:hi], table_in.at[lo:hi]) for lo, hi in spans]
    copies = fetch(pairs, sems)
    copies[0].wait()
    wide_source[0:count] = source_in[...].astype(F32)
    wide_source[count] = jnp.zeros(source.shape[1:], F32)
    for copy, (lo, hi) in zip(copies[1:], spans, strict=True):
        copy.wait()
        wide_table[lo:hi] = table_in[lo:hi].astype(F32)
    copies = fetch([(wide_table, table_out), (wide_source, source_out)], back)
    sums_body(groups, per, entries, me, code, wide_table, wide_source, *outs)
    for copy in copies:
        copy.wait()


def early_body(peers, rows, me, *refs):
    near, outs = refs[:4], refs[4 : 4 + peers]
    padded, summed, top, theta, phi, angles, sems = refs[4 + peers :]
    held = top.shape[0] // 4
    for copy in fetch(list(zip(near, (top, theta, phi, angles), strict=True)), sems):
        copy.wait()
    narrowed = lax.dot_general(top[...], phi[...], NT, preferred_element_type=F32)
    padded[...] = jnp.zeros(padded.shape, F32)
    for k in range(4):
        padded[k, me[0]] = narrowed[k * held : (k + 1) * held]
    for k in range(4):
        full = padded[k].reshape(peers * held, narrowed.shape[1])
        part = split_dot(theta[...], full, (((1,), (0,)), ((), ())))
        summed[k] = part.reshape(peers, rows, narrowed.shape[1])
    low = angles.shape[1]
    half = angles.shape[0] // 2
    for mask, out in enumerate(outs):
        for k in range(4):
            out[k * rows : (k + 1) * rows] = summed[k, jnp.bitwise_xor(me[0], mask)]
        for c in range(half):
            start = 4 * rows + c * low
            out[start : start + low, 0:128] = angles[c]
            out[start : start + low, 128:256] = angles[half + c]


def shift_body(peers, rows, low, me, *refs):
    parts, near = refs[:peers], refs[peers : peers + 4]
    shifted, trig, mix, low_out, switch_out, angles, phi, theta, switch, sems = refs[peers + 4 :]
    for copy in fetch(list(zip(near, (angles, phi, theta, switch), strict=True)), sems):
        copy.wait()
    low_out[...] = theta[...]
    switch_out[...] = switch[...]
    size = phi.shape[1]
    mix[0:size, 0:size] = phi[0]
    mix[0:size, size:] = -phi[1]
    mix[size:, 0:size] = phi[1]
    mix[size:, size:] = phi[0]
    children = angles.shape[0]
    half = children // 2
    for c in range(children):
        cosine, sine = jnp.cos(angles[c]), jnp.sin(angles[c])
        for b in range(2):
            re = parts[0][2 * b * rows : (2 * b + 1) * rows]
            im = parts[0][(2 * b + 1) * rows : (2 * b + 2) * rows]
            for part in parts[1:]:
                re = re + part[2 * b * rows : (2 * b + 1) * rows]
                im = im + part[(2 * b + 1) * rows : (2 * b + 2) * rows]
            shifted[b * children + c, 0] = re * cosine - im * sine
            shifted[b * children + c, 1] = re * sine + im * cosine
    for mask, part in enumerate(parts):
        for c in range(half):
            start = 4 * rows + c * low
            for side in range(2):
                angle = part[start : start + low, side * 128 : side * 128 + 128]
                place = jnp.bitwise_xor(me[0], mask)
                trig[0, side * half + c, place] = jnp.cos(angle)
                trig[1, side * half + c, place] = jnp.sin(angle)


def join(owns, got, extras=()):
    count, more = len(owns), len(extras)
    behind = [extras[k].shape[0] if extras else 0 for k in range(count)]

    def body(*refs):
        first = 0
        for k, (own, out) in enumerate(zip(refs[:count], refs[count + 1 + more :], strict=True)):
            size = own.shape[0]
            out[0:size] = (own[...] + refs[count][first : first + size].astype(F32)).astype(BF16)
            if extras:
                out[size:] = refs[count + 1 + k][...]
            first += size

    shapes = [struct((a.shape[0] + n, *a.shape[1:]), BF16) for a, n in zip(owns, behind, strict=True)]
    return kernel_call(body, shapes, [], [*owns, got, *extras], "join")


def upper_body(masks, peers, entries, me, home, ids, offsets, own, far, table, shifted, phi, *refs):
    outs, (pool, rounded) = refs[: len(masks)], refs[len(masks) :]
    boxes, _, rows, wide = own.shape
    pool[0:boxes] = own[...].astype(F32)
    pool[boxes:] = far[...].astype(F32)
    spans = [slice(r, r + 8) for r in range(0, rows, 8)]
    per = boxes // peers
    for turn, mask in enumerate(masks):
        first = jnp.bitwise_xor(me[0], mask) * per

        def one(i, carry, first=first, turn=turn):
            box = first + i
            real = [shifted[box, 0, span] for span in spans]
            imag = [shifted[box, 1, span] for span in spans]
            for entry in range(entries):
                offset, ident = offsets[box, entry], ids[box, entry]
                if boxes & (boxes - 1):
                    place = lax.rem(ident, boxes)
                else:
                    place = ident & (boxes - 1)
                place = jnp.where(ident - place == home[0] * boxes, place, place + boxes)
                for k, span in enumerate(spans):
                    fr, fi = table[offset, 0, span].astype(F32), table[offset, 1, span].astype(F32)
                    sr, si = pool[place, 0, span], pool[place, 1, span]
                    real[k] = real[k] + (fr * sr - fi * si)
                    imag[k] = imag[k] + (fr * si + fi * sr)
            rounded[turn * per + i] = jnp.concatenate([*real, *imag], axis=0).astype(BF16)
            return carry

        lax.fori_loop(0, per, one, 0)
    for turn, out in enumerate(outs):
        incoming = rounded[turn * per : (turn + 1) * per].reshape(per * 2 * rows, wide)
        narrow = lax.dot_general(incoming, phi[...], NT, preferred_element_type=F32)
        out[...] = narrow.astype(BF16).reshape(out.shape)


def place_body(*refs):
    count = len(refs) // 2
    for low, out in zip(refs[:count], refs[count:], strict=True):
        out[...] = low[...].astype(F32)


def final_body(peers, parents, me, *refs):
    near = peers // 2
    ups, lows = refs[:near], refs[near : near + peers]
    trig, theta, mix, expand, out, rows_up, rows_low, turned, ready, sems = refs[near + peers :]
    children, rows = trig.shape[1], trig.shape[2]
    high_rows, low_rows = rows_up.shape[3], rows_low.shape[3]
    orders = expand.shape[0]
    boxes = parents * children
    for mask in range(peers):
        place = jnp.bitwise_xor(me[0], mask)
        for c in range(2):
            for b in range(parents):
                if mask < near:
                    piece = lows[mask][boxes + 2 * b + c]
                else:
                    piece = ups[mask - near][b, c * high_rows : (c + 1) * high_rows]
                rows_up[b, c, place] = piece.astype(F32)
            piece = lows[mask][0:boxes, c * low_rows : (c + 1) * low_rows]
            rows_low[:, c, place] = piece.astype(F32)
    copies = []
    for b in range(parents):
        coarse = []
        for c in range(2):
            full = rows_up[b, c].reshape(peers * high_rows, 128).astype(BF16)
            coarse.append(jnp.dot(theta[...], full, preferred_element_type=F32))
        for k in range(children):
            cosine, sine = trig[0, k], trig[1, k]
            box = b * children + k
            real = coarse[0] * cosine - coarse[1] * sine + rows_low[box, 0].reshape(rows, 128)
            imag = coarse[0] * sine + coarse[1] * cosine + rows_low[box, 1].reshape(rows, 128)
            pattern = jnp.concatenate([real.astype(BF16), imag.astype(BF16)], axis=1)
            half = jnp.dot(expand[...], pattern, preferred_element_type=F32)
            high = half.astype(BF16)
            turned[k * orders : (k + 1) * orders] = high
            low = (half - high.astype(F32)).astype(BF16)
            turned[(children + k) * orders : (children + k + 1) * orders] = low
        both = lax.dot_general(turned[...], mix[...], NT, preferred_element_type=F32)
        size = children * orders
        result = both[:size] + both[size:]
        start = b * 2 * size
        ready[pl.ds(start, size, stride=2)] = result[:, :128]
        ready[pl.ds(start + 1, size, stride=2)] = result[:, 128:]
        span = pl.ds(start, 2 * size)
        copies += fetch([(ready.at[span], out.at[span])], sems.at[pl.ds(b, 1)])
    for copy in copies:
        copy.wait()


def struct(shape, dtype):
    return jax.ShapeDtypeStruct(shape, dtype)


def per_device(
    top_patterns,
    theta_upper,
    phi_upper,
    angles_upper,
    table_upper,
    outgoing_upper,
    list_upper,
    offset_upper,
    theta_lower,
    phi_lower,
    angles_lower,
    table_lower,
    outgoing_lower,
    list_lower,
    offset_lower,
    switch_theta,
    switch_phi,
):
    peers = lax.axis_size("angle")
    home = lax.axis_index("box")
    me = lax.axis_index("angle").astype(jnp.int32).reshape(1)
    far_mask = lax.axis_size("box") // 2
    boxes, _, low, lanes = outgoing_lower.shape
    per = boxes // peers
    entries = list_lower.shape[1]
    upper_boxes, _, rows, wide = outgoing_upper.shape
    upper_per = upper_boxes // peers

    other = list_lower.T // boxes != home
    spot = list_lower.T % boxes
    ask_code = (jnp.where(other, spot, boxes) << SHIFT) + offset_lower.T
    own_code = (jnp.where(other, boxes, spot) << SHIFT) + offset_lower.T
    far_code = swap(ask_code, "box", 1)
    far_upper = swap(outgoing_upper, "box", far_mask)

    places = table_lower.shape[0]
    outer, inner = list(range(peers - 1, peers // 2 - 1, -1)), list(range(peers // 2 - 1, -1, -1))

    def sums(groups, outs, codes, order, name):
        return kernel_call(
            functools.partial(sums_body, groups, per, entries),
            outs,
            [order, *codes],
            [table, source],
            name,
        )

    own_shape = struct((per, 2 * low, lanes), F32)
    far_shape = struct((len(outer) * per, 2 * low, lanes), BF16)
    *first, table, source = kernel_call(
        functools.partial(first_body, [((mask,), 0) for mask in outer], per, entries),
        [
            *[struct((per, 2 * low, lanes), BF16)] * len(outer),
            struct((places, 2 * low, lanes), F32),
            struct((boxes + 1, 2 * low, lanes), F32),
        ],
        [me, far_code],
        [table_lower.reshape(-1, 2 * low, lanes), outgoing_lower.reshape(-1, 2 * low, lanes)],
        "sums_first",
        scratch=[
            pltpu.VMEM((places, 2 * low, lanes), BF16),
            pltpu.VMEM((boxes, 2 * low, lanes), BF16),
            pltpu.VMEM((places, 2 * low, lanes), F32),
            pltpu.VMEM((boxes + 1, 2 * low, lanes), F32),
            pltpu.SemaphoreType.DMA((5,)),
            pltpu.SemaphoreType.DMA((2,)),
        ],
        held=2,
        away=2,
        vmem=53 << 20,
    )
    got_outer = [swap(value, "box", 1) for value in first]

    children = angles_lower.shape[0]
    part_rows = 4 * rows + children * low // 2
    held = top_patterns.shape[2]
    top = top_patterns.reshape(4 * held, -1)
    parts = kernel_call(
        functools.partial(early_body, peers, rows),
        [struct((part_rows, wide), F32)] * peers,
        [after(me, first[0])],
        [top, theta_upper, phi_upper, angles_lower],
        "early",
        scratch=[
            pltpu.VMEM((4, peers, held, wide), F32),
            pltpu.VMEM((4, peers, rows, wide), F32),
            *(pltpu.VMEM(a.shape, a.dtype) for a in (top, theta_upper, phi_upper, angles_lower)),
            pltpu.SemaphoreType.DMA((4,)),
        ],
        held=4,
    )
    order = after(me, parts[0])
    parts = [swap(part, "angle", mask) if mask in outer else part for mask, part in enumerate(parts)]
    own_outer = sums(
        [((mask,), 0) for mask in outer],
        [own_shape] * len(outer),
        [own_code],
        order,
        "sums_third",
    )
    lows = {}
    for mask, own, got in list(zip(outer, own_outer, got_outer, strict=True))[: len(outer) // 2]:
        (lows[mask],) = join([own], got)
    (second,) = sums([(tuple(inner), 0)], [far_shape], [far_code], after(me, lows[outer[0]]), "sums_second")
    got_inner = swap(after(second, *parts[len(inner) :]), "box", 1)
    late = after(parts[1], second)
    parts = [parts[0]] + [swap(late if mask == 1 else parts[mask], "angle", mask) for mask in inner[-2::-1]] + [*parts[len(inner) :]]
    orders = switch_theta.shape[0]
    azimuths = switch_phi.shape[1]
    shifted, trig, mix, theta_low, theta_switch = kernel_call(
        functools.partial(shift_body, peers, rows, low),
        [
            struct((upper_boxes, 2, rows, wide), F32),
            struct((2, children, peers, low, lanes), F32),
            struct((2 * azimuths, 2 * azimuths), BF16),
            struct(theta_lower.shape, BF16),
            struct(switch_theta.shape, BF16),
        ],
        [after(me, second)],
        [*parts, angles_upper, switch_phi, theta_lower, switch_theta],
        "shift",
        scratch=[
            *(pltpu.VMEM(a.shape, a.dtype) for a in (angles_upper, switch_phi, theta_lower, switch_theta)),
            pltpu.SemaphoreType.DMA((4,)),
        ],
        held=4,
    )
    for mask, own, got in list(zip(outer, own_outer, got_outer, strict=True))[len(outer) // 2 :]:
        (lows[mask],) = join([after(own, trig)], got)
    trig = trig.reshape(2, children, peers * low, lanes)
    ups = kernel_call(
        functools.partial(upper_body, outer + inner, peers, entries),
        [struct((upper_per, 2 * rows, lanes), BF16)] * peers,
        [after(me, lows[outer[-1]]), home.astype(jnp.int32).reshape(1), list_upper, offset_upper],
        [outgoing_upper, far_upper, table_upper, shifted, phi_lower],
        "upper",
        scratch=[
            pltpu.VMEM((2 * upper_boxes, 2, rows, wide), F32),
            pltpu.VMEM((upper_boxes, 2 * rows, wide), BF16),
        ],
    )
    ups = dict(zip(outer + inner, ups, strict=True))
    order = after(me, ups[0])
    behind = {mask: ups.pop(mask).reshape(-1, 2 * low, lanes) for mask in inner}
    own_inner = sums(
        [((mask,), 0) for mask in inner],
        [own_shape] * len(inner),
        [own_code],
        order,
        "sums_fourth",
    )
    close = join(own_inner, got_inner, [behind[mask] for mask in inner])
    lows.update(zip(inner, close, strict=True))
    ups = [swap(ups[mask], "angle", mask) for mask in reversed(outer)]
    lows = [swap(lows[mask], "angle", mask) if mask else lows[mask] for mask in range(peers)]

    arrived = kernel_call(
        place_body,
        [struct(lows[mask].shape, F32) for mask in outer],
        [],
        [lows[mask] for mask in outer],
        "place",
    )
    lows = [*lows[: len(inner)], *reversed(arrived)]
    (out,) = kernel_call(
        functools.partial(final_body, peers, upper_per),
        [struct((per * 2 * orders, azimuths), F32)],
        [me],
        [*ups, *lows, trig, theta_low, mix, theta_switch],
        "expand",
        scratch=[
            pltpu.VMEM((upper_per, 2, peers, rows, lanes), F32),
            pltpu.VMEM((per, 2, peers, low, lanes), F32),
            pltpu.VMEM((2 * children * orders, 2 * lanes), BF16),
            pltpu.VMEM((per * 2 * orders + 8, azimuths), F32),
            pltpu.SemaphoreType.DMA((upper_per,)),
        ],
        away=1,
        vmem=12 << 20,
    )
    out = out.reshape(per, orders, 2, azimuths)
    return jnp.transpose(out, (0, 2, 1, 3)).reshape(per, 2, orders * azimuths)


def solution(mesh):
    return jax.shard_map(
        per_device,
        mesh=mesh,
        in_specs=(
            P("box", None, "angle", None),
            P(),
            P(),
            P(None, "angle", None),
            P(None, None, "angle", None),
            P("box", None, "angle", None),
            P("box", None),
            P("box", None),
            P(),
            P(),
            P(None, "angle", None),
            P(None, None, "angle", None),
            P("box", None, "angle", None),
            P("box", None),
            P("box", None),
            P(),
            P(),
        ),
        out_specs=P(("box", "angle"), None, None),
        check_vma=False,
    )
```
